32 devices in a mesh: seq: 8 (over z, x), head: 4 (over y, core).
Axes of the slice: x: 2, y: 2, z: 4, core: 2. Of those that a mesh axis runs over, the one named last changes fastest.
Arguments:
- queries: bfloat16 [768, 16384], P('head', 'seq'), may hold values from -10 to 10
- key_vectors: bfloat16 [768, 16384], P('head', 'seq'), may hold values from -4 to 4
- value_vectors: bfloat16 [768, 16384], P('head', 'seq'), may hold values from -6 to 6
- offsets: int32 [3, 12], replicated, may hold values from 0 to 15, as said below
- out_weight: bfloat16 [768, 768], replicated, may hold values from -0.75 to 0.75
Outputs:
- layer_out: bfloat16 [16384, 768], P(('seq', 'head'))
The draws below stay inside these ranges and needn't reach their ends.
Inputs may be any that keep to these rules, and one draw needn't show every extreme that they name: offsets[0, h] < 4, offsets[1, h] < 16 and offsets[2, h] < 16; in each row some head has 0 and some head the largest allowed value.
All inputs are finite; a program needn't handle non-finite values.
Results may differ from the reference program's by a relative error of at most 0.0052.
Values may be sent and summed in bfloat16 or wider, within the bound.
No kernel may reach another device: no remote copies, remote signals or barrier semaphores. Data moves between devices by JAX's collectives and lax.ppermute only.
A program may use at most 128 MiB of HBM per device.

```python
import jax
import jax.numpy as jnp
from jax import lax

D = 768
HEADS = 12
DH = 64
KEYS = 1024
TOKENS = 16384


def draw_queries(key, part):
    return jnp.transpose(2.5 * jnp.clip(jax.random.normal(jax.random.fold_in(key, 11), (TOKENS, D), jnp.float32), -4.0, 4.0)).astype(jnp.bfloat16)


def draw_key_vectors(key, part):
    return jnp.transpose(jnp.clip(jax.random.normal(jax.random.fold_in(key, 13), (TOKENS, D), jnp.float32), -4.0, 4.0)).astype(jnp.bfloat16)


def draw_offsets(key, part):
    dilations = jnp.array([4, 16, TOKENS // KEYS], jnp.int32)[:, None]
    drawn_vals = jax.random.randint(jax.random.fold_in(key, 21), (3, HEADS), 0, dilations)
    top_column = jax.random.randint(jax.random.fold_in(key, 22), (3, 1), 0, HEADS)
    low_column = (top_column + 1 + jax.random.randint(jax.random.fold_in(key, 23), (3, 1), 0, HEADS - 1)) % HEADS
    columns = jnp.arange(HEADS)[None, :]
    placed = jnp.where(columns == top_column, dilations - 1, drawn_vals)
    return jnp.where(columns == low_column, 0, placed).astype(jnp.int32)


def shard_levels(stream_key, shape, pieces, smallest, top_value):
    level, own = 1.0, jax.random.fold_in(stream_key, 6)
    for axis_at, parts in pieces:
        steps = jnp.exp(jax.random.uniform(jax.random.fold_in(own, axis_at), (parts,), jnp.float32, smallest / len(pieces), top_value / len(pieces)))
        level = level * jnp.repeat(steps, shape[axis_at] // parts).reshape([-1 if axis == axis_at else 1 for axis in range(len(shape))])
    return level


def centred(stream_key, dims, width, bound, pieces=(), held_as=jnp.bfloat16):
    loudness = shard_levels(stream_key, dims, pieces, -0.22, 0.18) if pieces else 1.0
    result = jax.random.normal(stream_key, dims, jnp.float32) * width * loudness
    return jnp.minimum(jnp.maximum(result, -bound), bound).astype(held_as)


def setup_inputs(seed: int = 0) -> dict:
    key_of = jax.random.split(jax.random.key(seed), 6)
    return {
        "queries": draw_queries(jax.random.fold_in(key_of[5], 71), 0),
        "key_vectors": draw_key_vectors(jax.random.fold_in(key_of[5], 71), 0),
        "value_vectors": centred(key_of[2], (D, TOKENS), 1.0, 6.0, ((0, 4), (1, 8))),
        "offsets": draw_offsets(jax.random.fold_in(key_of[5], 71), 0),
        "out_weight": centred(key_of[4], (D, D), DH ** -0.5, 0.75),
    }


def pick(values_in, dilation, offset):
    shaped = values_in.reshape((values_in.shape[0] // dilation, dilation) + values_in.shape[1:])
    return lax.dynamic_index_in_dim(shaped, offset, 1, keepdims=False)


def combine(running, branch):
    old_max, old_sum, old_acc = running
    new_max, new_sum, new_acc = branch
    both_max = jnp.maximum(old_max, new_max)
    keep_old = jnp.exp(old_max - both_max)
    keep_new = jnp.exp(new_max - both_max)
    return (both_max, old_sum * keep_old + new_sum * keep_new,
            old_acc * keep_old[:, None] + new_acc * keep_new[:, None])


def merge_at(running, branch, dilation, offset):
    current = tuple(pick(member, dilation, offset) for member in running)
    merged = combine(current, branch)
    result_list = []
    for member, update in zip(running, merged):
        shaped = member.reshape((member.shape[0] // dilation, dilation) + member.shape[1:])
        shaped = lax.dynamic_update_index_in_dim(shaped, update, offset, 1)
        result_list.append(shaped.reshape(member.shape))
    return tuple(result_list)


def attend(query_seg, key_seg, value_seg):
    def per_segment(inputs):
        query_blk, key_blk, value_blk = inputs
        scores = jnp.dot(query_blk, key_blk.T, preferred_element_type=jnp.float32) * (DH ** -0.5)
        row_max = jnp.max(scores, axis=1)
        weights_f = jnp.exp(scores - row_max[:, None])
        row_sum = jnp.sum(weights_f, axis=1)
        summed = jnp.dot(weights_f.astype(jnp.bfloat16), value_blk, preferred_element_type=jnp.float32)
        return row_max, row_sum, summed
    return lax.map(per_segment, (query_seg, key_seg, value_seg))


def one_head(inputs):
    query_h, key_h, value_h, head_offsets = inputs
    branch_specs = ((KEYS, 1), (4 * KEYS, 4), (16 * KEYS, 16), (TOKENS, TOKENS // KEYS))
    running = None
    for branch_idx, (seg_len, dilation) in enumerate(branch_specs):
        if branch_idx == 0:
            offset = jnp.int32(0)
        else:
            offset = head_offsets[branch_idx - 1].astype(jnp.int32)
        segments = TOKENS // seg_len
        query_sel = pick(query_h, dilation, offset).reshape(segments, KEYS, DH)
        key_sel = pick(key_h, dilation, offset).reshape(segments, KEYS, DH)
        value_sel = pick(value_h, dilation, offset).reshape(segments, KEYS, DH)
        row_max, row_sum, summed = attend(query_sel, key_sel, value_sel)
        flat = (row_max.reshape(-1), row_sum.reshape(-1), summed.reshape(-1, DH))
        if branch_idx == 0:
            running = flat
        else:
            running = merge_at(running, flat, dilation, offset)
    run_max, run_sum, run_acc = running
    return (run_acc / run_sum[:, None]).astype(jnp.bfloat16)


def reference(queries, key_vectors, value_vectors, offsets, out_weight):
    def by_head(values_in):
        return jnp.transpose(values_in.reshape(HEADS, DH, TOKENS), (0, 2, 1))

    attended = lax.map(one_head, (by_head(queries), by_head(key_vectors), by_head(value_vectors),
                                  jnp.transpose(offsets)))
    attended_rows = jnp.transpose(attended, (1, 0, 2)).reshape(TOKENS, D)
    return jnp.dot(attended_rows, out_weight, preferred_element_type=jnp.float32).astype(jnp.bfloat16)
```

```python
import functools
import math

import jax
import jax.numpy as jnp
from jax import lax
from jax.experimental import pallas as pl
from jax.experimental.pallas import tpu as pltpu
from jax.sharding import PartitionSpec as P

DH = 64
KEYS = 1024
LANES = 128
QBLK = 256
EXP2_SCALE = DH ** (-0.5) * math.log2(math.e)
NT = (((1,), (1,)), ((), ()))
NN = (((1,), (0,)), ((), ()))
VMEM_BYTES = 48 << 20


def dot(a, b, dims):
    return lax.dot_general(a, b, dims, preferred_element_type=jnp.float32)


def lane_of(shape):
    return lax.broadcasted_iota(jnp.int32, shape, len(shape) - 1)


def softmax_block(scores):
    row_max = jnp.max(scores, axis=1, keepdims=True)
    weights = jnp.exp2((scores - row_max) * EXP2_SCALE).astype(jnp.bfloat16)
    return row_max, weights


def merge_rows(cur, cur_max, new, new_max):
    both = jnp.maximum(cur_max, new_max)
    keep_cur = jnp.exp2((cur_max - both) * EXP2_SCALE)
    keep_new = jnp.exp2((new_max - both) * EXP2_SCALE)
    return both, cur * keep_cur + new * keep_new


def select_kernel(dils, off_ref, q_ref, k_ref, v_ref, q1_ref, near_ref, far_ref, kvt, qt):
    heads = q_ref.shape[0] // DH
    tok = q_ref.shape[1]
    first = lax.axis_index("head") * heads
    n1 = tok // dils[0]
    for h in range(heads):
        rows = slice(h * DH, (h + 1) * DH)
        kvt[...] = jnp.concatenate([k_ref[rows, :], v_ref[rows, :]], 0).T.astype(jnp.float32)
        qt[...] = q_ref[rows, :].T.astype(jnp.float32)
        o1 = off_ref[0, first + h]
        q1_ref[h] = qt[pl.ds(o1, n1, stride=dils[0]), :].astype(jnp.bfloat16)
        near_ref[h, :n1, :] = kvt[pl.ds(o1, n1, stride=dils[0]), :].astype(jnp.bfloat16)
        q_parts = []
        for b in range(1, len(dils)):
            o = off_ref[b, first + h]
            n = tok // dils[b]
            q_parts.append(qt[pl.ds(o, n, stride=dils[b]), :])
            picked = kvt[pl.ds(o, n, stride=dils[b]), :]
            if b == 2:
                picked = pltpu.roll(picked, DH, 1)
            far_ref[b - 1, h] = picked.astype(jnp.bfloat16)
        if len(q_parts) == 1:
            q_parts.append(jnp.zeros_like(q_parts[0]))
        near_ref[h, n1:, :] = jnp.concatenate(q_parts, 1).astype(jnp.bfloat16)


def local_kernel(q_ref, k_ref, v_ref, acc_ref):
    tok = q_ref.shape[1]
    qt = q_ref[...].T
    for seg in range(tok // KEYS):
        cols = slice(seg * KEYS, (seg + 1) * KEYS)
        keys = k_ref[:, cols]
        vals = v_ref[:, cols]
        vals = jnp.concatenate([jnp.ones_like(vals), vals], 0)
        for blk in range(KEYS // QBLK):
            at = seg * KEYS + blk * QBLK
            row_max, weights = softmax_block(dot(qt[at : at + QBLK], keys, NN))
            out = dot(weights, vals, NT)
            acc_ref[0, at : at + QBLK, :] = jnp.where(lane_of(out.shape) == 0, row_max, out)


def pair_kernel(dil, off_ref, q_ref, own_ref, other_ref, acc_in, acc_ref):
    h = pl.program_id(0)
    heads = pl.num_programs(0)
    o = off_ref[0, lax.axis_index("head") * heads + h]
    n1 = q_ref.shape[1]
    acc_ref[...] = acc_in[...]
    kv = jnp.concatenate([own_ref[0, :n1, :], other_ref[0, :n1, :]], 0)
    keys = kv[:, :DH]
    vals = jnp.where(lane_of(kv.shape) < DH, jnp.ones_like(kv), kv)
    for blk in range(n1 // QBLK):
        rows = pl.ds(o + blk * QBLK * dil, QBLK, stride=dil)
        row_max, weights = softmax_block(dot(q_ref[0, blk * QBLK : (blk + 1) * QBLK], keys, NT))
        out = dot(weights, vals, NN)
        cur = acc_ref[0, rows, :]
        both, new = merge_rows(cur, cur[:, :1], out, row_max)
        acc_ref[0, rows, :] = jnp.where(lane_of(new.shape) == 0, both, new)


def far_kernel(branches, own_ref, other_ref, kv0, kv1, kv2, kv3, part_ref, send_ref):
    n1 = own_ref.shape[1] - LANES
    q_all = jnp.concatenate([own_ref[0, n1:, :], other_ref[0, n1:, :]], 0)
    lane_q = lane_of(q_all.shape)
    outs = []
    maxes = []
    for b in range(branches):
        kv = jnp.concatenate([r[b, 0] for r in (kv0, kv1, kv2, kv3)], 0)
        in_keys = (lane_of(kv.shape) < DH) == (b == 0)
        q_b = jnp.where((lane_q < DH) == (b == 0), q_all, jnp.zeros_like(q_all))
        row_max, weights = softmax_block(dot(q_b, kv, NT))
        vals = jnp.where(in_keys, jnp.ones_like(kv), kv)
        outs.append(dot(weights, vals, NN))
        maxes.append(row_max)
    n = q_all.shape[0] // 2
    lane = lane_of((n, LANES))
    for b in range(branches):
        part_ref[b, 0] = jnp.where(lane == (0 if b == 0 else LANES - 1), maxes[b][:n], outs[b][:n])
    out_a = outs[0][n:]
    out_b = outs[1][n:] if branches == 2 else out_a
    max_a = maxes[0][n:]
    max_b = maxes[1][n:] if branches == 2 else max_a
    send_ref[0, :n, :] = jnp.where(lane < DH, out_b, out_a).astype(jnp.bfloat16)
    sums = jnp.where(lane < DH, out_a, out_b)
    tops = jnp.where(lane < DH, max_a, max_b)
    slot = lane % DH
    stats = jnp.where(slot >= 3, sums, tops)
    high = stats.astype(jnp.bfloat16).astype(jnp.float32)
    mid = (stats - high).astype(jnp.bfloat16).astype(jnp.float32)
    low = stats - high - mid
    kind = slot % 3
    coded = jnp.where(kind == 0, high, jnp.where(kind == 1, mid, low))
    send_ref[0, n:, :] = coded.astype(jnp.bfloat16)


def finish_kernel(dils, off_ref, acc_in, part_ref, got_ref, o0, o1, o2, o3, acc):
    h = pl.program_id(0)
    heads = pl.num_programs(0)
    me = lax.axis_index("head")
    acc[...] = acc_in[0]
    n = part_ref.shape[2]
    got = got_ref[0, :n, :].astype(jnp.float32)
    coded = got_ref[0, n:, :].astype(jnp.float32)
    lane = lane_of((n, LANES))
    for b in range(len(dils)):
        o = off_ref[b + 1, me * heads + h]
        rows = pl.ds(o, n, stride=dils[b])
        cur = acc[rows, :]
        c = DH * b
        part = part_ref[b, 0]
        part_max = part[:, :1] if b == 0 else part[:, LANES - 1 :]
        got_max = coded[:, c : c + 1] + coded[:, c + 1 : c + 2] + coded[:, c + 2 : c + 3]
        got_sum = coded[:, c + 3 : c + 4] + coded[:, c + 4 : c + 5] + coded[:, c + 5 : c + 6]
        if b == 1:
            part = pltpu.roll(part, DH, 1)
            got_acc = pltpu.roll(got, DH, 1)
        else:
            got_acc = got
        new = jnp.where(lane < DH, got_sum, got_acc)
        part_max, part = merge_rows(part, part_max, new, got_max)
        both, cur = merge_rows(cur, cur[:, :1], part, part_max)
        acc[rows, :] = jnp.where(lane == 0, both, cur)
    flipped = acc[...].T
    done = (flipped[DH:, :] / flipped[1:2, :]).astype(jnp.bfloat16)
    outs = (o0, o1, o2, o3)
    width = o0.shape[1]
    for s, out in enumerate(outs):
        for dest in range(len(outs)):

            @pl.when((me ^ s) == dest)
            def _():
                out[...] = done[:, dest * width : (dest + 1) * width]


def project_kernel(x0, x1, x2, x3, w_ref, out_ref, xs):
    me = lax.axis_index("head")
    rows = x0.shape[0]
    for s, x in enumerate((x0, x1, x2, x3)):
        xs[pl.ds(pl.multiple_of((me ^ s) * rows, 64), rows), :] = x[...]
    out_ref[...] = dot(xs[...], w_ref[...], (((0,), (0,)), ((), ()))).astype(jnp.bfloat16)


def partner(block, axis, apart):
    count = lax.axis_size(axis)
    return lax.ppermute(block, axis, [(i, i ^ apart) for i in range(count)])


def params():
    return pltpu.CompilerParams(vmem_limit_bytes=VMEM_BYTES)


def whole():
    return pl.BlockSpec(memory_space=pltpu.VMEM)


def smem():
    return pl.BlockSpec(memory_space=pltpu.SMEM)


def by_head(shape):
    return pl.BlockSpec((1,) + shape, lambda h: (h, 0, 0))


def cost(queries, keys):
    return pl.CostEstimate(
        flops=queries * keys * 512, bytes_accessed=queries * 2048, transcendentals=queries * keys
    )


def spread_far(acc, query_h, key_h, value_h, dil, head_offsets):
    hit = jnp.arange(dil)[None, :] == head_offsets[:, None]

    def pick(x):
        shaped = x.reshape(x.shape[:2] + (x.shape[2] // dil, dil))
        return jnp.sum(shaped * hit[:, None, None, :].astype(x.dtype), axis=-1, dtype=x.dtype)

    pair = lax.all_gather(jnp.stack([pick(key_h), pick(value_h)], 0), "seq", axis=3, tiled=True)
    scores = jnp.einsum("hdq,hdk->hqk", pick(query_h), pair[0], preferred_element_type=jnp.float32)
    new_max = jnp.max(scores, axis=2)
    e = jnp.exp2((scores - new_max[:, :, None]) * EXP2_SCALE)
    new_sum = jnp.sum(e, axis=2)
    new_acc = jnp.einsum(
        "hqk,hdk->hqd", e.astype(jnp.bfloat16), pair[1], preferred_element_type=jnp.float32
    )
    heads, tok, _ = acc.shape
    shaped = acc.reshape(heads, tok // dil, dil, LANES)
    cur = jnp.sum(jnp.where(hit[:, None, :, None], shaped, 0.0), axis=2)
    new = jnp.concatenate([jnp.broadcast_to(new_sum[:, :, None], new_acc.shape), new_acc], 2)
    both, out = merge_rows(cur, cur[:, :, :1], new, new_max[:, :, None])
    out = jnp.where(jnp.arange(LANES) == 0, both, out)
    return jnp.where(hit[:, None, :, None], out[:, :, None, :], shaped).reshape(acc.shape)


def local(queries, key_vectors, value_vectors, offsets, out_weight):
    tok = queries.shape[1]
    heads = queries.shape[0] // DH
    seq_count = lax.axis_size("seq")
    far_rate = tok * seq_count // KEYS
    dils = (4, 16, far_rate) if far_rate == 16 else (4, 16)
    branches = len(dils) - 1
    n1, n2 = tok // 4, tok // 16
    bf16, f32 = jnp.bfloat16, jnp.float32
    struct = jax.ShapeDtypeStruct

    q1, near, far = pl.pallas_call(
        functools.partial(select_kernel, dils),
        out_shape=(
            struct((heads, n1, DH), bf16),
            struct((heads, n1 + n2, LANES), bf16),
            struct((branches, heads, n2, LANES), bf16),
        ),
        in_specs=[smem(), whole(), whole(), whole()],
        out_specs=(whole(), whole(), whole()),
        scratch_shapes=[pltpu.VMEM((tok, LANES), f32), pltpu.VMEM((tok, DH), f32)],
        compiler_params=params(),
        name="select",
    )(offsets, queries, key_vectors, value_vectors)

    fars = [far] + [partner(far, "seq", apart) for apart in (2, 4, 6)]
    near_other = partner(near, "seq", 1)

    by_rows = pl.BlockSpec((DH, tok), lambda h: (h, 0))
    acc = pl.pallas_call(
        local_kernel,
        grid=(heads,),
        out_shape=struct((heads, tok, LANES), f32),
        in_specs=[by_rows, by_rows, by_rows],
        out_specs=by_head((tok, LANES)),
        compiler_params=params(),
        cost_estimate=cost(heads * tok, KEYS),
        name="local",
    )(queries, key_vectors, value_vectors)

    acc = pl.pallas_call(
        functools.partial(pair_kernel, 4),
        grid=(heads,),
        out_shape=struct((heads, tok, LANES), f32),
        in_specs=[smem(), by_head((n1, DH)), by_head((n1 + n2, LANES)), by_head((n1 + n2, LANES)), by_head((tok, LANES))],
        out_specs=by_head((tok, LANES)),
        input_output_aliases={4: 0},
        compiler_params=params(),
        cost_estimate=cost(heads * n1, KEYS),
        name="pair",
    )(offsets, q1, near, near_other, acc)

    if branches == 1:
        shape = (heads, DH, tok)
        my_offsets = lax.dynamic_slice_in_dim(offsets[2], lax.axis_index("head") * heads, heads, 0)
        acc = spread_far(
            acc, queries.reshape(shape), key_vectors.reshape(shape), value_vectors.reshape(shape), far_rate, my_offsets
        )

    far_spec = pl.BlockSpec((branches, 1, n2, LANES), lambda h: (0, h, 0, 0))
    part, send = pl.pallas_call(
        functools.partial(far_kernel, branches),
        grid=(heads,),
        out_shape=(struct((branches, heads, n2, LANES), f32), struct((heads, 2 * n2, LANES), bf16)),
        in_specs=[by_head((n1 + n2, LANES))] * 2 + [far_spec] * 4,
        out_specs=(far_spec, by_head((2 * n2, LANES))),
        compiler_params=params(),
        cost_estimate=cost(heads * n2 * 4, KEYS // 2),
        name="far",
    )(near, near_other, *fars)
    got = partner(send, "seq", 1)

    head_count = lax.axis_size("head")
    width = tok // head_count
    out_spec = pl.BlockSpec((DH, width), lambda h: (h, 0))
    blocks = pl.pallas_call(
        functools.partial(finish_kernel, dils[1:]),
        grid=(heads,),
        out_shape=(struct((heads * DH, width), bf16),) * head_count,
        in_specs=[smem(), by_head((tok, LANES)), far_spec, by_head((2 * n2, LANES))],
        out_specs=(out_spec,) * head_count,
        scratch_shapes=[pltpu.VMEM((tok, LANES), f32)],
        compiler_params=params(),
        name="finish",
    )(offsets, acc, part, got)

    landed = [blocks[0]] + [partner(blocks[s], "head", s) for s in range(1, head_count)]
    return pl.pallas_call(
        project_kernel,
        out_shape=struct((width, out_weight.shape[1]), bf16),
        in_specs=[whole()] * (head_count + 1),
        out_specs=whole(),
        scratch_shapes=[pltpu.VMEM((head_count * heads * DH, width), bf16)],
        compiler_params=params(),
        name="project",
    )(*landed, out_weight)


def solution(mesh):
    in_specs = (P("head", "seq"), P("head", "seq"), P("head", "seq"), P(), P())
    out_specs = P(("seq", "head"), None)
    return jax.shard_map(local, mesh=mesh, in_specs=in_specs, out_specs=out_specs, check_vma=False)
```

```python
import functools
import math

import jax
import jax.numpy as jnp
from jax import lax
from jax.experimental import pallas as pl
from jax.experimental.pallas import tpu as pltpu
from jax.sharding import PartitionSpec as P

DH = 64
KEYS = 1024
LANES = 128
QBLK = 256
EXP2_SCALE = DH ** (-0.5) * math.log2(math.e)
NT = (((1,), (1,)), ((), ()))
NN = (((1,), (0,)), ((), ()))
VMEM_BYTES = 48 << 20


def dot(a, b, dims):
    return lax.dot_general(a, b, dims, preferred_element_type=jnp.float32)


def lane_of(shape):
    return lax.broadcasted_iota(jnp.int32, shape, len(shape) - 1)


def softmax_block(scores):
    row_max = jnp.max(scores, axis=1, keepdims=True)
    weights = jnp.exp2((scores - row_max) * EXP2_SCALE).astype(jnp.bfloat16)
    return row_max, weights


def merge_rows(cur, cur_max, new, new_max):
    both = jnp.maximum(cur_max, new_max)
    keep_cur = jnp.exp2((cur_max - both) * EXP2_SCALE)
    keep_new = jnp.exp2((new_max - both) * EXP2_SCALE)
    return both, cur * keep_cur + new * keep_new


def select_kernel(dils, off_ref, q_ref, k_ref, v_ref, q1_ref, near_ref, far_ref, kvt, qt):
    tok = q_ref.shape[1]
    head = lax.axis_index("head") * pl.num_programs(0) + pl.program_id(0)
    n1 = tok // dils[0]
    kvt[...] = jnp.concatenate([k_ref[...], v_ref[...]], 0).T.astype(jnp.float32)
    qt[...] = q_ref[...].T.astype(jnp.float32)
    o1 = off_ref[0, head]
    q1_ref[0] = qt[pl.ds(o1, n1, stride=dils[0]), :].astype(jnp.bfloat16)
    near_ref[0, :n1, :] = kvt[pl.ds(o1, n1, stride=dils[0]), :].astype(jnp.bfloat16)
    q_parts = []
    for b in range(1, len(dils)):
        o = off_ref[b, head]
        n = tok // dils[b]
        q_parts.append(qt[pl.ds(o, n, stride=dils[b]), :])
        picked = kvt[pl.ds(o, n, stride=dils[b]), :]
        if b == 2:
            picked = pltpu.roll(picked, DH, 1)
        far_ref[b - 1, 0] = picked.astype(jnp.bfloat16)
    if len(q_parts) == 1:
        q_parts.append(jnp.zeros_like(q_parts[0]))
    near_ref[0, n1:, :] = jnp.concatenate(q_parts, 1).astype(jnp.bfloat16)


def local_kernel(q_ref, k_ref, v_ref, acc_ref):
    tok = q_ref.shape[1]
    qt = q_ref[...].T
    for seg in range(tok // KEYS):
        cols = slice(seg * KEYS, (seg + 1) * KEYS)
        keys = k_ref[:, cols]
        vals = v_ref[:, cols]
        vals = jnp.concatenate([jnp.ones_like(vals), vals], 0)
        for blk in range(KEYS // QBLK):
            at = seg * KEYS + blk * QBLK
            row_max, weights = softmax_block(dot(qt[at : at + QBLK], keys, NN))
            out = dot(weights, vals, NT)
            acc_ref[0, at : at + QBLK, :] = jnp.where(lane_of(out.shape) == 0, row_max, out)


def pair_kernel(dil, off_ref, q_ref, own_ref, other_ref, acc_in, acc_ref):
    h = pl.program_id(0)
    heads = pl.num_programs(0)
    o = off_ref[0, lax.axis_index("head") * heads + h]
    n1 = q_ref.shape[1]
    acc_ref[...] = acc_in[...]
    kv = jnp.concatenate([own_ref[0, :n1, :], other_ref[0, :n1, :]], 0)
    keys = kv[:, :DH]
    vals = jnp.where(lane_of(kv.shape) < DH, jnp.ones_like(kv), kv)
    for blk in range(n1 // QBLK):
        rows = pl.ds(o + blk * QBLK * dil, QBLK, stride=dil)
        row_max, weights = softmax_block(dot(q_ref[0, blk * QBLK : (blk + 1) * QBLK], keys, NT))
        out = dot(weights, vals, NN)
        cur = acc_ref[0, rows, :]
        both, new = merge_rows(cur, cur[:, :1], out, row_max)
        acc_ref[0, rows, :] = jnp.where(lane_of(new.shape) == 0, both, new)


def far_kernel(branches, own_ref, other_ref, kv0, kv1, kv2, kv3, part_ref, send_ref):
    n1 = own_ref.shape[1] - LANES
    q_all = jnp.concatenate([own_ref[0, n1:, :], other_ref[0, n1:, :]], 0)
    lane_q = lane_of(q_all.shape)
    outs = []
    maxes = []
    for b in range(branches):
        kv = jnp.concatenate([r[b, 0] for r in (kv0, kv1, kv2, kv3)], 0)
        in_keys = (lane_of(kv.shape) < DH) == (b == 0)
        q_b = jnp.where((lane_q < DH) == (b == 0), q_all, jnp.zeros_like(q_all))
        row_max, weights = softmax_block(dot(q_b, kv, NT))
        vals = jnp.where(in_keys, jnp.ones_like(kv), kv)
        outs.append(dot(weights, vals, NN))
        maxes.append(row_max)
    n = q_all.shape[0] // 2
    lane = lane_of((n, LANES))
    for b in range(branches):
        part_ref[b, 0] = jnp.where(lane == (0 if b == 0 else LANES - 1), maxes[b][:n], outs[b][:n])
    out_a = outs[0][n:]
    out_b = outs[1][n:] if branches == 2 else out_a
    max_a = maxes[0][n:]
    max_b = maxes[1][n:] if branches == 2 else max_a
    send_ref[0, :n, :] = jnp.where(lane < DH, out_b, out_a).astype(jnp.bfloat16)
    sums = jnp.where(lane < DH, out_a, out_b)
    tops = jnp.where(lane < DH, max_a, max_b)
    slot = lane % DH
    stats = jnp.where(slot >= 3, sums, tops)
    high = stats.astype(jnp.bfloat16).astype(jnp.float32)
    mid = (stats - high).astype(jnp.bfloat16).astype(jnp.float32)
    low = stats - high - mid
    kind = slot % 3
    coded = jnp.where(kind == 0, high, jnp.where(kind == 1, mid, low))
    send_ref[0, n:, :] = coded.astype(jnp.bfloat16)


def finish_kernel(dils, off_ref, acc_in, part_ref, got_ref, o0, o1, o2, o3, acc):
    h = pl.program_id(0)
    heads = pl.num_programs(0)
    me = lax.axis_index("head")
    acc[...] = acc_in[0]
    n = part_ref.shape[2]
    got = got_ref[0, :n, :].astype(jnp.float32)
    coded = got_ref[0, n:, :].astype(jnp.float32)
    lane = lane_of((n, LANES))
    for b in range(len(dils)):
        o = off_ref[b + 1, me * heads + h]
        rows = pl.ds(o, n, stride=dils[b])
        cur = acc[rows, :]
        c = DH * b
        part = part_ref[b, 0]
        part_max = part[:, :1] if b == 0 else part[:, LANES - 1 :]
        got_max = coded[:, c : c + 1] + coded[:, c + 1 : c + 2] + coded[:, c + 2 : c + 3]
        got_sum = coded[:, c + 3 : c + 4] + coded[:, c + 4 : c + 5] + coded[:, c + 5 : c + 6]
        if b == 1:
            part = pltpu.roll(part, DH, 1)
            got_acc = pltpu.roll(got, DH, 1)
        else:
            got_acc = got
        new = jnp.where(lane < DH, got_sum, got_acc)
        part_max, part = merge_rows(part, part_max, new, got_max)
        both, cur = merge_rows(cur, cur[:, :1], part, part_max)
        acc[rows, :] = jnp.where(lane == 0, both, cur)
    flipped = acc[...].T
    done = (flipped[DH:, :] / flipped[1:2, :]).astype(jnp.bfloat16)
    outs = (o0, o1, o2, o3)
    width = o0.shape[1]
    for s, out in enumerate(outs):
        for dest in range(len(outs)):

            @pl.when((me ^ s) == dest)
            def _():
                out[...] = done[:, dest * width : (dest + 1) * width]


def project_kernel(x0, x1, x2, x3, w_ref, out_ref, xs):
    me = lax.axis_index("head")
    rows = x0.shape[0]
    for s, x in enumerate((x0, x1, x2, x3)):
        xs[pl.ds(pl.multiple_of((me ^ s) * rows, 64), rows), :] = x[...]
    out_ref[...] = dot(xs[...], w_ref[...], (((0,), (0,)), ((), ()))).astype(jnp.bfloat16)


def partner(block, axis, apart):
    count = lax.axis_size(axis)
    return lax.ppermute(block, axis, [(i, i ^ apart) for i in range(count)])


def params(limit=None):
    return pltpu.CompilerParams(vmem_limit_bytes=limit)


def whole():
    return pl.BlockSpec(memory_space=pltpu.VMEM)


def smem():
    return pl.BlockSpec(memory_space=pltpu.SMEM)


def by_head(shape):
    return pl.BlockSpec((1,) + shape, lambda h: (h, 0, 0))


def cost(queries, keys):
    return pl.CostEstimate(
        flops=queries * keys * 512, bytes_accessed=queries * 2048, transcendentals=queries * keys
    )


def spread_far(acc, query_h, key_h, value_h, dil, head_offsets):
    hit = jnp.arange(dil)[None, :] == head_offsets[:, None]

    def pick(x):
        shaped = x.reshape(x.shape[:2] + (x.shape[2] // dil, dil))
        return jnp.sum(shaped * hit[:, None, None, :].astype(x.dtype), axis=-1, dtype=x.dtype)

    pair = lax.all_gather(jnp.stack([pick(key_h), pick(value_h)], 0), "seq", axis=3, tiled=True)
    scores = jnp.einsum("hdq,hdk->hqk", pick(query_h), pair[0], preferred_element_type=jnp.float32)
    new_max = jnp.max(scores, axis=2)
    e = jnp.exp2((scores - new_max[:, :, None]) * EXP2_SCALE)
    new_sum = jnp.sum(e, axis=2)
    new_acc = jnp.einsum(
        "hqk,hdk->hqd", e.astype(jnp.bfloat16), pair[1], preferred_element_type=jnp.float32
    )
    heads, tok, _ = acc.shape
    shaped = acc.reshape(heads, tok // dil, dil, LANES)
    cur = jnp.sum(jnp.where(hit[:, None, :, None], shaped, 0.0), axis=2)
    new = jnp.concatenate([jnp.broadcast_to(new_sum[:, :, None], new_acc.shape), new_acc], 2)
    both, out = merge_rows(cur, cur[:, :, :1], new, new_max[:, :, None])
    out = jnp.where(jnp.arange(LANES) == 0, both, out)
    return jnp.where(hit[:, None, :, None], out[:, :, None, :], shaped).reshape(acc.shape)


def local(queries, key_vectors, value_vectors, offsets, out_weight):
    tok = queries.shape[1]
    heads = queries.shape[0] // DH
    seq_count = lax.axis_size("seq")
    far_rate = tok * seq_count // KEYS
    dils = (4, 16, far_rate) if far_rate == 16 else (4, 16)
    branches = len(dils) - 1
    n1, n2 = tok // 4, tok // 16
    bf16, f32 = jnp.bfloat16, jnp.float32
    struct = jax.ShapeDtypeStruct

    by_rows = pl.BlockSpec((DH, tok), lambda h: (h, 0))
    far_spec = pl.BlockSpec((branches, 1, n2, LANES), lambda h: (0, h, 0, 0))
    q1, near, far = pl.pallas_call(
        functools.partial(select_kernel, dils),
        out_shape=(
            struct((heads, n1, DH), bf16),
            struct((heads, n1 + n2, LANES), bf16),
            struct((branches, heads, n2, LANES), bf16),
        ),
        grid=(heads,),
        in_specs=[smem(), by_rows, by_rows, by_rows],
        out_specs=(by_head((n1, DH)), by_head((n1 + n2, LANES)), far_spec),
        scratch_shapes=[pltpu.VMEM((tok, LANES), f32), pltpu.VMEM((tok, DH), f32)],
        compiler_params=params(),
        name="select",
    )(offsets, queries, key_vectors, value_vectors)

    fars = [far] + [partner(far, "seq", apart) for apart in (2, 4, 6)]
    near_other = partner(near, "seq", 1)

    acc = pl.pallas_call(
        local_kernel,
        grid=(heads,),
        out_shape=struct((heads, tok, LANES), f32),
        in_specs=[by_rows, by_rows, by_rows],
        out_specs=by_head((tok, LANES)),
        compiler_params=params(),
        cost_estimate=cost(heads * tok, KEYS),
        name="local",
    )(queries, key_vectors, value_vectors)

    acc = pl.pallas_call(
        functools.partial(pair_kernel, 4),
        grid=(heads,),
        out_shape=struct((heads, tok, LANES), f32),
        in_specs=[smem(), by_head((n1, DH)), by_head((n1 + n2, LANES)), by_head((n1 + n2, LANES)), by_head((tok, LANES))],
        out_specs=by_head((tok, LANES)),
        input_output_aliases={4: 0},
        compiler_params=params(),
        cost_estimate=cost(heads * n1, KEYS),
        name="pair",
    )(offsets, q1, near, near_other, acc)

    if branches == 1:
        shape = (heads, DH, tok)
        my_offsets = lax.dynamic_slice_in_dim(offsets[2], lax.axis_index("head") * heads, heads, 0)
        acc = spread_far(
            acc, queries.reshape(shape), key_vectors.reshape(shape), value_vectors.reshape(shape), far_rate, my_offsets
        )

    fars, acc = lax.optimization_barrier((fars, acc))
    part, send = pl.pallas_call(
        functools.partial(far_kernel, branches),
        grid=(heads,),
        out_shape=(struct((branches, heads, n2, LANES), f32), struct((heads, 2 * n2, LANES), bf16)),
        in_specs=[by_head((n1 + n2, LANES))] * 2 + [far_spec] * 4,
        out_specs=(far_spec, by_head((2 * n2, LANES))),
        compiler_params=params(),
        cost_estimate=cost(heads * n2 * 4, KEYS // 2),
        name="far",
    )(near, near_other, *fars)
    got = partner(send, "seq", 1)

    head_count = lax.axis_size("head")
    width = tok // head_count
    out_spec = pl.BlockSpec((DH, width), lambda h: (h, 0))
    blocks = pl.pallas_call(
        functools.partial(finish_kernel, dils[1:]),
        grid=(heads,),
        out_shape=(struct((heads * DH, width), bf16),) * head_count,
        in_specs=[smem(), by_head((tok, LANES)), far_spec, by_head((2 * n2, LANES))],
        out_specs=(out_spec,) * head_count,
        scratch_shapes=[pltpu.VMEM((tok, LANES), f32)],
        compiler_params=params(),
        name="finish",
    )(offsets, acc, part, got)

    landed = [blocks[0]] + [partner(blocks[s], "head", s) for s in range(1, head_count)]
    return pl.pallas_call(
        project_kernel,
        out_shape=struct((width, out_weight.shape[1]), bf16),
        in_specs=[whole()] * (head_count + 1),
        out_specs=whole(),
        scratch_shapes=[pltpu.VMEM((head_count * heads * DH, width), bf16)],
        compiler_params=params(VMEM_BYTES),
        name="project",
    )(*landed, out_weight)


def solution(mesh):
    in_specs = (P("head", "seq"), P("head", "seq"), P("head", "seq"), P(), P())
    out_specs = P(("seq", "head"), None)
    return jax.shard_map(local, mesh=mesh, in_specs=in_specs, out_specs=out_specs, check_vma=False)
```

```python
import functools
import math

import jax
import jax.numpy as jnp
from jax import lax
from jax.experimental import pallas as pl
from jax.experimental.pallas import tpu as pltpu
from jax.sharding import PartitionSpec as P

DH = 64
KEYS = 1024
LANES = 128
QBLK = 256
EXP2_SCALE = DH ** (-0.5) * math.log2(math.e)
NT = (((1,), (1,)), ((), ()))
NN = (((1,), (0,)), ((), ()))
VMEM_BYTES = 24 << 20
BF16, F32 = jnp.bfloat16, jnp.float32


def dot(a, b, dims):
    return lax.dot_general(a, b, dims, preferred_element_type=F32)


def lane_of(shape):
    return lax.broadcasted_iota(jnp.int32, shape, len(shape) - 1)


def in_values(shape, head):
    return (lane_of(shape) < DH) == (head % 2 == 0)


def stack_halves(values, others, head):
    return jnp.concatenate([values, others] if head % 2 == 0 else [others, values], 0)


def max_lane(head):
    return LANES - 1 if head % 2 == 0 else 0


def max_of(rows, head):
    at = max_lane(head)
    return rows[:, at : at + 1]


def over_sum(rows, head):
    at = DH if head % 2 == 0 else DH - 1
    return rows / rows[:, at : at + 1]


def put_max(rows, row_max, head):
    return jnp.where(lane_of(rows.shape) == max_lane(head), row_max, rows)


def swap(rows):
    return pltpu.roll(rows, DH, 1)


def softmax_block(scores):
    row_max = jnp.max(scores, axis=1, keepdims=True)
    weights = jnp.exp2((scores - row_max) * EXP2_SCALE).astype(BF16)
    return row_max, weights


def merge_rows(cur, cur_max, new, new_max):
    both = jnp.maximum(cur_max, new_max)
    keep_cur = jnp.exp2((cur_max - both) * EXP2_SCALE)
    keep_new = jnp.exp2((new_max - both) * EXP2_SCALE)
    return both, cur * keep_cur + new * keep_new


def select_kernel(dils, off_ref, q_hbm, k_hbm, v_hbm, q_ref, k_ref, v_ref, q1_ref, near_ref, far_ref, kvt, qt, sems):
    heads = q_ref.shape[0] // DH
    tok = q_ref.shape[1]
    n1 = tok // dils[0]
    copies = []
    for h in range(heads):
        rows = pl.ds(h * DH, DH)
        for i, (src, dst) in enumerate(((k_hbm, k_ref), (v_hbm, v_ref), (q_hbm, q_ref))):
            copy = pltpu.make_async_copy(src.at[rows, :], dst.at[rows, :], sems.at[h, i])
            copy.start()
            copies.append(copy)
    for h in range(heads):
        rows = slice(h * DH, (h + 1) * DH)
        head = lax.axis_index("head") * heads + h
        for copy in copies[3 * h : 3 * h + 3]:
            copy.wait()
        kvt[...] = stack_halves(v_ref[rows, :], k_ref[rows, :], h).T.astype(F32)
        query = q_ref[rows, :]
        qt[...] = stack_halves(jnp.zeros_like(query), query, h).T.astype(F32)
        picks = [pl.ds(off_ref[b, head], tok // d, stride=d) for b, d in enumerate(dils)]
        q1_ref[h] = qt[picks[0], :].astype(BF16)
        near_ref[h, :n1, :] = kvt[picks[0], :].astype(BF16)
        far_q = qt[picks[1], :]
        if len(dils) == 3:
            far_q = far_q + swap(qt[picks[2], :])
        near_ref[h, n1:, :] = far_q.astype(BF16)
        for b in range(1, len(dils)):
            far_ref[b - 1, h] = kvt[picks[b], :].astype(BF16)


def local_kernel(q_ref, k_ref, v_ref, acc_ref):
    tok = q_ref.shape[1]
    for h in range(q_ref.shape[0] // DH):
        rows = slice(h * DH, (h + 1) * DH)
        qt = q_ref[rows, :].T
        for seg in range(tok // KEYS):
            cols = slice(seg * KEYS, (seg + 1) * KEYS)
            keys = k_ref[rows, cols]
            vals = v_ref[rows, cols]
            vals = stack_halves(vals, jnp.ones_like(vals), h)
            for blk in range(KEYS // QBLK):
                at = seg * KEYS + blk * QBLK
                row_max, weights = softmax_block(dot(qt[at : at + QBLK], keys, NN))
                acc_ref[h, at : at + QBLK, :] = put_max(dot(weights, vals, NT), row_max, h)


def pair_kernel(dils, off_ref, q_ref, own_ref, other_ref, acc_in, m0, m1, m2, m3, cur_ref, acc):
    heads, n1, _ = q_ref.shape
    tok = acc.shape[0]
    me = lax.axis_index("head")
    mains = (m0, m1, m2, m3)
    width = tok // len(mains)
    held = None
    for h in range(heads):
        head = me * heads + h
        acc[...] = acc_in[h]
        kv = jnp.concatenate([own_ref[h, :n1, :], other_ref[h, :n1, :]], 0)
        vals = jnp.where(in_values(kv.shape, h), kv, jnp.ones_like(kv))
        for blk in range(n1 // QBLK):
            rows = pl.ds(off_ref[0, head] + blk * QBLK * dils[0], QBLK, stride=dils[0])
            row_max, weights = softmax_block(dot(q_ref[h, blk * QBLK : (blk + 1) * QBLK], kv, NT))
            out = dot(weights, vals, NN)
            cur = acc[rows, :]
            both, new = merge_rows(cur, max_of(cur, h), out, row_max)
            acc[rows, :] = put_max(new, both, h)
        for b in range(1, len(dils)):
            cur_ref[b - 1, h] = acc[pl.ds(off_ref[b, head], tok // dils[b], stride=dils[b]), :]
        whole = acc[...]
        done = over_sum(whole, h)
        if h % 2 == 0:
            held = done
            if h + 1 < heads:
                continue
            pieces = []
            for dest in range(len(mains)):
                half = width // 2
                lo = done[dest * width : dest * width + half]
                hi = done[dest * width + half : (dest + 1) * width]
                pieces.append(jnp.where(lane_of(lo.shape) < DH, lo, swap(hi)))
            packed = jnp.concatenate(pieces, 0).astype(BF16)
        else:
            packed = jnp.where(lane_of(done.shape) < DH, held, done).astype(BF16)
        size = packed.shape[0] // len(mains)
        start = (h // 2) * width
        for s, out in enumerate(mains):
            for dest in range(len(mains)):

                @pl.when((me ^ s) == dest)
                def _():
                    out[start : start + size, :] = packed[dest * size : (dest + 1) * size]


def far_kernel(branches, own_ref, other_ref, kv0, kv1, kv2, kv3, part_ref, send_ref):
    heads = own_ref.shape[0]
    n = kv0.shape[2]
    n1 = own_ref.shape[1] - n
    for h in range(heads):
        q_all = jnp.concatenate([own_ref[h, n1:, :], other_ref[h, n1:, :]], 0)
        outs, tops = [], []
        for b in range(branches):
            kv = jnp.concatenate([r[b, h] for r in (kv0, kv1, kv2, kv3)], 0)
            q_b = q_all if b == 0 else swap(q_all.astype(F32)).astype(BF16)
            q_b = jnp.where(in_values(q_b.shape, h), jnp.zeros_like(q_b), q_b)
            row_max, weights = softmax_block(dot(q_b, kv, NT))
            out = dot(weights, jnp.where(in_values(kv.shape, h), kv, jnp.ones_like(kv)), NN)
            part_ref[b, h] = put_max(out[:n], row_max[:n], h)
            outs.append(out[n:])
            tops.append(row_max[n:])
        a_lanes = in_values((n, LANES), h)
        other, other_top = (swap(outs[1]), tops[1]) if branches == 2 else (outs[0], tops[0])
        send_ref[h, :n, :] = jnp.where(a_lanes, outs[0], other).astype(BF16)
        slot = lane_of((n, LANES)) % DH
        stats = jnp.where(
            slot >= 3, jnp.where(a_lanes, other, outs[0]), jnp.where(a_lanes, other_top, tops[0])
        )
        high = stats.astype(BF16).astype(F32)
        mid = (stats - high).astype(BF16).astype(F32)
        low = stats - high - mid
        coded = jnp.where(slot % 3 == 0, high, jnp.where(slot % 3 == 1, mid, low))
        send_ref[h, n:, :] = coded.astype(BF16)


def patch_kernel(branches, off_ref, cur_ref, part_ref, got_ref, p0, p1, p2, p3):
    heads, two_n, _ = got_ref.shape
    n = two_n // 2
    me = lax.axis_index("head")
    patches = (p0, p1, p2, p3)
    size = n // len(patches)
    done = []
    for h in range(heads):
        a_lanes = in_values((n, LANES), h)
        got = got_ref[h, :n, :].astype(F32)
        coded = got_ref[h, n:, :].astype(F32)
        merged, states = [], []
        for b in range(branches):
            c = DH * (1 - h % 2) if b == 0 else DH * (h % 2)
            got_max = coded[:, c : c + 1] + coded[:, c + 1 : c + 2] + coded[:, c + 2 : c + 3]
            got_sum = coded[:, c + 3 : c + 4] + coded[:, c + 4 : c + 5] + coded[:, c + 5 : c + 6]
            new = jnp.where(a_lanes, got if b == 0 else swap(got), got_sum)
            part = part_ref[b, h]
            states.append(merge_rows(part, max_of(part, h), new, got_max))
        head = me * heads + h
        cur = cur_ref[0, h]
        first_max, first = merge_rows(cur, max_of(cur, h), states[0][1], states[0][0])
        merged.append(first)
        if branches == 2:
            same = off_ref[1, head] == off_ref[2, head]
            cur = cur_ref[1, h]
            base = jnp.where(same, first, cur)
            base_max = jnp.where(same, first_max, max_of(cur, h))
            _, second = merge_rows(base, base_max, states[1][1], states[1][0])
            merged = [jnp.where(same, second, first), second]
        done.append([over_sum(m, h) for m in merged])
    lane = lane_of((n, LANES))
    rows = []
    for b in range(branches):
        rows.append(jnp.where(lane < DH, done[0][b], done[1][b]).astype(BF16))
    last = done[2]
    rows.append(jnp.where(lane < DH, last[0], swap(last[-1])).astype(BF16))
    for s, out in enumerate(patches):
        for dest in range(len(patches)):

            @pl.when((me ^ s) == dest)
            def _():
                for i, r in enumerate(rows):
                    out[i * size : (i + 1) * size, :] = r[dest * size : (dest + 1) * size]


def project_kernel(branches, dil, off_ref, x0, x1, x2, x3, p0, p1, p2, p3, w_ref, out_ref, pairs, lasts):
    me = lax.axis_index("head")
    width = out_ref.shape[0]
    half = width // 2
    size = width // dil
    heads = 3
    rows = heads * DH
    sources = [me ^ s for s in range(4)]
    xs, ps = (x0, x1, x2, x3), (p0, p1, p2, p3)
    low = lane_of((size, LANES)) < DH
    for s in range(4):
        pairs[s] = xs[s][:width, :].astype(F32)
    for t in range(2):
        a = xs[2 * t][width:, :].astype(F32)
        b = xs[2 * t + 1][width:, :].astype(F32)
        lane = lane_of(a.shape)
        lasts[t, :half, :] = jnp.where(lane < DH, a, swap(b))
        lasts[t, half:, :] = jnp.where(lane < DH, swap(a), b)
    for s in range(4):
        for b in range(branches):
            new = ps[s][b * size : (b + 1) * size, :].astype(F32)
            for h in range(2):
                at = pl.ds(off_ref[b + 1, sources[s] * heads + h], size, stride=dil)
                pairs[s, at, :] = jnp.where(low == (h == 0), new, pairs[s, at, :])
            new = ps[s][branches * size :, :].astype(F32)
            if b != s % 2:
                new = swap(new)
            at = pl.ds(off_ref[b + 1, sources[s] * heads + 2], size, stride=dil)
            lasts[s // 2, at, :] = jnp.where(low == (s % 2 == 0), new, lasts[s // 2, at, :])

    def w_rows(s, start, count):
        return w_ref[pl.ds(pl.multiple_of(sources[s] * rows + start, DH), count), :]

    total = None
    for t in range(3):
        if t < 2:
            x = jnp.concatenate([pairs[2 * t], pairs[2 * t + 1]], 1)
            w = jnp.concatenate([w_rows(2 * t, 0, LANES), w_rows(2 * t + 1, 0, LANES)], 0)
        else:
            x = jnp.concatenate([lasts[0], lasts[1]], 1)
            w = jnp.concatenate([w_rows(s, LANES, DH) for s in range(4)], 0)
        part = dot(x.astype(BF16), w, NN)
        total = part if total is None else total + part
    out_ref[...] = total.astype(BF16)


def partner(block, axis, apart):
    count = lax.axis_size(axis)
    return lax.ppermute(block, axis, [(i, i ^ apart) for i in range(count)])


def call(kernel, name, outs, in_specs, scratch=(), queries=0, keys=0):
    estimate = None
    if queries:
        estimate = pl.CostEstimate(
            flops=queries * keys * 512, bytes_accessed=queries * 1024, transcendentals=queries * keys
        )
    return pl.pallas_call(
        kernel,
        out_shape=tuple(jax.ShapeDtypeStruct(*o) for o in outs),
        in_specs=in_specs,
        out_specs=(pl.BlockSpec(memory_space=pltpu.VMEM),) * len(outs),
        scratch_shapes=scratch,
        compiler_params=pltpu.CompilerParams(vmem_limit_bytes=VMEM_BYTES),
        cost_estimate=estimate,
        name=name,
    )


def spread_far(acc, query_h, key_h, value_h, dil, head_offsets):
    hit = jnp.arange(dil)[None, :] == head_offsets[:, None]

    def pick(x):
        shaped = x.reshape(x.shape[:2] + (x.shape[2] // dil, dil))
        return jnp.sum(shaped * hit[:, None, None, :].astype(x.dtype), axis=-1, dtype=x.dtype)

    pair = lax.all_gather(jnp.stack([pick(key_h), pick(value_h)], 0), "seq", axis=3, tiled=True)
    scores = jnp.einsum("hdq,hdk->hqk", pick(query_h), pair[0], preferred_element_type=F32)
    new_max = jnp.max(scores, axis=2, keepdims=True)
    e = jnp.exp2((scores - new_max) * EXP2_SCALE)
    new_sum = jnp.sum(e, axis=2, keepdims=True)
    new_acc = jnp.einsum("hqk,hdk->hqd", e.astype(BF16), pair[1], preferred_element_type=F32)
    heads, tok, _ = acc.shape
    shaped = acc.reshape(heads, tok // dil, dil, LANES)
    cur = jnp.sum(jnp.where(hit[:, None, :, None], shaped, 0.0), axis=2)
    sums = jnp.broadcast_to(new_sum, new_acc.shape)
    rows = []
    for h in range(heads):
        halves = [new_acc[h], sums[h]] if h % 2 == 0 else [sums[h], new_acc[h]]
        both, out = merge_rows(cur[h], max_of(cur[h], h), jnp.concatenate(halves, 1), new_max[h])
        rows.append(put_max(out, both, h))
    out = jnp.stack(rows, 0)
    return jnp.where(hit[:, None, :, None], out[:, :, None, :], shaped).reshape(acc.shape)


def local(queries, key_vectors, value_vectors, offsets, out_weight):
    tok = queries.shape[1]
    heads = queries.shape[0] // DH
    seq_count = lax.axis_size("seq")
    far_rate = tok * seq_count // KEYS
    dils = (4, 16, 16) if far_rate == 16 else (4, 16)
    branches = len(dils) - 1
    n1, n2 = tok // 4, tok // 16
    width = tok // 4
    whole = pl.BlockSpec(memory_space=pltpu.VMEM)
    smem = pl.BlockSpec(memory_space=pltpu.SMEM)
    hbm = pl.BlockSpec(memory_space=pltpu.HBM)

    q, k, v, q1, near, far = call(
        functools.partial(select_kernel, dils),
        "select",
        [(queries.shape, BF16)] * 3
        + [
            ((heads, n1, LANES), BF16),
            ((heads, n1 + n2, LANES), BF16),
            ((branches, heads, n2, LANES), BF16),
        ],
        [smem, hbm, hbm, hbm],
        [
            pltpu.VMEM((tok, LANES), F32),
            pltpu.VMEM((tok, LANES), F32),
            pltpu.SemaphoreType.DMA((heads, 3)),
        ],
    )(offsets, queries, key_vectors, value_vectors)

    near_other = partner(near, "seq", 1)
    fars = [far] + [partner(far, "seq", apart) for apart in (2, 4, 6)]

    (acc,) = call(
        local_kernel, "local", [((heads, tok, LANES), F32)], [whole] * 3, queries=heads * tok, keys=KEYS
    )(q, k, v)

    if branches == 1:
        shape = (heads, DH, tok)
        my_offsets = lax.dynamic_slice_in_dim(offsets[2], lax.axis_index("head") * heads, heads, 0)
        parts = [a.reshape(shape) for a in (queries, key_vectors, value_vectors)]
        acc = spread_far(acc, *parts, far_rate, my_offsets)

    *mains, cur = call(
        functools.partial(pair_kernel, dils),
        "pair",
        [((heads * width // 2, LANES), BF16)] * 4 + [((branches, heads, n2, LANES), F32)],
        [smem] + [whole] * 4,
        [pltpu.VMEM((tok, LANES), F32)],
        queries=heads * n1,
        keys=KEYS,
    )(offsets, q1, near, near_other, acc)
    landed = [mains[0]] + [partner(mains[s], "head", s) for s in range(1, 4)]

    fars, cur, landed[1] = lax.optimization_barrier((fars, cur, landed[1]))
    part, send = call(
        functools.partial(far_kernel, branches),
        "far",
        [((branches, heads, n2, LANES), F32), ((heads, 2 * n2, LANES), BF16)],
        [whole] * 6,
        queries=heads * n2 * 4,
        keys=KEYS // 2,
    )(near, near_other, *fars)
    got = partner(send, "seq", 1)

    patches = call(
        functools.partial(patch_kernel, branches),
        "patch",
        [(((branches + 1) * n2 // 4, LANES), BF16)] * 4,
        [smem] + [whole] * 3,
    )(offsets, cur, part, got)
    fixes = [patches[0]] + [partner(patches[s], "head", s) for s in range(1, 4)]

    (out,) = call(
        functools.partial(project_kernel, branches, dils[1]),
        "project",
        [((width, out_weight.shape[1]), BF16)],
        [smem] + [whole] * 9,
        [pltpu.VMEM((4, width, LANES), F32), pltpu.VMEM((2, width, LANES), F32)],
    )(offsets, *landed, *fixes, out_weight)
    return out


def solution(mesh):
    in_specs = (P("head", "seq"), P("head", "seq"), P("head", "seq"), P(), P())
    out_specs = P(("seq", "head"), None)
    return jax.shard_map(local, mesh=mesh, in_specs=in_specs, out_specs=out_specs, check_vma=False)
```

```python
import functools
import math

import jax
import jax.numpy as jnp
from jax import lax
from jax.experimental import pallas as pl
from jax.experimental.pallas import tpu as pltpu
from jax.sharding import PartitionSpec as P

DH = 64
KEYS = 1024
LANES = 128
QBLK = 256
EXP2_SCALE = DH ** (-0.5) * math.log2(math.e)
NT = (((1,), (1,)), ((), ()))
NN = (((1,), (0,)), ((), ()))
VMEM_BYTES = 24 << 20
BF16, F32 = jnp.bfloat16, jnp.float32


def dot(a, b, dims):
    return lax.dot_general(a, b, dims, preferred_element_type=F32)


def lane_of(shape):
    return lax.broadcasted_iota(jnp.int32, shape, len(shape) - 1)


def in_values(shape, head):
    return (lane_of(shape) < DH) == (head % 2 == 0)


def stack_halves(values, others, head):
    return jnp.concatenate([values, others] if head % 2 == 0 else [others, values], 0)


def swap(rows):
    return pltpu.roll(rows, DH, 1)


def softmax_block(scores):
    row_max = jnp.max(scores, axis=1, keepdims=True)
    weights = jnp.exp2((scores - row_max) * EXP2_SCALE).astype(BF16)
    return row_max, weights


def merge_rows(cur, cur_max, new, new_max):
    both = jnp.maximum(cur_max, new_max)
    keep_cur = jnp.exp2((cur_max - both) * EXP2_SCALE)
    keep_new = jnp.exp2((new_max - both) * EXP2_SCALE)
    return both, cur * keep_cur + new * keep_new


def pack_pair(even, odd):
    low = lane_of(even.shape) < DH
    return jnp.where(low, even, odd) / swap(jnp.where(low, odd, even))


def pack_even(first, second):
    low = lane_of(first.shape) < DH
    return jnp.where(low, first, swap(second)) / jnp.where(low, swap(first), second)


def select_kernel(dils, off_hbm, q_hbm, k_hbm, v_hbm, q_ref, k_ref, v_ref, near_ref, far_ref, kvt, off_ref, sems, off_sem):
    heads = q_ref.shape[0] // DH
    tok = q_ref.shape[1]
    off_copy = pltpu.make_async_copy(off_hbm, off_ref, off_sem)
    off_copy.start()
    copies = []
    for h in range(heads):
        rows = pl.ds(h * DH, DH)
        for i, (src, dst) in enumerate(((k_hbm, k_ref), (v_hbm, v_ref))):
            copies.append(pltpu.make_async_copy(src.at[rows, :], dst.at[rows, :], sems.at[h, i]))
            copies[-1].start()
    q_copy = pltpu.make_async_copy(q_hbm, q_ref, sems.at[0, 2])
    q_copy.start()
    off_copy.wait()
    for h in range(heads):
        rows = slice(h * DH, (h + 1) * DH)
        head = lax.axis_index("head") * heads + h
        copies[2 * h].wait()
        copies[2 * h + 1].wait()
        kvt[h] = stack_halves(v_ref[rows, :], k_ref[rows, :], h).T.astype(F32)
        near_ref[h] = kvt[h, pl.ds(off_ref[0, head], tok // dils[0], stride=dils[0]), :].astype(BF16)
        for b in range(1, len(dils)):
            pick = pl.ds(off_ref[b, head], tok // dils[b], stride=dils[b])
            far_ref[b - 1, h] = kvt[h, pick, :].astype(BF16)
    q_copy.wait()


def query_kernel(dils, off_ref, q_ref, q1_ref, q23_ref, qt):
    heads = q_ref.shape[0] // DH
    tok = q_ref.shape[1]
    for h in range(heads):
        head = lax.axis_index("head") * heads + h
        query = q_ref[h * DH : (h + 1) * DH, :]
        qt[h] = stack_halves(jnp.zeros_like(query), query, h).T.astype(F32)
        picks = [pl.ds(off_ref[b, head], tok // d, stride=d) for b, d in enumerate(dils)]
        q1_ref[h] = qt[h, picks[0], :].astype(BF16)
        far_q = qt[h, picks[1], :]
        if len(dils) == 3:
            far_q = far_q + swap(qt[h, picks[2], :])
        q23_ref[h] = far_q.astype(BF16)


def local_kernel(q_ref, k_ref, v_ref, acc_ref, max_ref):
    tok = q_ref.shape[1]
    for h in range(q_ref.shape[0] // DH):
        rows = slice(h * DH, (h + 1) * DH)
        qt = q_ref[rows, :].T
        for seg in range(tok // KEYS):
            cols = slice(seg * KEYS, (seg + 1) * KEYS)
            keys = k_ref[rows, cols]
            vals = v_ref[rows, cols]
            vals = stack_halves(vals, jnp.ones_like(vals), h)
            for blk in range(KEYS // QBLK):
                at = seg * KEYS + blk * QBLK
                row_max, weights = softmax_block(dot(qt[at : at + QBLK], keys, NN))
                acc_ref[h, at : at + QBLK, :] = dot(weights, vals, NT)
                max_ref[h, at : at + QBLK, :] = jnp.broadcast_to(row_max, (QBLK, LANES))


def pair_kernel(dils, off_ref, q_ref, own_ref, other_ref, acc_in, max_in, m0, m1, m2, m3, cur_ref, top_ref, acc, top):
    heads, n1, _ = q_ref.shape
    tok = acc.shape[1]
    me = lax.axis_index("head")
    mains = (m0, m1, m2, m3)
    width = tok // len(mains)
    half = width // 2
    for h in range(heads):
        head = me * heads + h
        kv = jnp.concatenate([own_ref[h], other_ref[h]], 0)
        vals = jnp.where(in_values(kv.shape, h), kv, jnp.ones_like(kv))
        for blk in range(n1 // QBLK):
            rows = pl.ds(off_ref[0, head] + blk * QBLK * dils[0], QBLK, stride=dils[0])
            row_max, weights = softmax_block(dot(q_ref[h, blk * QBLK : (blk + 1) * QBLK], kv, NT))
            out = dot(weights, vals, NN)
            both, new = merge_rows(acc[h, rows, :], top[h, rows, :], out, row_max)
            acc[h, rows, :] = new
            top[h, rows, :] = both
        for b in range(1, len(dils)):
            pick = pl.ds(off_ref[b, head], tok // dils[b], stride=dils[b])
            cur_ref[b - 1, h] = acc[h, pick, :]
            top_ref[b - 1, h] = top[h, pick, :]
        for s, out in enumerate(mains):
            start = pl.multiple_of((me ^ s) * width, width)
            if h == 1:
                rows = pl.ds(start, width)
                out[:width, :] = pack_pair(acc[0, rows, :], acc[1, rows, :]).astype(BF16)
            elif h == 2:
                lo = acc[2, pl.ds(start, half), :]
                hi = acc[2, pl.ds(start + half, half), :]
                out[width:, :] = pack_even(lo, hi).astype(BF16)


def far_kernel(branches, q_own, q_other, kv0, kv1, kv2, kv3, part_ref, top_ref, send_ref):
    heads, n, _ = q_own.shape
    for h in range(heads):
        q_all = jnp.concatenate([q_own[h], q_other[h]], 0)
        outs, tops = [], []
        for b in range(branches):
            kv = jnp.concatenate([r[b, h] for r in (kv0, kv1, kv2, kv3)], 0)
            q_b = q_all if b == 0 else swap(q_all.astype(F32)).astype(BF16)
            q_b = jnp.where(in_values(q_b.shape, h), jnp.zeros_like(q_b), q_b)
            row_max, weights = softmax_block(dot(q_b, kv, NT))
            out = dot(weights, jnp.where(in_values(kv.shape, h), kv, jnp.ones_like(kv)), NN)
            part_ref[b, h] = out[:n]
            top_ref[b, h] = jnp.broadcast_to(row_max[:n], (n, LANES))
            outs.append(out[n:])
            tops.append(row_max[n:])
        a_lanes = in_values((n, LANES), h)
        other, other_top = (swap(outs[1]), tops[1]) if branches == 2 else (outs[0], tops[0])
        send_ref[h, :n, :] = jnp.where(a_lanes, outs[0], other).astype(BF16)
        slot = lane_of((n, LANES)) % DH
        stats = jnp.where(
            slot >= 3, jnp.where(a_lanes, other, outs[0]), jnp.where(a_lanes, other_top, tops[0])
        )
        high = stats.astype(BF16).astype(F32)
        mid = (stats - high).astype(BF16).astype(F32)
        low = stats - high - mid
        coded = jnp.where(slot % 3 == 0, high, jnp.where(slot % 3 == 1, mid, low))
        send_ref[h, n:, :] = coded.astype(BF16)


def patch_kernel(branches, off_ref, cur_ref, cur_top, part_ref, part_top, got_ref, p0, p1, p2, p3, packed):
    heads, two_n, _ = got_ref.shape
    n = two_n // 2
    me = lax.axis_index("head")
    patches = (p0, p1, p2, p3)
    size = n // len(patches)
    spread = []
    for parity in range(2):
        first = lax.broadcasted_iota(jnp.int32, (LANES, 4 * LANES), 0)
        kind = lax.broadcasted_iota(jnp.int32, (LANES, 4 * LANES), 1) // LANES
        base = jnp.where((kind // 2 == 0) == (parity == 0), DH, 0) + 3 * (kind % 2)
        spread.append(jnp.where((first >= base) & (first < base + 3), 1.0, 0.0).astype(BF16))
    done = []
    for h in range(heads):
        a_lanes = in_values((n, LANES), h)
        got = got_ref[h, :n, :].astype(F32)
        stats = dot(got_ref[h, n:, :], spread[h % 2], NN)
        states = []
        for b in range(branches):
            got_max = stats[:, 2 * b * LANES : (2 * b + 1) * LANES]
            got_sum = stats[:, (2 * b + 1) * LANES : (2 * b + 2) * LANES]
            new = jnp.where(a_lanes, got if b == 0 else swap(got), got_sum)
            states.append(merge_rows(part_ref[b, h], part_top[b, h], new, got_max))
        head = me * heads + h
        first_max, first = merge_rows(cur_ref[0, h], cur_top[0, h], states[0][1], states[0][0])
        merged = [first]
        if branches == 2:
            same = off_ref[1, head] == off_ref[2, head]
            base = jnp.where(same, first, cur_ref[1, h])
            base_max = jnp.where(same, first_max, cur_top[1, h])
            _, second = merge_rows(base, base_max, states[1][1], states[1][0])
            merged = [jnp.where(same, second, first), second]
        done.append(merged)
    for b in range(branches):
        packed[b] = pack_pair(done[0][b], done[1][b])
    packed[branches] = pack_even(done[2][0], done[2][-1])
    for s, out in enumerate(patches):
        start = pl.multiple_of((me ^ s) * size, size)
        for i in range(branches + 1):
            out[i * size : (i + 1) * size, :] = packed[i, pl.ds(start, size), :].astype(BF16)


def project_kernel(branches, dil, off_ref, x0, x1, x2, x3, p0, p1, p2, p3, w_ref, out_hbm, pairs, lasts, out_ref, sems):
    me = lax.axis_index("head")
    width = out_ref.shape[0]
    half = width // 2
    size = width // dil
    heads = 3
    rows = heads * DH
    sources = [me ^ s for s in range(4)]
    xs, ps = (x0, x1, x2, x3), (p0, p1, p2, p3)
    low = lane_of((size, LANES)) < DH
    for s in range(4):
        pairs[s] = xs[s][:width, :].astype(F32)
    for t in range(2):
        a = xs[2 * t][width:, :].astype(F32)
        b = xs[2 * t + 1][width:, :].astype(F32)
        lane = lane_of(a.shape)
        lasts[t, :half, :] = jnp.where(lane < DH, a, swap(b))
        lasts[t, half:, :] = jnp.where(lane < DH, swap(a), b)
    for s in range(4):
        for b in range(branches):
            new = ps[s][b * size : (b + 1) * size, :].astype(F32)
            for h in range(2):
                at = pl.ds(off_ref[b + 1, sources[s] * heads + h], size, stride=dil)
                pairs[s, at, :] = jnp.where(low == (h == 0), new, pairs[s, at, :])
            new = ps[s][branches * size :, :].astype(F32)
            if b != s % 2:
                new = swap(new)
            at = pl.ds(off_ref[b + 1, sources[s] * heads + 2], size, stride=dil)
            lasts[s // 2, at, :] = jnp.where(low == (s % 2 == 0), new, lasts[s // 2, at, :])

    def w_rows(s, start, count):
        return w_ref[pl.ds(pl.multiple_of(sources[s] * rows + start, DH), count), :]

    ws = [jnp.concatenate([w_rows(2 * t, 0, LANES), w_rows(2 * t + 1, 0, LANES)], 0) for t in range(2)]
    ws.append(jnp.concatenate([w_rows(s, LANES, DH) for s in range(4)], 0))
    copies = []
    step = width // 4
    for c in range(4):
        at = slice(c * step, (c + 1) * step)
        total = None
        for t in range(3):
            halves = (pairs[2 * t, at], pairs[2 * t + 1, at]) if t < 2 else (lasts[0, at], lasts[1, at])
            part = dot(jnp.concatenate(halves, 1).astype(BF16), ws[t], NN)
            total = part if total is None else total + part
        out_ref[at, :] = total.astype(BF16)
        copies.append(pltpu.make_async_copy(out_ref.at[pl.ds(c * step, step), :], out_hbm.at[pl.ds(c * step, step), :], sems.at[c]))
        copies[-1].start()
    for copy in copies:
        copy.wait()


def partner(block, axis, apart):
    count = lax.axis_size(axis)
    return lax.ppermute(block, axis, [(i, i ^ apart) for i in range(count)])


def call(kernel, name, outs, in_specs, scratch=(), queries=0, keys=0, aliases={}, space=pltpu.VMEM):
    estimate = None
    if queries:
        estimate = pl.CostEstimate(
            flops=queries * keys * 512, bytes_accessed=queries * 1024, transcendentals=queries * keys
        )
    return pl.pallas_call(
        kernel,
        out_shape=tuple(jax.ShapeDtypeStruct(*o) for o in outs),
        in_specs=in_specs,
        out_specs=(pl.BlockSpec(memory_space=space),) * len(outs),
        input_output_aliases=aliases,
        scratch_shapes=scratch,
        compiler_params=pltpu.CompilerParams(vmem_limit_bytes=VMEM_BYTES),
        cost_estimate=estimate,
        name=name,
    )


def spread_far(acc, top, query_h, key_h, value_h, dil, head_offsets):
    hit = jnp.arange(dil)[None, :] == head_offsets[:, None]

    def pick(x):
        shaped = x.reshape(x.shape[:2] + (x.shape[2] // dil, dil))
        return jnp.sum(shaped * hit[:, None, None, :].astype(x.dtype), axis=-1, dtype=x.dtype)

    pair = lax.all_gather(jnp.stack([pick(key_h), pick(value_h)], 0), "seq", axis=3, tiled=True)
    scores = jnp.einsum("hdq,hdk->hqk", pick(query_h), pair[0], preferred_element_type=F32)
    new_max = jnp.max(scores, axis=2, keepdims=True)
    e = jnp.exp2((scores - new_max) * EXP2_SCALE)
    new_sum = jnp.sum(e, axis=2, keepdims=True)
    new_acc = jnp.einsum("hqk,hdk->hqd", e.astype(BF16), pair[1], preferred_element_type=F32)
    heads, tok, _ = acc.shape
    shaped = acc.reshape(heads, tok // dil, dil, LANES)
    cur = jnp.sum(jnp.where(hit[:, None, :, None], shaped, 0.0), axis=2)
    sums = jnp.broadcast_to(new_sum, new_acc.shape)
    cur_top = jnp.sum(jnp.where(hit[:, None, :, None], top.reshape(shaped.shape), 0.0), axis=2)
    rows = []
    for h in range(heads):
        halves = [new_acc[h], sums[h]] if h % 2 == 0 else [sums[h], new_acc[h]]
        rows.append(merge_rows(cur[h], cur_top[h], jnp.concatenate(halves, 1), new_max[h]))

    def put(update, old):
        return jnp.where(hit[:, None, :, None], update[:, :, None, :], old).reshape(acc.shape)

    out_top, out = (jnp.stack(r, 0) for r in zip(*rows))
    return put(out, shaped), put(out_top, top.reshape(shaped.shape))


def local(queries, key_vectors, value_vectors, offsets, out_weight):
    tok = queries.shape[1]
    heads = queries.shape[0] // DH
    seq_count = lax.axis_size("seq")
    far_rate = tok * seq_count // KEYS
    dils = (4, 16, 16) if far_rate == 16 else (4, 16)
    branches = len(dils) - 1
    n1, n2 = tok // 4, tok // 16
    width = tok // 4
    whole = pl.BlockSpec(memory_space=pltpu.VMEM)
    smem = pl.BlockSpec(memory_space=pltpu.SMEM)
    hbm = pl.BlockSpec(memory_space=pltpu.HBM)
    far_shape = ((branches, heads, n2, LANES), F32)
    acc_shape = ((heads, tok, LANES), F32)

    stay = [
        pltpu.with_memory_space_constraint(a, pltpu.HBM) for a in (offsets, queries, key_vectors, value_vectors)
    ]
    q, k, v, near, far = call(
        functools.partial(select_kernel, dils),
        "select",
        [(queries.shape, BF16)] * 3 + [((heads, n1, LANES), BF16), ((branches, heads, n2, LANES), BF16)],
        [hbm] * 4,
        [
            pltpu.VMEM((heads, tok, LANES), F32),
            pltpu.SMEM(offsets.shape, jnp.int32),
            pltpu.SemaphoreType.DMA((heads, 3)),
            pltpu.SemaphoreType.DMA,
        ],
    )(*stay)
    fars = [far] + [partner(far, "seq", apart) for apart in (2, 4, 6)]
    near_other = partner(near, "seq", 1)

    q1, q23 = call(
        functools.partial(query_kernel, dils),
        "query",
        [((heads, n1, LANES), BF16), ((heads, n2, LANES), BF16)],
        [smem, whole],
        [pltpu.VMEM((heads, tok, LANES), F32)],
    )(offsets, q)
    q23_other = partner(q23, "seq", 1)

    acc, top = call(local_kernel, "local", [acc_shape] * 2, [whole] * 3, queries=heads * tok, keys=KEYS)(q, k, v)

    if branches == 1:
        shape = (heads, DH, tok)
        my_offsets = lax.dynamic_slice_in_dim(offsets[2], lax.axis_index("head") * heads, heads, 0)
        parts = [a.reshape(shape) for a in (queries, key_vectors, value_vectors)]
        acc, top = spread_far(acc, top, *parts, far_rate, my_offsets)

    acc, q23_other = lax.optimization_barrier((acc, q23_other))
    *mains, cur, cur_top, _, _ = call(
        functools.partial(pair_kernel, dils),
        "pair",
        [((heads * width // 2, LANES), BF16)] * 4 + [far_shape] * 2 + [acc_shape] * 2,
        [smem] + [whole] * 5,
        queries=heads * n1,
        keys=KEYS,
        aliases={4: 6, 5: 7},
    )(offsets, q1, near, near_other, acc, top)
    landed = [mains[0]] + [partner(mains[s], "head", s) for s in range(1, 4)]

    fars, cur, landed[1] = lax.optimization_barrier((fars, cur, landed[1]))
    part, part_top, send = call(
        functools.partial(far_kernel, branches),
        "far",
        [far_shape] * 2 + [((heads, 2 * n2, LANES), BF16)],
        [whole] * 6,
        queries=heads * n2 * 4,
        keys=KEYS // 2,
    )(q23, q23_other, *fars)
    got = partner(send, "seq", 1)

    patches = call(
        functools.partial(patch_kernel, branches),
        "patch",
        [(((branches + 1) * n2 // 4, LANES), BF16)] * 4,
        [smem] + [whole] * 5,
        [pltpu.VMEM((branches + 1, n2, LANES), F32)],
    )(offsets, cur, cur_top, part, part_top, got)
    fixes = [patches[0]] + [partner(patches[s], "head", s) for s in range(1, 4)]

    out_shape = (width, out_weight.shape[1])
    (out,) = call(
        functools.partial(project_kernel, branches, dils[1]),
        "project",
        [(out_shape, BF16)],
        [smem] + [whole] * 9,
        [
            pltpu.VMEM((4, width, LANES), F32),
            pltpu.VMEM((2, width, LANES), F32),
            pltpu.VMEM(out_shape, BF16),
            pltpu.SemaphoreType.DMA((4,)),
        ],
        space=pltpu.HBM,
    )(offsets, *landed, *fixes, out_weight)
    return out


def solution(mesh):
    in_specs = (P("head", "seq"), P("head", "seq"), P("head", "seq"), P(), P())
    out_specs = P(("seq", "head"), None)
    return jax.shard_map(local, mesh=mesh, in_specs=in_specs, out_specs=out_specs, check_vma=False)
```

```python
import functools
import math

import jax
import jax.numpy as jnp
from jax import lax
from jax.experimental import pallas as pl
from jax.experimental.pallas import tpu as pltpu
from jax.sharding import PartitionSpec as P

DH = 64
KEYS = 1024
LANES = 128
QBLK = 256
EXP2_SCALE = DH ** (-0.5) * math.log2(math.e)
NT = (((1,), (1,)), ((), ()))
NN = (((1,), (0,)), ((), ()))
STATS = 16
VMEM_BYTES = 24 << 20
COVER = dict(select=6, query=4, local=25, far=1, pair=3, patch=5, arrange=4, project=6)
BF16, F32 = jnp.bfloat16, jnp.float32


def dot(a, b, dims):
    return lax.dot_general(a, b, dims, preferred_element_type=F32)


def lane_of(shape):
    return lax.broadcasted_iota(jnp.int32, shape, len(shape) - 1)


def in_values(shape, head):
    return (lane_of(shape) < DH) == (head % 2 == 0)


def stack_halves(values, others, head):
    return jnp.concatenate([values, others] if head % 2 == 0 else [others, values], 0)


def swap(rows):
    return pltpu.roll(rows, DH, 1)


def softmax_block(scores):
    row_max = jnp.max(scores, axis=1, keepdims=True)
    weights = jnp.exp2((scores - row_max) * EXP2_SCALE).astype(BF16)
    return row_max, weights


def attend(items):
    scores = items[0][0]()
    for i, (_, values, sink) in enumerate(items):
        ahead = items[i + 1][0]() if i + 1 < len(items) else None
        row_max, weights = softmax_block(scores)
        sink(row_max, values(weights))
        scores = ahead


def merge_rows(cur, cur_max, new, new_max):
    both = jnp.maximum(cur_max, new_max)
    keep_cur = jnp.exp2((cur_max - both) * EXP2_SCALE)
    keep_new = jnp.exp2((new_max - both) * EXP2_SCALE)
    return both, cur * keep_cur + new * keep_new


def pack_pair(even, odd):
    low = lane_of(even.shape) < DH
    return jnp.where(low, even, odd) / swap(jnp.where(low, odd, even))


def pack_even(first, second):
    low = lane_of(first.shape) < DH
    return jnp.where(low, first, swap(second)) / jnp.where(low, swap(first), second)


def select_kernel(dils, off_hbm, q_hbm, k_hbm, v_hbm, q_ref, k_ref, v_ref, near_ref, far_ref, kvt, off_ref, sems, off_sem):
    heads = q_ref.shape[0] // DH
    tok = q_ref.shape[1]
    off_copy = pltpu.make_async_copy(off_hbm, off_ref, off_sem)
    off_copy.start()
    copies = []
    for h in range(heads):
        rows = pl.ds(h * DH, DH)
        for i, (src, dst) in enumerate(((k_hbm, k_ref), (v_hbm, v_ref))):
            copies.append(pltpu.make_async_copy(src.at[rows, :], dst.at[rows, :], sems.at[h, i]))
            copies[-1].start()
    q_copy = pltpu.make_async_copy(q_hbm, q_ref, sems.at[0, 2])
    q_copy.start()
    off_copy.wait()
    for h in range(heads):
        rows = slice(h * DH, (h + 1) * DH)
        head = lax.axis_index("head") * heads + h
        copies[2 * h].wait()
        copies[2 * h + 1].wait()
        kvt[h] = stack_halves(v_ref[rows, :], k_ref[rows, :], h).T.astype(F32)
        near_ref[h] = kvt[h, pl.ds(off_ref[0, head], tok // dils[0], stride=dils[0]), :].astype(BF16)
        for b in range(1, len(dils)):
            pick = pl.ds(off_ref[b, head], tok // dils[b], stride=dils[b])
            far_ref[b - 1, h] = kvt[h, pick, :].astype(BF16)
    q_copy.wait()


def query_kernel(dils, off_hbm, q_ref, q1_ref, q23_ref, qt, off_ref, off_sem):
    heads = q_ref.shape[0] // DH
    tok = q_ref.shape[1]
    copy = pltpu.make_async_copy(off_hbm, off_ref, off_sem)
    copy.start()
    for h in range(heads):
        head = lax.axis_index("head") * heads + h
        query = q_ref[h * DH : (h + 1) * DH, :]
        qt[h] = stack_halves(jnp.zeros_like(query), query, h).T.astype(F32)
        if h == 0:
            copy.wait()
        picks = [pl.ds(off_ref[b, head], tok // d, stride=d) for b, d in enumerate(dils)]
        q1_ref[h] = qt[h, picks[0], :].astype(BF16)
        far_q = qt[h, picks[1], :]
        if len(dils) == 3:
            far_q = far_q + swap(qt[h, picks[2], :])
        q23_ref[h] = far_q.astype(BF16)


def local_kernel(q_ref, k_ref, v_ref, acc_ref, max_ref, own_ref, core_ref, far_ref, qts):
    heads = q_ref.shape[0] // DH
    tok = q_ref.shape[1]
    width = tok // 4
    half = width // 2
    size = own_ref.shape[0]
    me = lax.axis_index("head")
    mains = (own_ref, core_ref, far_ref.at[:size, :], far_ref.at[size:, :])
    items = []

    def block(h, seg, keys, vals, s, part):
        start = pl.multiple_of((me ^ s) * width + part * half, half)
        at = pl.ds(start, half)

        def sink(row_max, out):
            acc_ref[h, at, :] = out
            max_ref[h, at, :] = jnp.broadcast_to(row_max, out.shape)
            if h == 1:
                mains[s][part * half : (part + 1) * half, :] = pack_pair(acc_ref[0, at, :], out).astype(BF16)
            elif h == 2 and part == 1:
                first = acc_ref[2, pl.ds(start - half, half), :]
                mains[s][width:, :] = pack_even(first, out).astype(BF16)

        items.append((lambda: dot(qts[h, at, :], keys, NN), lambda weights: dot(weights, vals, NT), sink))

    for h in range(heads):
        rows = slice(h * DH, (h + 1) * DH)
        qts[h] = q_ref[rows, :].T
        for pair in range(2):
            cols = pl.ds(pl.multiple_of(((me // 2) ^ pair) * KEYS, KEYS), KEYS)
            keys = k_ref[rows, cols]
            vals = v_ref[rows, cols]
            vals = stack_halves(vals, jnp.ones_like(vals), h)
            for s in (2 * pair, 2 * pair + 1):
                for part in range(2):
                    block(h, pair, keys, vals, s, part)
    attend(items)


def pair_kernel(dils, off_ref, q_ref, own_ref, other_ref, acc_in, max_in, p0, p1, p2, p3, cur_ref, top_ref, acc, top, merged):
    heads, n1, _ = q_ref.shape
    tok = acc.shape[1]
    me = lax.axis_index("head")
    patches = (p0, p1, p2, p3)
    size = n1 // len(patches)
    half = size // 2
    items = []

    def block(h, kv, vals, blk):
        rows = pl.ds(off_ref[0, me * heads + h] + blk * QBLK * dils[0], QBLK, stride=dils[0])

        def sink(row_max, out):
            both, new = merge_rows(acc[h, rows, :], top[h, rows, :], out, row_max)
            acc[h, rows, :] = new
            top[h, rows, :] = both
            merged[h, blk * QBLK : (blk + 1) * QBLK, :] = new
            if (blk + 1) * QBLK == n1:
                finish(h)

        query = q_ref[h, blk * QBLK : (blk + 1) * QBLK]
        items.append((lambda: dot(query, kv, NT), lambda weights: dot(weights, vals, NN), sink))

    def finish(h):
        for b in range(1, len(dils)):
            pick = pl.ds(off_ref[b, me * heads + h], tok // dils[b], stride=dils[b])
            cur_ref[b - 1, h] = acc[h, pick, :]
            top_ref[b - 1, h] = top[h, pick, :]
        for s, out in enumerate(patches):
            start = pl.multiple_of((me ^ s) * size, size)
            if h == 1:
                rows = pl.ds(start, size)
                out[:size, :] = pack_pair(merged[0, rows, :], merged[1, rows, :]).astype(BF16)
            elif h == 2:
                lo = merged[2, pl.ds(start, half), :]
                hi = merged[2, pl.ds(start + half, half), :]
                out[size : size + half, :] = pack_even(lo, hi).astype(BF16)

    for h in range(heads):
        kv = jnp.concatenate([own_ref[h], other_ref[h]], 0)
        vals = jnp.where(in_values(kv.shape, h), kv, jnp.ones_like(kv))
        for blk in range(n1 // QBLK):
            block(h, kv, vals, blk)
    attend(items)


def far_kernel(branches, q_own, q_other, kv0, kv1, kv2, kv3, part_ref, top_ref, send_ref):
    heads, n, _ = q_own.shape
    a_lanes = [in_values((n, LANES), h) for h in range(2)]
    items = []
    held = {}

    def block(h, b, query, kv, vals):
        def sink(row_max, out):
            part_ref[b, h] = out[:n]
            top_ref[b, h] = jnp.broadcast_to(row_max[:n], (n, LANES))
            held[b] = out[n:], row_max[n:]
            if b == branches - 1:
                pack(h)

        items.append((lambda: dot(query, kv, NT), lambda weights: dot(weights, vals, NN), sink))

    def pack(h):
        first, first_top = held[0]
        other, other_top = held[branches - 1]
        if branches == 2:
            other = swap(other)
        mine = a_lanes[h % 2]
        send_ref[h, :n, :] = jnp.where(mine, first, other).astype(BF16)
        slot = lane_of((n, LANES)) % DH
        stats = jnp.where(slot >= 3, jnp.where(mine, other, first), jnp.where(mine, other_top, first_top))
        high = stats.astype(BF16).astype(F32)
        mid = (stats - high).astype(BF16).astype(F32)
        low = stats - high - mid
        coded = jnp.where(slot % 3 == 0, high, jnp.where(slot % 3 == 1, mid, low))
        coded = coded.T
        send_ref[h, n : n + STATS, :] = coded[:STATS].astype(BF16)
        send_ref[h, n + STATS :, :] = coded[DH : DH + STATS].astype(BF16)

    for h in range(heads):
        q_all = jnp.concatenate([q_own[h], q_other[h]], 0)
        for b in range(branches):
            kv = jnp.concatenate([r[b, h] for r in (kv0, kv1, kv2, kv3)], 0)
            query = q_all if b == 0 else swap(q_all.astype(F32)).astype(BF16)
            query = jnp.where(in_values(query.shape, h), jnp.zeros_like(query), query)
            block(h, b, query, kv, jnp.where(in_values(kv.shape, h), kv, jnp.ones_like(kv)))
    attend(items)


def patch_kernel(branches, off_ref, cur_ref, cur_top, part_ref, part_top, got_ref, i0, i1, i2, i3, p0, p1, p2, p3, packed):
    heads, n = cur_ref.shape[1:3]
    me = lax.axis_index("head")
    patches = (p0, p1, p2, p3)
    size = n // len(patches)
    spread = []
    for parity in range(2):
        first = lax.broadcasted_iota(jnp.int32, (2 * STATS, 4 * LANES), 0)
        kind = lax.broadcasted_iota(jnp.int32, (2 * STATS, 4 * LANES), 1) // LANES
        base = jnp.where((kind // 2 == 0) == (parity == 0), STATS, 0) + 3 * (kind % 2)
        spread.append(jnp.where((first >= base) & (first < base + 3), 1.0, 0.0).astype(BF16))
    done = []
    for h in range(heads):
        a_lanes = in_values((n, LANES), h)
        got = got_ref[h, :n, :].astype(F32)
        stats = dot(got_ref[h, n:, :], spread[h % 2], (((0,), (0,)), ((), ())))
        states = []
        for b in range(branches):
            got_max = stats[:, 2 * b * LANES : (2 * b + 1) * LANES]
            got_sum = stats[:, (2 * b + 1) * LANES : (2 * b + 2) * LANES]
            new = jnp.where(a_lanes, got if b == 0 else swap(got), got_sum)
            states.append(merge_rows(part_ref[b, h], part_top[b, h], new, got_max))
        head = me * heads + h
        first_max, first = merge_rows(cur_ref[0, h], cur_top[0, h], states[0][1], states[0][0])
        merged = [first]
        if branches == 2:
            same = off_ref[1, head] == off_ref[2, head]
            base = jnp.where(same, first, cur_ref[1, h])
            base_max = jnp.where(same, first_max, cur_top[1, h])
            _, second = merge_rows(base, base_max, states[1][1], states[1][0])
            merged = [jnp.where(same, second, first), second]
        done.append(merged)
    for b in range(branches):
        packed[b] = pack_pair(done[0][b], done[1][b])
    packed[branches] = pack_even(done[2][0], done[2][-1])
    for s, out in enumerate(patches):
        start = pl.multiple_of((me ^ s) * size, size)
        base = out.shape[0] - (branches + 1) * size
        for i in range(branches + 1):
            out[base + i * size : base + (i + 1) * size, :] = packed[i, pl.ds(start, size), :].astype(BF16)


def arrange_kernel(x0, x1, x2, x3, pairs, lasts):
    count = x0.shape[0]
    width = pairs.shape[1]
    half = width // 2
    xs = (x0, x1, x2.at[:count, :], x3.at[count:, :])
    for s in range(4):
        pairs[s] = xs[s][:width, :].astype(F32)
    for t in range(2):
        a = xs[2 * t][width:, :].astype(F32)
        b = xs[2 * t + 1][width:, :].astype(F32)
        lane = lane_of(a.shape)
        lasts[t, :half, :] = jnp.where(lane < DH, a, swap(b))
        lasts[t, half:, :] = jnp.where(lane < DH, swap(a), b)


def project_kernel(dils, off_ref, pairs_in, lasts_in, p0, p1, p2, p3, w_ref, out_hbm, pairs, lasts, out_ref, sems):
    me = lax.axis_index("head")
    width = out_ref.shape[0]
    branches = len(dils) - 1
    near = width // dils[0]
    size = width // dils[1]
    heads = 3
    rows = heads * DH
    sources = [me ^ s for s in range(4)]
    ps = (p0, p1, p2, p3)

    def put(ref, index, branch, source, h, first, new, in_low):
        dil = dils[branch]
        at = pl.ds(off_ref[branch, sources[source] * heads + h] + first * dil, new.shape[0], stride=dil)
        old = ref[index, at, :]
        ref[index, at, :] = jnp.where((lane_of(new.shape) < DH) == in_low, new, old)

    for s in range(4):
        in_low = s % 2 == 0
        new = ps[s][:near, :].astype(F32)
        for h in range(2):
            put(pairs, s, 0, s, h, 0, new, h == 0)
        new = ps[s][near : near + near // 2, :].astype(F32)
        turned = swap(new)
        put(lasts, s // 2, 0, s, 2, 0, new if in_low else turned, in_low)
        put(lasts, s // 2, 0, s, 2, near // 2, turned if in_low else new, in_low)
        base = near + near // 2
        for b in range(branches):
            new = ps[s][base + b * size : base + (b + 1) * size, :].astype(F32)
            for h in range(2):
                put(pairs, s, b + 1, s, h, 0, new, h == 0)
            new = ps[s][base + branches * size :, :].astype(F32)
            if b != s % 2:
                new = swap(new)
            put(lasts, s // 2, b + 1, s, 2, 0, new, in_low)

    def w_rows(s, start, count):
        return w_ref[pl.ds(pl.multiple_of(sources[s] * rows + start, DH), count), :]

    ws = [jnp.concatenate([w_rows(2 * t, 0, LANES), w_rows(2 * t + 1, 0, LANES)], 0) for t in range(2)]
    ws.append(jnp.concatenate([w_rows(s, LANES, DH) for s in range(4)], 0))
    copies = []
    step = width // 4
    for c in range(4):
        at = slice(c * step, (c + 1) * step)
        total = None
        for t in range(3):
            halves = (pairs[2 * t, at], pairs[2 * t + 1, at]) if t < 2 else (lasts[0, at], lasts[1, at])
            part = dot(jnp.concatenate(halves, 1).astype(BF16), ws[t], NN)
            total = part if total is None else total + part
        out_ref[at, :] = total.astype(BF16)
        copies.append(pltpu.make_async_copy(out_ref.at[pl.ds(c * step, step), :], out_hbm.at[pl.ds(c * step, step), :], sems.at[c]))
        copies[-1].start()
    for copy in copies:
        copy.wait()


def partner(block, axis, apart):
    count = lax.axis_size(axis)
    return lax.ppermute(block, axis, [(i, i ^ apart) for i in range(count)])


def call(kernel, name, outs, in_specs, scratch=(), aliases={}, spaces=None):
    estimate = pl.CostEstimate(flops=int(COVER[name] * 1e9), bytes_accessed=1024, transcendentals=0)
    return pl.pallas_call(
        kernel,
        out_shape=tuple(jax.ShapeDtypeStruct(*o) for o in outs),
        in_specs=in_specs,
        out_specs=tuple(pl.BlockSpec(memory_space=m) for m in spaces or (pltpu.VMEM,) * len(outs)),
        input_output_aliases=aliases,
        scratch_shapes=scratch,
        compiler_params=pltpu.CompilerParams(vmem_limit_bytes=VMEM_BYTES),
        cost_estimate=estimate,
        name=name,
    )


def spread_far(acc, top, query_h, key_h, value_h, dil, head_offsets):
    hit = jnp.arange(dil)[None, :] == head_offsets[:, None]

    def pick(x):
        shaped = x.reshape(x.shape[:2] + (x.shape[2] // dil, dil))
        return jnp.sum(shaped * hit[:, None, None, :].astype(x.dtype), axis=-1, dtype=x.dtype)

    pair = lax.all_gather(jnp.stack([pick(key_h), pick(value_h)], 0), "seq", axis=3, tiled=True)
    scores = jnp.einsum("hdq,hdk->hqk", pick(query_h), pair[0], preferred_element_type=F32)
    new_max = jnp.max(scores, axis=2, keepdims=True)
    e = jnp.exp2((scores - new_max) * EXP2_SCALE)
    new_sum = jnp.sum(e, axis=2, keepdims=True)
    new_acc = jnp.einsum("hqk,hdk->hqd", e.astype(BF16), pair[1], preferred_element_type=F32)
    heads, tok, _ = acc.shape
    shaped = acc.reshape(heads, tok // dil, dil, LANES)
    cur = jnp.sum(jnp.where(hit[:, None, :, None], shaped, 0.0), axis=2)
    sums = jnp.broadcast_to(new_sum, new_acc.shape)
    cur_top = jnp.sum(jnp.where(hit[:, None, :, None], top.reshape(shaped.shape), 0.0), axis=2)
    rows = []
    for h in range(heads):
        halves = [new_acc[h], sums[h]] if h % 2 == 0 else [sums[h], new_acc[h]]
        rows.append(merge_rows(cur[h], cur_top[h], jnp.concatenate(halves, 1), new_max[h]))

    def put(update, old):
        return jnp.where(hit[:, None, :, None], update[:, :, None, :], old).reshape(acc.shape)

    out_top, out = (jnp.stack(r, 0) for r in zip(*rows))
    return put(out, shaped), put(out_top, top.reshape(shaped.shape))


def packed_mains(acc):
    heads, tok, _ = acc.shape
    width = tok // 4
    me = lax.axis_index("head")
    rows = []
    for h in range(heads):
        low, high = acc[h, :, :DH], acc[h, :, DH:]
        rows.append(low / high if h % 2 == 0 else high / low)
    blocks = []
    for s in range(4):
        mine = [lax.dynamic_slice_in_dim(r, (me ^ s) * width, width, 0) for r in rows]
        last = jnp.concatenate([mine[2][: width // 2], mine[2][width // 2 :]], 1)
        blocks.append(jnp.concatenate([jnp.concatenate(mine[:2], 1), last], 0).astype(BF16))
    return blocks[0], blocks[1], jnp.concatenate(blocks[2:], 0)


def local(queries, key_vectors, value_vectors, offsets, out_weight):
    tok = queries.shape[1]
    heads = queries.shape[0] // DH
    seq_count = lax.axis_size("seq")
    far_rate = tok * seq_count // KEYS
    dils = (4, 16, 16) if far_rate == 16 else (4, 16)
    branches = len(dils) - 1
    n1, n2 = tok // 4, tok // 16
    width = tok // 4
    whole = pl.BlockSpec(memory_space=pltpu.VMEM)
    smem = pl.BlockSpec(memory_space=pltpu.SMEM)
    hbm = pl.BlockSpec(memory_space=pltpu.HBM)
    far_shape = ((branches, heads, n2, LANES), F32)
    acc_shape = ((heads, tok, LANES), F32)

    stay = [
        pltpu.with_memory_space_constraint(a, pltpu.HBM) for a in (offsets, queries, key_vectors, value_vectors)
    ]
    q, k, v, near, far = call(
        functools.partial(select_kernel, dils),
        "select",
        [(queries.shape, BF16)] * 3 + [((heads, n1, LANES), BF16), ((branches, heads, n2, LANES), BF16)],
        [hbm] * 4,
        [
            pltpu.VMEM((heads, tok, LANES), F32),
            pltpu.SMEM(offsets.shape, jnp.int32),
            pltpu.SemaphoreType.DMA((heads, 3)),
            pltpu.SemaphoreType.DMA,
        ],
    )(*stay)
    fars = [far] + [partner(far, "seq", apart) for apart in (2, 4, 6)]
    near_other = partner(near, "seq", 1)

    q1, q23 = call(
        functools.partial(query_kernel, dils),
        "query",
        [((heads, n1, LANES), BF16), ((heads, n2, LANES), BF16)],
        [hbm, whole],
        [
            pltpu.VMEM((heads, tok, LANES), F32),
            pltpu.SMEM(offsets.shape, jnp.int32),
            pltpu.SemaphoreType.DMA,
        ],
    )(stay[0], q)
    q23_other = partner(q23, "seq", 1)

    q, q23 = lax.optimization_barrier((q, q23))
    main = heads * width // 2
    acc, top, m_own, m_core, m_far = call(
        local_kernel,
        "local",
        [acc_shape] * 2 + [((main, LANES), BF16)] * 2 + [((2 * main, LANES), BF16)],
        [whole] * 3,
        [pltpu.VMEM((heads, tok, DH), BF16)],
    )(q, k, v)

    if branches == 1:
        shape = (heads, DH, tok)
        my_offsets = lax.dynamic_slice_in_dim(offsets[2], lax.axis_index("head") * heads, heads, 0)
        parts = [a.reshape(shape) for a in (queries, key_vectors, value_vectors)]
        acc, top = spread_far(acc, top, *parts, far_rate, my_offsets)
        m_own, m_core, m_far = packed_mains(acc)

    m_far, q23_other = lax.optimization_barrier((m_far, q23_other))
    y_in = partner(m_far, "head", 2)
    core_in = partner(m_core, "head", 1)

    patch_rows = n1 // 4 * 3 // 2 + (branches + 1) * n2 // 4
    fars, acc = lax.optimization_barrier((fars, acc))
    part, part_top, send = call(
        functools.partial(far_kernel, branches),
        "far",
        [far_shape] * 2 + [((heads, n2 + 2 * STATS, LANES), BF16)],
        [whole] * 6,
    )(q23, q23_other, *fars)
    acc, part = lax.optimization_barrier((acc, part))
    *patches, cur, cur_top, _, _ = call(
        functools.partial(pair_kernel, dils),
        "pair",
        [((patch_rows, LANES), BF16)] * 4 + [far_shape] * 2 + [acc_shape] * 2,
        [smem] + [whole] * 5,
        [pltpu.VMEM((heads, n1, LANES), F32)],
        aliases={4: 6, 5: 7},
    )(offsets, q1, near, near_other, acc, top)
    got = partner(send, "seq", 1)
    cur, y_in = lax.optimization_barrier((cur, y_in))
    y_core = partner(y_in, "head", 1)

    patches = call(
        functools.partial(patch_kernel, branches),
        "patch",
        [((patch_rows, LANES), BF16)] * 4,
        [smem] + [whole] * 9,
        [pltpu.VMEM((branches + 1, n2, LANES), F32)],
        aliases={6: 0, 7: 1, 8: 2, 9: 3},
    )(offsets, cur, cur_top, part, part_top, got, *patches)
    fixes = [patches[0]] + [partner(patches[s], "head", s) for s in range(1, 4)]

    out_shape = (width, out_weight.shape[1])
    spread_shapes = [((4, width, LANES), F32), ((2, width, LANES), F32)]
    pairs, lasts = call(arrange_kernel, "arrange", spread_shapes, [whole] * 4)(
        m_own, core_in, y_in, y_core
    )
    out, _, _ = call(
        functools.partial(project_kernel, dils),
        "project",
        [(out_shape, BF16)] + spread_shapes,
        [smem] + [whole] * 7,
        [pltpu.VMEM(out_shape, BF16), pltpu.SemaphoreType.DMA((4,))],
        aliases={1: 1, 2: 2},
        spaces=(pltpu.HBM, pltpu.VMEM, pltpu.VMEM),
    )(offsets, pairs, lasts, *fixes, out_weight)
    return out


def solution(mesh):
    in_specs = (P("head", "seq"), P("head", "seq"), P("head", "seq"), P(), P())
    out_specs = P(("seq", "head"), None)
    return jax.shard_map(local, mesh=mesh, in_specs=in_specs, out_specs=out_specs, check_vma=False)
```

```python
import functools
import math

import jax
import jax.numpy as jnp
from jax import lax
from jax.experimental import pallas as pl
from jax.experimental.pallas import tpu as pltpu
from jax.sharding import PartitionSpec as P

DH = 64
KEYS = 1024
LANES = 128
QBLK = 256
EXP2_SCALE = DH ** (-0.5) * math.log2(math.e)
NT = (((1,), (1,)), ((), ()))
NN = (((1,), (0,)), ((), ()))
STATS = 16
VMEM_BYTES = 24 << 20
COVER = dict(select=6, query=4, local=25, far=1, pair=3, patch=5, arrange=4, project=6)
BF16, F32 = jnp.bfloat16, jnp.float32


def dot(a, b, dims):
    return lax.dot_general(a, b, dims, preferred_element_type=F32)


def lane_of(shape):
    return lax.broadcasted_iota(jnp.int32, shape, len(shape) - 1)


def in_values(shape, head):
    return (lane_of(shape) < DH) == (head % 2 == 0)


def stack_halves(values, others, head):
    return jnp.concatenate([values, others] if head % 2 == 0 else [others, values], 0)


def swap(rows):
    return pltpu.roll(rows, DH, 1)


def softmax_block(scores):
    row_max = jnp.max(scores, axis=1, keepdims=True)
    weights = jnp.exp2((scores - row_max) * EXP2_SCALE).astype(BF16)
    return row_max, weights


def attend(items):
    scores = items[0][0]()
    for i, (_, values, sink) in enumerate(items):
        ahead = items[i + 1][0]() if i + 1 < len(items) else None
        row_max, weights = softmax_block(scores)
        sink(row_max, values(weights))
        scores = ahead


def merge_rows(cur, cur_max, new, new_max):
    both = jnp.maximum(cur_max, new_max)
    keep_cur = jnp.exp2((cur_max - both) * EXP2_SCALE)
    keep_new = jnp.exp2((new_max - both) * EXP2_SCALE)
    return both, cur * keep_cur + new * keep_new


def pack_pair(even, odd):
    low = lane_of(even.shape) < DH
    return jnp.where(low, even, odd) / swap(jnp.where(low, odd, even))


def pack_even(first, second):
    low = lane_of(first.shape) < DH
    return jnp.where(low, first, swap(second)) / jnp.where(low, swap(first), second)


def select_kernel(dils, off_hbm, q_hbm, k_hbm, v_hbm, q_ref, k_ref, v_ref, near_ref, far_ref, kvt, off_ref, sems, off_sem):
    heads = q_ref.shape[0] // DH
    tok = q_ref.shape[1]
    off_copy = pltpu.make_async_copy(off_hbm, off_ref, off_sem)
    off_copy.start()
    copies = []
    for h in range(heads):
        rows = pl.ds(h * DH, DH)
        for i, (src, dst) in enumerate(((k_hbm, k_ref), (v_hbm, v_ref))):
            copies.append(pltpu.make_async_copy(src.at[rows, :], dst.at[rows, :], sems.at[h, i]))
            copies[-1].start()
    q_copy = pltpu.make_async_copy(q_hbm, q_ref, sems.at[0, 2])
    q_copy.start()
    off_copy.wait()
    for h in range(heads):
        rows = slice(h * DH, (h + 1) * DH)
        head = lax.axis_index("head") * heads + h
        copies[2 * h].wait()
        copies[2 * h + 1].wait()
        kvt[h] = stack_halves(v_ref[rows, :], k_ref[rows, :], h).T.astype(F32)
        near_ref[h] = kvt[h, pl.ds(off_ref[0, head], tok // dils[0], stride=dils[0]), :].astype(BF16)
        for b in range(1, len(dils)):
            pick = pl.ds(off_ref[b, head], tok // dils[b], stride=dils[b])
            far_ref[b - 1, h] = kvt[h, pick, :].astype(BF16)
    q_copy.wait()


def query_kernel(dils, off_hbm, q_ref, q1_ref, q23_ref, qt, off_ref, off_sem):
    heads = q_ref.shape[0] // DH
    tok = q_ref.shape[1]
    copy = pltpu.make_async_copy(off_hbm, off_ref, off_sem)
    copy.start()
    for h in range(heads):
        head = lax.axis_index("head") * heads + h
        query = q_ref[h * DH : (h + 1) * DH, :]
        qt[h] = stack_halves(jnp.zeros_like(query), query, h).T.astype(F32)
        if h == 0:
            copy.wait()
        picks = [pl.ds(off_ref[b, head], tok // d, stride=d) for b, d in enumerate(dils)]
        q1_ref[h] = qt[h, picks[0], :].astype(BF16)
        far_q = qt[h, picks[1], :]
        if len(dils) == 3:
            far_q = far_q + swap(qt[h, picks[2], :])
        q23_ref[h] = far_q.astype(BF16)


def local_kernel(q_ref, k_ref, v_ref, acc_ref, max_ref, own_ref, core_ref, far_ref, qts):
    heads = q_ref.shape[0] // DH
    tok = q_ref.shape[1]
    width = tok // 4
    half = width // 2
    size = own_ref.shape[0]
    me = lax.axis_index("head")
    mains = (own_ref, core_ref, far_ref.at[:size, :], far_ref.at[size:, :])
    items = []

    def block(h, seg, keys, vals, s, part):
        start = pl.multiple_of((me ^ s) * width + part * half, half)
        at = pl.ds(start, half)

        def sink(row_max, out):
            acc_ref[h, at, :] = out
            max_ref[h, at, :] = jnp.broadcast_to(row_max, out.shape)
            if h == 1:
                mains[s][part * half : (part + 1) * half, :] = pack_pair(acc_ref[0, at, :], out).astype(BF16)
            elif h == 2 and part == 1:
                first = acc_ref[2, pl.ds(start - half, half), :]
                mains[s][width:, :] = pack_even(first, out).astype(BF16)

        items.append((lambda: dot(qts[h, at, :], keys, NN), lambda weights: dot(weights, vals, NT), sink))

    for h in range(heads):
        rows = slice(h * DH, (h + 1) * DH)
        qts[h] = q_ref[rows, :].T
        for pair in range(2):
            cols = pl.ds(pl.multiple_of(((me // 2) ^ pair) * KEYS, KEYS), KEYS)
            keys = k_ref[rows, cols]
            vals = v_ref[rows, cols]
            vals = stack_halves(vals, jnp.ones_like(vals), h)
            for s in (2 * pair, 2 * pair + 1):
                for part in range(2):
                    block(h, pair, keys, vals, s, part)
    attend(items)


def pair_kernel(dils, off_ref, q_ref, own_ref, other_ref, acc_in, max_in, p0, p1, p2, p3, cur_ref, top_ref, acc, top):
    heads, n1, _ = q_ref.shape
    tok = acc.shape[1]
    me = lax.axis_index("head")
    patches = (p0, p1, p2, p3)
    size = n1 // len(patches)
    half = size // 2
    items = []
    held = {}
    odd = me % 2 == 1

    def block(h, kv, vals, blk):
        first = pl.multiple_of(((me // 2) ^ blk) * QBLK, QBLK)
        rows = pl.ds(off_ref[0, me * heads + h] + first * dils[0], QBLK, stride=dils[0])

        def sink(row_max, out):
            both, new = merge_rows(acc[h, rows, :], top[h, rows, :], out, row_max)
            acc[h, rows, :] = new
            top[h, rows, :] = both
            if h == 0:
                held[blk] = new
                return
            if h == 1:
                done = pack_pair(held[blk], new)
                ends = [done[:size], done[size:]]
                at = slice(0, size)
            else:
                ends = [pack_even(new[i : i + half], new[i + half : i + size]) for i in (0, size)]
                at = slice(size, size + half)
            patches[2 * blk][at, :] = jnp.where(odd, ends[1], ends[0]).astype(BF16)
            patches[2 * blk + 1][at, :] = jnp.where(odd, ends[0], ends[1]).astype(BF16)

        query = q_ref[h, pl.ds(first, QBLK), :]
        items.append((lambda: dot(query, kv, NT), lambda weights: dot(weights, vals, NN), sink))

    for h in range(heads):
        kv = jnp.concatenate([own_ref[h], other_ref[h]], 0)
        vals = jnp.where(in_values(kv.shape, h), kv, jnp.ones_like(kv))
        for blk in range(n1 // QBLK):
            block(h, kv, vals, blk)
    attend(items)
    for h in range(heads):
        for b in range(1, len(dils)):
            pick = pl.ds(off_ref[b, me * heads + h], tok // dils[b], stride=dils[b])
            cur_ref[b - 1, h] = acc[h, pick, :]
            top_ref[b - 1, h] = top[h, pick, :]


def far_kernel(branches, q_own, q_other, kv0, kv1, kv2, kv3, part_ref, top_ref, send_ref):
    heads, n, _ = q_own.shape
    a_lanes = [in_values((n, LANES), h) for h in range(2)]
    items = []
    held = {}

    def block(h, b, query, kv, vals):
        def sink(row_max, out):
            part_ref[b, h] = out[:n]
            top_ref[b, h] = jnp.broadcast_to(row_max[:n], (n, LANES))
            held[b] = out[n:], row_max[n:]
            if b == branches - 1:
                pack(h)

        items.append((lambda: dot(query, kv, NT), lambda weights: dot(weights, vals, NN), sink))

    def pack(h):
        first, first_top = held[0]
        other, other_top = held[branches - 1]
        if branches == 2:
            other = swap(other)
        mine = a_lanes[h % 2]
        send_ref[h, :n, :] = jnp.where(mine, first, other).astype(BF16)
        slot = lane_of((n, LANES)) % DH
        stats = jnp.where(slot >= 3, jnp.where(mine, other, first), jnp.where(mine, other_top, first_top))
        high = stats.astype(BF16).astype(F32)
        mid = (stats - high).astype(BF16).astype(F32)
        low = stats - high - mid
        coded = jnp.where(slot % 3 == 0, high, jnp.where(slot % 3 == 1, mid, low))
        coded = coded.T
        send_ref[h, n : n + STATS, :] = coded[:STATS].astype(BF16)
        send_ref[h, n + STATS :, :] = coded[DH : DH + STATS].astype(BF16)

    for h in range(heads):
        q_all = jnp.concatenate([q_own[h], q_other[h]], 0)
        for b in range(branches):
            kv = jnp.concatenate([r[b, h] for r in (kv0, kv1, kv2, kv3)], 0)
            query = q_all if b == 0 else swap(q_all.astype(F32)).astype(BF16)
            query = jnp.where(in_values(query.shape, h), jnp.zeros_like(query), query)
            block(h, b, query, kv, jnp.where(in_values(kv.shape, h), kv, jnp.ones_like(kv)))
    attend(items)


def patch_kernel(branches, off_ref, cur_ref, cur_top, part_ref, part_top, got_ref, p0, p1, p2, p3, packed):
    heads, n = cur_ref.shape[1:3]
    me = lax.axis_index("head")
    patches = (p0, p1, p2, p3)
    size = n // len(patches)
    spread = []
    for parity in range(2):
        first = lax.broadcasted_iota(jnp.int32, (2 * STATS, 4 * LANES), 0)
        kind = lax.broadcasted_iota(jnp.int32, (2 * STATS, 4 * LANES), 1) // LANES
        base = jnp.where((kind // 2 == 0) == (parity == 0), STATS, 0) + 3 * (kind % 2)
        spread.append(jnp.where((first >= base) & (first < base + 3), 1.0, 0.0).astype(BF16))
    done = []
    for h in range(heads):
        a_lanes = in_values((n, LANES), h)
        got = got_ref[h, :n, :].astype(F32)
        stats = dot(got_ref[h, n:, :], spread[h % 2], (((0,), (0,)), ((), ())))
        states = []
        for b in range(branches):
            got_max = stats[:, 2 * b * LANES : (2 * b + 1) * LANES]
            got_sum = stats[:, (2 * b + 1) * LANES : (2 * b + 2) * LANES]
            new = jnp.where(a_lanes, got if b == 0 else swap(got), got_sum)
            states.append(merge_rows(part_ref[b, h], part_top[b, h], new, got_max))
        head = me * heads + h
        first_max, first = merge_rows(cur_ref[0, h], cur_top[0, h], states[0][1], states[0][0])
        merged = [first]
        if branches == 2:
            same = off_ref[1, head] == off_ref[2, head]
            base = jnp.where(same, first, cur_ref[1, h])
            base_max = jnp.where(same, first_max, cur_top[1, h])
            _, second = merge_rows(base, base_max, states[1][1], states[1][0])
            merged = [jnp.where(same, second, first), second]
        done.append(merged)
    for b in range(branches):
        packed[b] = pack_pair(done[0][b], done[1][b])
    packed[branches] = pack_even(done[2][0], done[2][-1])
    for s, out in enumerate(patches):
        start = pl.multiple_of((me ^ s) * size, size)
        for i in range(branches + 1):
            out[i * size : (i + 1) * size, :] = packed[i, pl.ds(start, size), :].astype(BF16)


def put_rows(off_ref, dil, branch, head, first, ref, index, new, in_low):
    at = pl.ds(off_ref[branch, head] + first * dil, new.shape[0], stride=dil)
    ref[index, at, :] = jnp.where((lane_of(new.shape) < DH) == in_low, new, ref[index, at, :])


def arrange_kernel(dils, off_ref, x0, x1, x2, x3, p0, p1, p2, p3, pairs, lasts):
    me = lax.axis_index("head")
    count = x0.shape[0]
    width = pairs.shape[1]
    half = width // 2
    near = width // dils[0]
    xs, ps = (x0, x1, x2.at[:count, :], x3.at[count:, :]), (p0, p1, p2, p3)
    for s in range(4):
        pairs[s] = xs[s][:width, :].astype(F32)
    for t in range(2):
        a = xs[2 * t][width:, :].astype(F32)
        b = xs[2 * t + 1][width:, :].astype(F32)
        lane = lane_of(a.shape)
        lasts[t, :half, :] = jnp.where(lane < DH, a, swap(b))
        lasts[t, half:, :] = jnp.where(lane < DH, swap(a), b)
    for s in range(4):
        in_low = s % 2 == 0
        put = functools.partial(put_rows, off_ref, dils[0], 0)
        head = (me ^ s) * 3
        new = ps[s][:near, :].astype(F32)
        for h in range(2):
            put(head + h, 0, pairs, s, new, h == 0)
        new = ps[s][near:, :].astype(F32)
        turned = swap(new)
        put(head + 2, 0, lasts, s // 2, new if in_low else turned, in_low)
        put(head + 2, near // 2, lasts, s // 2, turned if in_low else new, in_low)


def project_kernel(dils, off_ref, pairs_in, lasts_in, p0, p1, p2, p3, w_ref, out_hbm, pairs, lasts, out_ref, sem):
    me = lax.axis_index("head")
    width = out_ref.shape[0]
    branches = len(dils) - 1
    size = width // dils[1]
    rows = 3 * DH
    sources = [me ^ s for s in range(4)]
    ps = (p0, p1, p2, p3)
    for s in range(4):
        in_low = s % 2 == 0
        head = sources[s] * 3
        for b in range(branches):
            put = functools.partial(put_rows, off_ref, dils[b + 1], b + 1)
            new = ps[s][b * size : (b + 1) * size, :].astype(F32)
            for h in range(2):
                put(head + h, 0, pairs, s, new, h == 0)
            new = ps[s][branches * size :, :].astype(F32)
            if b != s % 2:
                new = swap(new)
            put(head + 2, 0, lasts, s // 2, new, in_low)

    def w_rows(s, start, count):
        return w_ref[pl.ds(pl.multiple_of(sources[s] * rows + start, DH), count), :]

    ws = [jnp.concatenate([w_rows(2 * t, 0, LANES), w_rows(2 * t + 1, 0, LANES)], 0) for t in range(2)]
    ws.append(jnp.concatenate([w_rows(s, LANES, DH) for s in range(4)], 0))
    total = None
    for t in range(3):
        halves = (pairs[2 * t], pairs[2 * t + 1]) if t < 2 else (lasts[0], lasts[1])
        part = dot(jnp.concatenate(halves, 1).astype(BF16), ws[t], NN)
        total = part if total is None else total + part
    out_ref[...] = total.astype(BF16)
    copy = pltpu.make_async_copy(out_ref, out_hbm, sem)
    copy.start()
    copy.wait()


def partner(block, axis, apart):
    count = lax.axis_size(axis)
    return lax.ppermute(block, axis, [(i, i ^ apart) for i in range(count)])


def call(kernel, name, outs, in_specs, scratch=(), aliases={}, spaces=None):
    estimate = pl.CostEstimate(flops=int(COVER[name] * 1e9), bytes_accessed=1024, transcendentals=0)
    return pl.pallas_call(
        kernel,
        out_shape=tuple(jax.ShapeDtypeStruct(*o) for o in outs),
        in_specs=in_specs,
        out_specs=tuple(pl.BlockSpec(memory_space=m) for m in spaces or (pltpu.VMEM,) * len(outs)),
        input_output_aliases=aliases,
        scratch_shapes=scratch,
        compiler_params=pltpu.CompilerParams(vmem_limit_bytes=VMEM_BYTES),
        cost_estimate=estimate,
        name=name,
    )


def spread_far(acc, top, query_h, key_h, value_h, dil, head_offsets):
    hit = jnp.arange(dil)[None, :] == head_offsets[:, None]

    def pick(x):
        shaped = x.reshape(x.shape[:2] + (x.shape[2] // dil, dil))
        return jnp.sum(shaped * hit[:, None, None, :].astype(x.dtype), axis=-1, dtype=x.dtype)

    pair = lax.all_gather(jnp.stack([pick(key_h), pick(value_h)], 0), "seq", axis=3, tiled=True)
    scores = jnp.einsum("hdq,hdk->hqk", pick(query_h), pair[0], preferred_element_type=F32)
    new_max = jnp.max(scores, axis=2, keepdims=True)
    e = jnp.exp2((scores - new_max) * EXP2_SCALE)
    new_sum = jnp.sum(e, axis=2, keepdims=True)
    new_acc = jnp.einsum("hqk,hdk->hqd", e.astype(BF16), pair[1], preferred_element_type=F32)
    heads, tok, _ = acc.shape
    shaped = acc.reshape(heads, tok // dil, dil, LANES)
    cur = jnp.sum(jnp.where(hit[:, None, :, None], shaped, 0.0), axis=2)
    sums = jnp.broadcast_to(new_sum, new_acc.shape)
    cur_top = jnp.sum(jnp.where(hit[:, None, :, None], top.reshape(shaped.shape), 0.0), axis=2)
    rows = []
    for h in range(heads):
        halves = [new_acc[h], sums[h]] if h % 2 == 0 else [sums[h], new_acc[h]]
        rows.append(merge_rows(cur[h], cur_top[h], jnp.concatenate(halves, 1), new_max[h]))

    def put(update, old):
        return jnp.where(hit[:, None, :, None], update[:, :, None, :], old).reshape(acc.shape)

    out_top, out = (jnp.stack(r, 0) for r in zip(*rows))
    return put(out, shaped), put(out_top, top.reshape(shaped.shape))


def packed_mains(acc):
    heads, tok, _ = acc.shape
    width = tok // 4
    me = lax.axis_index("head")
    rows = []
    for h in range(heads):
        low, high = acc[h, :, :DH], acc[h, :, DH:]
        rows.append(low / high if h % 2 == 0 else high / low)
    blocks = []
    for s in range(4):
        mine = [lax.dynamic_slice_in_dim(r, (me ^ s) * width, width, 0) for r in rows]
        last = jnp.concatenate([mine[2][: width // 2], mine[2][width // 2 :]], 1)
        blocks.append(jnp.concatenate([jnp.concatenate(mine[:2], 1), last], 0).astype(BF16))
    return blocks[0], blocks[1], jnp.concatenate(blocks[2:], 0)


def local(queries, key_vectors, value_vectors, offsets, out_weight):
    tok = queries.shape[1]
    heads = queries.shape[0] // DH
    seq_count = lax.axis_size("seq")
    far_rate = tok * seq_count // KEYS
    dils = (4, 16, 16) if far_rate == 16 else (4, 16)
    branches = len(dils) - 1
    n1, n2 = tok // 4, tok // 16
    width = tok // 4
    whole = pl.BlockSpec(memory_space=pltpu.VMEM)
    smem = pl.BlockSpec(memory_space=pltpu.SMEM)
    hbm = pl.BlockSpec(memory_space=pltpu.HBM)
    far_shape = ((branches, heads, n2, LANES), F32)
    acc_shape = ((heads, tok, LANES), F32)

    stay = [
        pltpu.with_memory_space_constraint(a, pltpu.HBM) for a in (offsets, queries, key_vectors, value_vectors)
    ]
    q, k, v, near, far = call(
        functools.partial(select_kernel, dils),
        "select",
        [(queries.shape, BF16)] * 3 + [((heads, n1, LANES), BF16), ((branches, heads, n2, LANES), BF16)],
        [hbm] * 4,
        [
            pltpu.VMEM((heads, tok, LANES), F32),
            pltpu.SMEM(offsets.shape, jnp.int32),
            pltpu.SemaphoreType.DMA((heads, 3)),
            pltpu.SemaphoreType.DMA,
        ],
    )(*stay)
    fars = [far] + [partner(far, "seq", apart) for apart in (2, 4, 6)]

    q1, q23 = call(
        functools.partial(query_kernel, dils),
        "query",
        [((heads, n1, LANES), BF16), ((heads, n2, LANES), BF16)],
        [hbm, whole],
        [
            pltpu.VMEM((heads, tok, LANES), F32),
            pltpu.SMEM(offsets.shape, jnp.int32),
            pltpu.SemaphoreType.DMA,
        ],
    )(stay[0], q)
    q23_other = partner(q23, "seq", 1)
    near_other = partner(near, "seq", 1)

    q, q23 = lax.optimization_barrier((q, q23))
    main = heads * width // 2
    acc, top, m_own, m_core, m_far = call(
        local_kernel,
        "local",
        [acc_shape] * 2 + [((main, LANES), BF16)] * 2 + [((2 * main, LANES), BF16)],
        [whole] * 3,
        [pltpu.VMEM((heads, tok, DH), BF16)],
    )(q, k, v)

    if branches == 1:
        shape = (heads, DH, tok)
        my_offsets = lax.dynamic_slice_in_dim(offsets[2], lax.axis_index("head") * heads, heads, 0)
        parts = [a.reshape(shape) for a in (queries, key_vectors, value_vectors)]
        acc, top = spread_far(acc, top, *parts, far_rate, my_offsets)
        m_own, m_core, m_far = packed_mains(acc)

    m_far, q23_other = lax.optimization_barrier((m_far, q23_other))
    y_in = partner(m_far, "head", 2)
    core_in = partner(m_core, "head", 1)

    acc, near_other = lax.optimization_barrier((acc, near_other))
    *early, cur, cur_top, _, _ = call(
        functools.partial(pair_kernel, dils),
        "pair",
        [((n1 * 3 // 8, LANES), BF16)] * 4 + [far_shape] * 2 + [acc_shape] * 2,
        [smem] + [whole] * 5,
        aliases={4: 6, 5: 7},
    )(offsets, q1, near, near_other, acc, top)
    early = [early[0]] + [partner(early[s], "head", s) for s in range(1, 4)]

    fars, cur = lax.optimization_barrier((fars, cur))
    part, part_top, send = call(
        functools.partial(far_kernel, branches),
        "far",
        [far_shape] * 2 + [((heads, n2 + 2 * STATS, LANES), BF16)],
        [whole] * 6,
    )(q23, q23_other, *fars)
    got = partner(send, "seq", 1)
    y_in, part = lax.optimization_barrier((y_in, part))
    y_core = partner(y_in, "head", 1)

    patches = call(
        functools.partial(patch_kernel, branches),
        "patch",
        [(((branches + 1) * n2 // 4, LANES), BF16)] * 4,
        [smem] + [whole] * 5,
        [pltpu.VMEM((branches + 1, n2, LANES), F32)],
    )(offsets, cur, cur_top, part, part_top, got)
    fixes = [patches[0]] + [partner(patches[s], "head", s) for s in range(1, 4)]

    out_shape = (width, out_weight.shape[1])
    spread_shapes = [((4, width, LANES), F32), ((2, width, LANES), F32)]
    pairs, lasts = call(
        functools.partial(arrange_kernel, dils), "arrange", spread_shapes, [smem] + [whole] * 8
    )(offsets, m_own, core_in, y_in, y_core, *early)
    out, _, _ = call(
        functools.partial(project_kernel, dils),
        "project",
        [(out_shape, BF16)] + spread_shapes,
        [smem] + [whole] * 7,
        [pltpu.VMEM(out_shape, BF16), pltpu.SemaphoreType.DMA],
        aliases={1: 1, 2: 2},
        spaces=(pltpu.HBM, pltpu.VMEM, pltpu.VMEM),
    )(offsets, pairs, lasts, *fixes, out_weight)
    return out


def solution(mesh):
    in_specs = (P("head", "seq"), P("head", "seq"), P("head", "seq"), P(), P())
    out_specs = P(("seq", "head"), None)
    return jax.shard_map(local, mesh=mesh, in_specs=in_specs, out_specs=out_specs, check_vma=False)
```

```python
import functools
import math

import jax
import jax.numpy as jnp
from jax import lax
from jax.experimental import pallas as pl
from jax.experimental.pallas import tpu as pltpu
from jax.sharding import PartitionSpec as P

DH = 64
KEYS = 1024
LANES = 128
QBLK = 256
EXP2_SCALE = DH ** (-0.5) * math.log2(math.e)
NT = (((1,), (1,)), ((), ()))
NN = (((1,), (0,)), ((), ()))
STATS = 16
VMEM_BYTES = 24 << 20
COVER = dict(select=6, query=4, local=25, far=1, pair=3, patch=5, arrange=4, project=6)
BF16, F32 = jnp.bfloat16, jnp.float32


def dot(a, b, dims):
    return lax.dot_general(a, b, dims, preferred_element_type=F32)


def lane_of(shape):
    return lax.broadcasted_iota(jnp.int32, shape, len(shape) - 1)


def in_values(shape, head):
    return (lane_of(shape) < DH) == (head % 2 == 0)


def stack_halves(values, others, head):
    return jnp.concatenate([values, others] if head % 2 == 0 else [others, values], 0)


def swap(rows):
    return pltpu.roll(rows, DH, 1)


def softmax_block(scores):
    row_max = jnp.max(scores, axis=1, keepdims=True)
    weights = jnp.exp2((scores - row_max) * EXP2_SCALE).astype(BF16)
    return row_max, weights


def attend(items):
    scores = items[0][0]()
    for i, (_, values, sink) in enumerate(items):
        ahead = items[i + 1][0]() if i + 1 < len(items) else None
        row_max, weights = softmax_block(scores)
        sink(row_max, values(weights))
        scores = ahead


def merge_rows(cur, cur_max, new, new_max):
    both = jnp.maximum(cur_max, new_max)
    keep_cur = jnp.exp2((cur_max - both) * EXP2_SCALE)
    keep_new = jnp.exp2((new_max - both) * EXP2_SCALE)
    return both, cur * keep_cur + new * keep_new


def pack_pair(even, odd):
    low = lane_of(even.shape) < DH
    return jnp.where(low, even, odd) / swap(jnp.where(low, odd, even))


def pack_even(first, second):
    low = lane_of(first.shape) < DH
    return jnp.where(low, first, swap(second)) / jnp.where(low, swap(first), second)


def select_kernel(dils, off_hbm, q_hbm, k_hbm, v_hbm, q_ref, k_ref, v_ref, near_ref, far_ref, kvt, off_ref, sems, off_sem):
    heads = q_ref.shape[0] // DH
    tok = q_ref.shape[1]
    off_copy = pltpu.make_async_copy(off_hbm, off_ref, off_sem)
    off_copy.start()
    copies = []
    for h in range(heads):
        rows = pl.ds(h * DH, DH)
        for i, (src, dst) in enumerate(((k_hbm, k_ref), (v_hbm, v_ref))):
            copies.append(pltpu.make_async_copy(src.at[rows, :], dst.at[rows, :], sems.at[h, i]))
            copies[-1].start()
    q_copy = pltpu.make_async_copy(q_hbm, q_ref, sems.at[0, 2])
    q_copy.start()
    off_copy.wait()
    for h in range(heads):
        rows = slice(h * DH, (h + 1) * DH)
        head = lax.axis_index("head") * heads + h
        copies[2 * h].wait()
        copies[2 * h + 1].wait()
        kvt[h] = stack_halves(v_ref[rows, :], k_ref[rows, :], h).T.astype(F32)
        near_ref[h] = kvt[h, pl.ds(off_ref[0, head], tok // dils[0], stride=dils[0]), :].astype(BF16)
        for b in range(1, len(dils)):
            pick = pl.ds(off_ref[b, head], tok // dils[b], stride=dils[b])
            far_ref[b - 1, h] = kvt[h, pick, :].astype(BF16)
    q_copy.wait()


def query_kernel(dils, off_hbm, q_ref, q1_ref, q23_ref, qt, off_ref, off_sem):
    heads = q_ref.shape[0] // DH
    tok = q_ref.shape[1]
    copy = pltpu.make_async_copy(off_hbm, off_ref, off_sem)
    copy.start()
    for h in range(heads):
        head = lax.axis_index("head") * heads + h
        query = q_ref[h * DH : (h + 1) * DH, :]
        qt[h] = stack_halves(jnp.zeros_like(query), query, h).T.astype(F32)
        if h == 0:
            copy.wait()
        picks = [pl.ds(off_ref[b, head], tok // d, stride=d) for b, d in enumerate(dils)]
        q1_ref[h] = qt[h, picks[0], :].astype(BF16)
        far_q = qt[h, picks[1], :]
        if len(dils) == 3:
            far_q = far_q + swap(qt[h, picks[2], :])
        q23_ref[h] = far_q.astype(BF16)


def local_kernel(q_ref, k_ref, v_ref, acc_ref, max_ref, own_ref, core_ref, far_ref, qts):
    heads = q_ref.shape[0] // DH
    tok = q_ref.shape[1]
    width = tok // 4
    half = width // 2
    size = own_ref.shape[0]
    me = lax.axis_index("head")
    mains = (own_ref, core_ref, far_ref.at[:size, :], far_ref.at[size:, :])
    items = []

    def block(h, seg, keys, vals, s, part):
        start = pl.multiple_of((me ^ s) * width + part * half, half)
        at = pl.ds(start, half)

        def sink(row_max, out):
            acc_ref[h, at, :] = out
            max_ref[h, at, :] = jnp.broadcast_to(row_max, out.shape)
            if h == 1:
                mains[s][part * half : (part + 1) * half, :] = pack_pair(acc_ref[0, at, :], out).astype(BF16)
            elif h == 2 and part == 1:
                first = acc_ref[2, pl.ds(start - half, half), :]
                mains[s][width:, :] = pack_even(first, out).astype(BF16)

        items.append((lambda: dot(qts[h, at, :], keys, NN), lambda weights: dot(weights, vals, NT), sink))

    for h in range(heads):
        rows = slice(h * DH, (h + 1) * DH)
        qts[h] = q_ref[rows, :].T
        for pair in range(2):
            cols = pl.ds(pl.multiple_of(((me // 2) ^ pair) * KEYS, KEYS), KEYS)
            keys = k_ref[rows, cols]
            vals = v_ref[rows, cols]
            vals = stack_halves(vals, jnp.ones_like(vals), h)
            for s in (2 * pair, 2 * pair + 1):
                for part in range(2):
                    block(h, pair, keys, vals, s, part)
    attend(items)


def pair_kernel(dils, off_ref, q_ref, own_ref, other_ref, acc_in, max_in, p0, p1, p2, p3, cur_ref, top_ref, acc, top):
    heads, n1, _ = q_ref.shape
    tok = acc.shape[1]
    me = lax.axis_index("head")
    patches = (p0, p1, p2, p3)
    size = n1 // len(patches)
    half = size // 2
    items = []
    held = {}
    odd = me % 2 == 1

    def block(h, kv, vals, blk):
        first = pl.multiple_of(((me // 2) ^ blk) * QBLK, QBLK)
        rows = pl.ds(off_ref[0, me * heads + h] + first * dils[0], QBLK, stride=dils[0])

        def sink(row_max, out):
            both, new = merge_rows(acc[h, rows, :], top[h, rows, :], out, row_max)
            acc[h, rows, :] = new
            top[h, rows, :] = both
            if h == 0:
                held[blk] = new
                return
            if h == 1:
                done = pack_pair(held[blk], new)
                ends = [done[:size], done[size:]]
                at = slice(0, size)
            else:
                ends = [pack_even(new[i : i + half], new[i + half : i + size]) for i in (0, size)]
                at = slice(size, size + half)
            patches[2 * blk][at, :] = jnp.where(odd, ends[1], ends[0]).astype(BF16)
            patches[2 * blk + 1][at, :] = jnp.where(odd, ends[0], ends[1]).astype(BF16)

        query = q_ref[h, pl.ds(first, QBLK), :]
        items.append((lambda: dot(query, kv, NT), lambda weights: dot(weights, vals, NN), sink))

    for h in range(heads):
        kv = jnp.concatenate([own_ref[h], other_ref[h]], 0)
        vals = jnp.where(in_values(kv.shape, h), kv, jnp.ones_like(kv))
        for blk in range(n1 // QBLK):
            block(h, kv, vals, blk)
    attend(items)
    for h in range(heads):
        for b in range(1, len(dils)):
            pick = pl.ds(off_ref[b, me * heads + h], tok // dils[b], stride=dils[b])
            cur_ref[b - 1, h] = acc[h, pick, :]
            top_ref[b - 1, h] = top[h, pick, :]


def far_kernel(branches, q_own, q_other, kv0, kv1, kv2, kv3, part_ref, top_ref, send_ref):
    heads, n, _ = q_own.shape
    a_lanes = [in_values((n, LANES), h) for h in range(2)]
    items = []
    held = {}

    def block(h, b, query, kv, vals):
        def sink(row_max, out):
            part_ref[b, h] = out[:n]
            top_ref[b, h] = jnp.broadcast_to(row_max[:n], (n, LANES))
            held[b] = out[n:], row_max[n:]
            if b == branches - 1:
                pack(h)

        items.append((lambda: dot(query, kv, NT), lambda weights: dot(weights, vals, NN), sink))

    def pack(h):
        first, first_top = held[0]
        other, other_top = held[branches - 1]
        if branches == 2:
            other = swap(other)
        mine = a_lanes[h % 2]
        send_ref[h, :n, :] = jnp.where(mine, first, other).astype(BF16)
        slot = lane_of((n, LANES)) % DH
        stats = jnp.where(slot >= 3, jnp.where(mine, other, first), jnp.where(mine, other_top, first_top))
        high = stats.astype(BF16).astype(F32)
        mid = (stats - high).astype(BF16).astype(F32)
        low = stats - high - mid
        coded = jnp.where(slot % 3 == 0, high, jnp.where(slot % 3 == 1, mid, low))
        coded = coded.T
        send_ref[h, n : n + STATS, :] = coded[:STATS].astype(BF16)
        send_ref[h, n + STATS :, :] = coded[DH : DH + STATS].astype(BF16)

    for h in range(heads):
        q_all = jnp.concatenate([q_own[h], q_other[h]], 0)
        for b in range(branches):
            kv = jnp.concatenate([r[b, h] for r in (kv0, kv1, kv2, kv3)], 0)
            query = q_all if b == 0 else swap(q_all.astype(F32)).astype(BF16)
            query = jnp.where(in_values(query.shape, h), jnp.zeros_like(query), query)
            block(h, b, query, kv, jnp.where(in_values(kv.shape, h), kv, jnp.ones_like(kv)))
    attend(items)


def patch_kernel(branches, off_ref, cur_ref, cur_top, part_ref, part_top, got_ref, p0, p1, p2, p3, packed):
    heads, n = cur_ref.shape[1:3]
    me = lax.axis_index("head")
    patches = (p0, p1, p2, p3)
    size = n // len(patches)
    spread = []
    for parity in range(2):
        first = lax.broadcasted_iota(jnp.int32, (2 * STATS, 4 * LANES), 0)
        kind = lax.broadcasted_iota(jnp.int32, (2 * STATS, 4 * LANES), 1) // LANES
        base = jnp.where((kind // 2 == 0) == (parity == 0), STATS, 0) + 3 * (kind % 2)
        spread.append(jnp.where((first >= base) & (first < base + 3), 1.0, 0.0).astype(BF16))
    done = []
    for h in range(heads):
        a_lanes = in_values((n, LANES), h)
        got = got_ref[h, :n, :].astype(F32)
        stats = dot(got_ref[h, n:, :], spread[h % 2], (((0,), (0,)), ((), ())))
        states = []
        for b in range(branches):
            got_max = stats[:, 2 * b * LANES : (2 * b + 1) * LANES]
            got_sum = stats[:, (2 * b + 1) * LANES : (2 * b + 2) * LANES]
            new = jnp.where(a_lanes, got if b == 0 else swap(got), got_sum)
            states.append(merge_rows(part_ref[b, h], part_top[b, h], new, got_max))
        head = me * heads + h
        first_max, first = merge_rows(cur_ref[0, h], cur_top[0, h], states[0][1], states[0][0])
        merged = [first]
        if branches == 2:
            same = off_ref[1, head] == off_ref[2, head]
            base = jnp.where(same, first, cur_ref[1, h])
            base_max = jnp.where(same, first_max, cur_top[1, h])
            _, second = merge_rows(base, base_max, states[1][1], states[1][0])
            merged = [jnp.where(same, second, first), second]
        done.append(merged)
    for b in range(branches):
        packed[b] = pack_pair(done[0][b], done[1][b])
    packed[branches] = pack_even(done[2][0], done[2][-1])
    for s, out in enumerate(patches):
        start = pl.multiple_of((me ^ s) * size, size)
        for i in range(branches + 1):
            out[i * size : (i + 1) * size, :] = packed[i, pl.ds(start, size), :].astype(BF16)


def put_rows(off_ref, dil, branch, head, first, ref, index, new, in_low):
    at = pl.ds(off_ref[branch, head] + first * dil, new.shape[0], stride=dil)
    ref[index, at, :] = jnp.where((lane_of(new.shape) < DH) == in_low, new, ref[index, at, :])


def arrange_kernel(dils, off_ref, x0, x1, x2, x3, p0, p1, p2, p3, pairs, lasts):
    me = lax.axis_index("head")
    count = x0.shape[0]
    width = pairs.shape[1]
    half = width // 2
    near = width // dils[0]
    xs, ps = (x0, x1, x2.at[:count, :], x3.at[count:, :]), (p0, p1, p2, p3)
    for s in range(4):
        pairs[s] = xs[s][:width, :].astype(F32)
    for t in range(2):
        a = xs[2 * t][width:, :].astype(F32)
        b = xs[2 * t + 1][width:, :].astype(F32)
        lane = lane_of(a.shape)
        lasts[t, :half, :] = jnp.where(lane < DH, a, swap(b))
        lasts[t, half:, :] = jnp.where(lane < DH, swap(a), b)
    for s in range(4):
        in_low = s % 2 == 0
        put = functools.partial(put_rows, off_ref, dils[0], 0)
        head = (me ^ s) * 3
        new = ps[s][:near, :].astype(F32)
        for h in range(2):
            put(head + h, 0, pairs, s, new, h == 0)
        new = ps[s][near:, :].astype(F32)
        turned = swap(new)
        put(head + 2, 0, lasts, s // 2, new if in_low else turned, in_low)
        put(head + 2, near // 2, lasts, s // 2, turned if in_low else new, in_low)


def project_kernel(dils, off_ref, pairs_in, lasts_in, p0, p1, p2, p3, w_ref, out_hbm, pairs, lasts, out_ref, sem):
    me = lax.axis_index("head")
    width = out_ref.shape[0]
    branches = len(dils) - 1
    size = width // dils[1]
    rows = 3 * DH
    sources = [me ^ s for s in range(4)]
    ps = (p0, p1, p2, p3)
    for s in range(4):
        in_low = s % 2 == 0
        head = sources[s] * 3
        for b in range(branches):
            put = functools.partial(put_rows, off_ref, dils[b + 1], b + 1)
            new = ps[s][b * size : (b + 1) * size, :].astype(F32)
            for h in range(2):
                put(head + h, 0, pairs, s, new, h == 0)
            new = ps[s][branches * size :, :].astype(F32)
            if b != s % 2:
                new = swap(new)
            put(head + 2, 0, lasts, s // 2, new, in_low)

    def w_rows(s, start, count):
        return w_ref[pl.ds(pl.multiple_of(sources[s] * rows + start, DH), count), :]

    ws = [jnp.concatenate([w_rows(2 * t, 0, LANES), w_rows(2 * t + 1, 0, LANES)], 0) for t in range(2)]
    ws.append(jnp.concatenate([w_rows(s, LANES, DH) for s in range(4)], 0))
    total = None
    for t in range(3):
        halves = (pairs[2 * t], pairs[2 * t + 1]) if t < 2 else (lasts[0], lasts[1])
        part = dot(jnp.concatenate(halves, 1).astype(BF16), ws[t], NN)
        total = part if total is None else total + part
    out_ref[...] = total.astype(BF16)
    copy = pltpu.make_async_copy(out_ref, out_hbm, sem)
    copy.start()
    copy.wait()


def partner(block, axis, apart):
    count = lax.axis_size(axis)
    return lax.ppermute(block, axis, [(i, i ^ apart) for i in range(count)])


def call(kernel, name, outs, in_specs, scratch=(), aliases={}, spaces=None):
    estimate = pl.CostEstimate(flops=int(COVER[name] * 1e9), bytes_accessed=1024, transcendentals=0)
    return pl.pallas_call(
        kernel,
        out_shape=tuple(jax.ShapeDtypeStruct(*o) for o in outs),
        in_specs=in_specs,
        out_specs=tuple(pl.BlockSpec(memory_space=m) for m in spaces or (pltpu.VMEM,) * len(outs)),
        input_output_aliases=aliases,
        scratch_shapes=scratch,
        compiler_params=pltpu.CompilerParams(vmem_limit_bytes=VMEM_BYTES),
        cost_estimate=estimate,
        name=name,
    )


def spread_far(acc, top, query_h, key_h, value_h, dil, head_offsets):
    hit = jnp.arange(dil)[None, :] == head_offsets[:, None]

    def pick(x):
        shaped = x.reshape(x.shape[:2] + (x.shape[2] // dil, dil))
        return jnp.sum(shaped * hit[:, None, None, :].astype(x.dtype), axis=-1, dtype=x.dtype)

    pair = lax.all_gather(jnp.stack([pick(key_h), pick(value_h)], 0), "seq", axis=3, tiled=True)
    scores = jnp.einsum("hdq,hdk->hqk", pick(query_h), pair[0], preferred_element_type=F32)
    new_max = jnp.max(scores, axis=2, keepdims=True)
    e = jnp.exp2((scores - new_max) * EXP2_SCALE)
    new_sum = jnp.sum(e, axis=2, keepdims=True)
    new_acc = jnp.einsum("hqk,hdk->hqd", e.astype(BF16), pair[1], preferred_element_type=F32)
    heads, tok, _ = acc.shape
    shaped = acc.reshape(heads, tok // dil, dil, LANES)
    cur = jnp.sum(jnp.where(hit[:, None, :, None], shaped, 0.0), axis=2)
    sums = jnp.broadcast_to(new_sum, new_acc.shape)
    cur_top = jnp.sum(jnp.where(hit[:, None, :, None], top.reshape(shaped.shape), 0.0), axis=2)
    rows = []
    for h in range(heads):
        halves = [new_acc[h], sums[h]] if h % 2 == 0 else [sums[h], new_acc[h]]
        rows.append(merge_rows(cur[h], cur_top[h], jnp.concatenate(halves, 1), new_max[h]))

    def put(update, old):
        return jnp.where(hit[:, None, :, None], update[:, :, None, :], old).reshape(acc.shape)

    out_top, out = (jnp.stack(r, 0) for r in zip(*rows))
    return put(out, shaped), put(out_top, top.reshape(shaped.shape))


def packed_mains(acc):
    heads, tok, _ = acc.shape
    width = tok // 4
    me = lax.axis_index("head")
    rows = []
    for h in range(heads):
        low, high = acc[h, :, :DH], acc[h, :, DH:]
        rows.append(low / high if h % 2 == 0 else high / low)
    blocks = []
    for s in range(4):
        mine = [lax.dynamic_slice_in_dim(r, (me ^ s) * width, width, 0) for r in rows]
        last = jnp.concatenate([mine[2][: width // 2], mine[2][width // 2 :]], 1)
        blocks.append(jnp.concatenate([jnp.concatenate(mine[:2], 1), last], 0).astype(BF16))
    return blocks[0], blocks[1], jnp.concatenate(blocks[2:], 0)


def local(queries, key_vectors, value_vectors, offsets, out_weight):
    tok = queries.shape[1]
    heads = queries.shape[0] // DH
    seq_count = lax.axis_size("seq")
    far_rate = tok * seq_count // KEYS
    dils = (4, 16, 16) if far_rate == 16 else (4, 16)
    branches = len(dils) - 1
    n1, n2 = tok // 4, tok // 16
    width = tok // 4
    whole = pl.BlockSpec(memory_space=pltpu.VMEM)
    smem = pl.BlockSpec(memory_space=pltpu.SMEM)
    hbm = pl.BlockSpec(memory_space=pltpu.HBM)
    far_shape = ((branches, heads, n2, LANES), F32)
    acc_shape = ((heads, tok, LANES), F32)

    stay = [
        pltpu.with_memory_space_constraint(a, pltpu.HBM) for a in (offsets, queries, key_vectors, value_vectors)
    ]
    q, k, v, near, far = call(
        functools.partial(select_kernel, dils),
        "select",
        [(queries.shape, BF16)] * 3 + [((heads, n1, LANES), BF16), ((branches, heads, n2, LANES), BF16)],
        [hbm] * 4,
        [
            pltpu.VMEM((heads, tok, LANES), F32),
            pltpu.SMEM(offsets.shape, jnp.int32),
            pltpu.SemaphoreType.DMA((heads, 3)),
            pltpu.SemaphoreType.DMA,
        ],
    )(*stay)
    fars = [far] + [partner(far, "seq", apart) for apart in (2, 4, 6)]

    q1, q23 = call(
        functools.partial(query_kernel, dils),
        "query",
        [((heads, n1, LANES), BF16), ((heads, n2, LANES), BF16)],
        [hbm, whole],
        [
            pltpu.VMEM((heads, tok, LANES), F32),
            pltpu.SMEM(offsets.shape, jnp.int32),
            pltpu.SemaphoreType.DMA,
        ],
    )(stay[0], q)
    q23_other = partner(q23, "seq", 1)
    near_other = partner(near, "seq", 1)

    q, q23 = lax.optimization_barrier((q, q23))
    main = heads * width // 2
    acc, top, m_own, m_core, m_far = call(
        local_kernel,
        "local",
        [acc_shape] * 2 + [((main, LANES), BF16)] * 2 + [((2 * main, LANES), BF16)],
        [whole] * 3,
        [pltpu.VMEM((heads, tok, DH), BF16)],
    )(q, k, v)

    if branches == 1:
        shape = (heads, DH, tok)
        my_offsets = lax.dynamic_slice_in_dim(offsets[2], lax.axis_index("head") * heads, heads, 0)
        parts = [a.reshape(shape) for a in (queries, key_vectors, value_vectors)]
        acc, top = spread_far(acc, top, *parts, far_rate, my_offsets)
        m_own, m_core, m_far = packed_mains(acc)

    y_in = partner(m_far, "head", 2)
    core_in = partner(m_core, "head", 1)

    acc, near_other = lax.optimization_barrier((acc, near_other))
    *early, cur, cur_top, _, _ = call(
        functools.partial(pair_kernel, dils),
        "pair",
        [((n1 * 3 // 8, LANES), BF16)] * 4 + [far_shape] * 2 + [acc_shape] * 2,
        [smem] + [whole] * 5,
        aliases={4: 6, 5: 7},
    )(offsets, q1, near, near_other, acc, top)
    early = [early[0]] + [partner(early[s], "head", s) for s in range(1, 4)]

    fars, cur = lax.optimization_barrier((fars, cur))
    part, part_top, send = call(
        functools.partial(far_kernel, branches),
        "far",
        [far_shape] * 2 + [((heads, n2 + 2 * STATS, LANES), BF16)],
        [whole] * 6,
    )(q23, q23_other, *fars)
    got = partner(send, "seq", 1)
    y_core = partner(y_in, "head", 1)

    patches = call(
        functools.partial(patch_kernel, branches),
        "patch",
        [(((branches + 1) * n2 // 4, LANES), BF16)] * 4,
        [smem] + [whole] * 5,
        [pltpu.VMEM((branches + 1, n2, LANES), F32)],
    )(offsets, cur, cur_top, part, part_top, got)
    fixes = [patches[0]] + [partner(patches[s], "head", s) for s in range(1, 4)]

    out_shape = (width, out_weight.shape[1])
    spread_shapes = [((4, width, LANES), F32), ((2, width, LANES), F32)]
    pairs, lasts = call(
        functools.partial(arrange_kernel, dils), "arrange", spread_shapes, [smem] + [whole] * 8
    )(offsets, m_own, core_in, y_in, y_core, *early)
    out, _, _ = call(
        functools.partial(project_kernel, dils),
        "project",
        [(out_shape, BF16)] + spread_shapes,
        [smem] + [whole] * 7,
        [pltpu.VMEM(out_shape, BF16), pltpu.SemaphoreType.DMA],
        aliases={1: 1, 2: 2},
        spaces=(pltpu.HBM, pltpu.VMEM, pltpu.VMEM),
    )(offsets, pairs, lasts, *fixes, out_weight)
    return out


def solution(mesh):
    in_specs = (P("head", "seq"), P("head", "seq"), P("head", "seq"), P(), P())
    out_specs = P(("seq", "head"), None)
    return jax.shard_map(local, mesh=mesh, in_specs=in_specs, out_specs=out_specs, check_vma=False)
```

```python
import functools
import math

import jax
import jax.numpy as jnp
from jax import lax
from jax.experimental import pallas as pl
from jax.experimental.pallas import tpu as pltpu
from jax.sharding import PartitionSpec as P

DH = 64
KEYS = 1024
LANES = 128
QBLK = 256
EXP2_SCALE = DH ** (-0.5) * math.log2(math.e)
NT = (((1,), (1,)), ((), ()))
NN = (((1,), (0,)), ((), ()))
STATS = 16
VMEM_BYTES = 24 << 20
COVER = dict(select=6, query=4, local=25, far=1, pair=3, patch=5, arrange=4, project=6)
BF16, F32 = jnp.bfloat16, jnp.float32


def dot(a, b, dims):
    return lax.dot_general(a, b, dims, preferred_element_type=F32)


def lane_of(shape):
    return lax.broadcasted_iota(jnp.int32, shape, len(shape) - 1)


def in_values(shape, head):
    return (lane_of(shape) < DH) == (head % 2 == 0)


def stack_halves(values, others, head):
    return jnp.concatenate([values, others] if head % 2 == 0 else [others, values], 0)


def swap(rows):
    return pltpu.roll(rows, DH, 1)


def softmax_block(scores):
    row_max = jnp.max(scores, axis=1, keepdims=True)
    weights = jnp.exp2((scores - row_max) * EXP2_SCALE).astype(BF16)
    return row_max, weights


def attend(items):
    scores = items[0][0]()
    for i, (_, values, sink) in enumerate(items):
        ahead = items[i + 1][0]() if i + 1 < len(items) else None
        row_max, weights = softmax_block(scores)
        sink(row_max, values(weights))
        scores = ahead


def merge_rows(cur, cur_max, new, new_max):
    both = jnp.maximum(cur_max, new_max)
    keep_cur = jnp.exp2((cur_max - both) * EXP2_SCALE)
    keep_new = jnp.exp2((new_max - both) * EXP2_SCALE)
    return both, cur * keep_cur + new * keep_new


def pack_pair(even, odd):
    low = lane_of(even.shape) < DH
    return jnp.where(low, even, odd) / swap(jnp.where(low, odd, even))


def pack_even(first, second):
    low = lane_of(first.shape) < DH
    return jnp.where(low, first, swap(second)) / jnp.where(low, swap(first), second)


def select_kernel(dils, off_hbm, q_hbm, k_hbm, v_hbm, q_ref, k_ref, v_ref, near_ref, far_ref, kvt, off_ref, sems, off_sem):
    heads = q_ref.shape[0] // DH
    tok = q_ref.shape[1]
    off_copy = pltpu.make_async_copy(off_hbm, off_ref, off_sem)
    off_copy.start()
    copies = []
    for h in range(heads):
        rows = pl.ds(h * DH, DH)
        for i, (src, dst) in enumerate(((k_hbm, k_ref), (v_hbm, v_ref))):
            copies.append(pltpu.make_async_copy(src.at[rows, :], dst.at[rows, :], sems.at[h, i]))
            copies[-1].start()
    q_copy = pltpu.make_async_copy(q_hbm, q_ref, sems.at[0, 2])
    q_copy.start()
    off_copy.wait()
    for h in range(heads):
        rows = slice(h * DH, (h + 1) * DH)
        head = lax.axis_index("head") * heads + h
        copies[2 * h].wait()
        copies[2 * h + 1].wait()
        kvt[h] = stack_halves(v_ref[rows, :], k_ref[rows, :], h).T.astype(F32)
        near_ref[h] = kvt[h, pl.ds(off_ref[0, head], tok // dils[0], stride=dils[0]), :].astype(BF16)
        for b in range(1, len(dils)):
            pick = pl.ds(off_ref[b, head], tok // dils[b], stride=dils[b])
            far_ref[b - 1, h] = kvt[h, pick, :].astype(BF16)
    q_copy.wait()


def query_kernel(dils, off_hbm, q_ref, q1_ref, q23_ref, qt, off_ref, off_sem):
    heads = q_ref.shape[0] // DH
    tok = q_ref.shape[1]
    copy = pltpu.make_async_copy(off_hbm, off_ref, off_sem)
    copy.start()
    for h in range(heads):
        head = lax.axis_index("head") * heads + h
        query = q_ref[h * DH : (h + 1) * DH, :]
        qt[h] = stack_halves(jnp.zeros_like(query), query, h).T.astype(F32)
        if h == 0:
            copy.wait()
        picks = [pl.ds(off_ref[b, head], tok // d, stride=d) for b, d in enumerate(dils)]
        q1_ref[h] = qt[h, picks[0], :].astype(BF16)
        far_q = qt[h, picks[1], :]
        if len(dils) == 3:
            far_q = far_q + swap(qt[h, picks[2], :])
        q23_ref[h] = far_q.astype(BF16)


def local_kernel(q_ref, k_ref, v_ref, acc_ref, max_ref, own_ref, core_ref, far_ref, qts):
    heads = q_ref.shape[0] // DH
    tok = q_ref.shape[1]
    width = tok // 4
    half = width // 2
    size = own_ref.shape[0]
    me = lax.axis_index("head")
    mains = (own_ref, core_ref, far_ref.at[:size, :], far_ref.at[size:, :])
    items = []

    def block(h, seg, keys, vals, s, part):
        start = pl.multiple_of((me ^ s) * width + part * half, half)
        at = pl.ds(start, half)

        def sink(row_max, out):
            acc_ref[h, at, :] = out
            max_ref[h, at, :] = jnp.broadcast_to(row_max, out.shape)
            if h == 1:
                mains[s][part * half : (part + 1) * half, :] = pack_pair(acc_ref[0, at, :], out).astype(BF16)
            elif h == 2 and part == 1:
                first = acc_ref[2, pl.ds(start - half, half), :]
                mains[s][width:, :] = pack_even(first, out).astype(BF16)

        items.append((lambda: dot(qts[h, at, :], keys, NN), lambda weights: dot(weights, vals, NT), sink))

    for h in range(heads):
        rows = slice(h * DH, (h + 1) * DH)
        qts[h] = q_ref[rows, :].T
        for pair in range(2):
            cols = pl.ds(pl.multiple_of(((me // 2) ^ pair) * KEYS, KEYS), KEYS)
            keys = k_ref[rows, cols]
            vals = v_ref[rows, cols]
            vals = stack_halves(vals, jnp.ones_like(vals), h)
            for s in (2 * pair, 2 * pair + 1):
                for part in range(2):
                    block(h, pair, keys, vals, s, part)
    attend(items)


def pair_kernel(dils, off_ref, q_ref, own_ref, other_ref, acc_in, max_in, p0, p1, p2, p3, cur_ref, top_ref, acc, top):
    heads, n1, _ = q_ref.shape
    tok = acc.shape[1]
    me = lax.axis_index("head")
    patches = (p0, p1, p2, p3)
    size = n1 // len(patches)
    half = size // 2
    items = []
    held = {}
    odd = me % 2 == 1

    def block(h, kv, vals, blk):
        first = pl.multiple_of(((me // 2) ^ blk) * QBLK, QBLK)
        rows = pl.ds(off_ref[0, me * heads + h] + first * dils[0], QBLK, stride=dils[0])

        def sink(row_max, out):
            both, new = merge_rows(acc[h, rows, :], top[h, rows, :], out, row_max)
            acc[h, rows, :] = new
            top[h, rows, :] = both
            if h == 0:
                held[blk] = new
                return
            if h == 1:
                done = pack_pair(held[blk], new)
                ends = [done[:size], done[size:]]
                at = slice(0, size)
            else:
                ends = [pack_even(new[i : i + half], new[i + half : i + size]) for i in (0, size)]
                at = slice(size, size + half)
            patches[2 * blk][at, :] = jnp.where(odd, ends[1], ends[0]).astype(BF16)
            patches[2 * blk + 1][at, :] = jnp.where(odd, ends[0], ends[1]).astype(BF16)

        query = q_ref[h, pl.ds(first, QBLK), :]
        items.append((lambda: dot(query, kv, NT), lambda weights: dot(weights, vals, NN), sink))

    for h in range(heads):
        kv = jnp.concatenate([own_ref[h], other_ref[h]], 0)
        vals = jnp.where(in_values(kv.shape, h), kv, jnp.ones_like(kv))
        for blk in range(n1 // QBLK):
            block(h, kv, vals, blk)
    attend(items)
    for h in range(heads):
        for b in range(1, len(dils)):
            pick = pl.ds(off_ref[b, me * heads + h], tok // dils[b], stride=dils[b])
            cur_ref[b - 1, h] = acc[h, pick, :]
            top_ref[b - 1, h] = top[h, pick, :]


def far_kernel(branches, q_own, q_other, kv0, kv1, kv2, kv3, part_ref, top_ref, send_ref):
    heads, n, _ = q_own.shape
    a_lanes = [in_values((n, LANES), h) for h in range(2)]
    items = []
    held = {}

    def block(h, b, query, kv, vals):
        def sink(row_max, out):
            part_ref[b, h] = out[:n]
            top_ref[b, h] = jnp.broadcast_to(row_max[:n], (n, LANES))
            held[b] = out[n:], row_max[n:]
            if b == branches - 1:
                pack(h)

        items.append((lambda: dot(query, kv, NT), lambda weights: dot(weights, vals, NN), sink))

    def pack(h):
        first, first_top = held[0]
        other, other_top = held[branches - 1]
        if branches == 2:
            other = swap(other)
        mine = a_lanes[h % 2]
        send_ref[h, :n, :] = jnp.where(mine, first, other).astype(BF16)
        slot = lane_of((n, LANES)) % DH
        stats = jnp.where(slot >= 3, jnp.where(mine, other, first), jnp.where(mine, other_top, first_top))
        high = stats.astype(BF16).astype(F32)
        mid = (stats - high).astype(BF16).astype(F32)
        low = stats - high - mid
        coded = jnp.where(slot % 3 == 0, high, jnp.where(slot % 3 == 1, mid, low))
        coded = coded.T
        send_ref[h, n : n + STATS, :] = coded[:STATS].astype(BF16)
        send_ref[h, n + STATS :, :] = coded[DH : DH + STATS].astype(BF16)

    for h in range(heads):
        q_all = jnp.concatenate([q_own[h], q_other[h]], 0)
        for b in range(branches):
            kv = jnp.concatenate([r[b, h] for r in (kv0, kv1, kv2, kv3)], 0)
            query = q_all if b == 0 else swap(q_all.astype(F32)).astype(BF16)
            query = jnp.where(in_values(query.shape, h), jnp.zeros_like(query), query)
            block(h, b, query, kv, jnp.where(in_values(kv.shape, h), kv, jnp.ones_like(kv)))
    attend(items)


def patch_kernel(branches, off_ref, cur_ref, cur_top, part_ref, part_top, got_ref, p0, p1, p2, p3, packed):
    heads, n = cur_ref.shape[1:3]
    me = lax.axis_index("head")
    patches = (p0, p1, p2, p3)
    size = n // len(patches)
    spread = []
    for parity in range(2):
        first = lax.broadcasted_iota(jnp.int32, (2 * STATS, 4 * LANES), 0)
        kind = lax.broadcasted_iota(jnp.int32, (2 * STATS, 4 * LANES), 1) // LANES
        base = jnp.where((kind // 2 == 0) == (parity == 0), STATS, 0) + 3 * (kind % 2)
        spread.append(jnp.where((first >= base) & (first < base + 3), 1.0, 0.0).astype(BF16))
    done = []
    for h in range(heads):
        a_lanes = in_values((n, LANES), h)
        got = got_ref[h, :n, :].astype(F32)
        stats = dot(got_ref[h, n:, :], spread[h % 2], (((0,), (0,)), ((), ())))
        states = []
        for b in range(branches):
            got_max = stats[:, 2 * b * LANES : (2 * b + 1) * LANES]
            got_sum = stats[:, (2 * b + 1) * LANES : (2 * b + 2) * LANES]
            new = jnp.where(a_lanes, got if b == 0 else swap(got), got_sum)
            states.append(merge_rows(part_ref[b, h], part_top[b, h], new, got_max))
        head = me * heads + h
        first_max, first = merge_rows(cur_ref[0, h], cur_top[0, h], states[0][1], states[0][0])
        merged = [first]
        if branches == 2:
            same = off_ref[1, head] == off_ref[2, head]
            base = jnp.where(same, first, cur_ref[1, h])
            base_max = jnp.where(same, first_max, cur_top[1, h])
            _, second = merge_rows(base, base_max, states[1][1], states[1][0])
            merged = [jnp.where(same, second, first), second]
        done.append(merged)
    for b in range(branches):
        packed[b] = pack_pair(done[0][b], done[1][b])
    packed[branches] = pack_even(done[2][0], done[2][-1])
    for s, out in enumerate(patches):
        start = pl.multiple_of((me ^ s) * size, size)
        for i in range(branches + 1):
            out[i * size : (i + 1) * size, :] = packed[i, pl.ds(start, size), :].astype(BF16)


def put_rows(off_ref, dil, branch, head, first, ref, index, new, in_low):
    at = pl.ds(off_ref[branch, head] + first * dil, new.shape[0], stride=dil)
    ref[index, at, :] = jnp.where((lane_of(new.shape) < DH) == in_low, new, ref[index, at, :])


def arrange_kernel(dils, off_ref, x0, x1, x2, x3, p0, p1, p2, p3, pairs, lasts):
    me = lax.axis_index("head")
    count = x0.shape[0]
    width = pairs.shape[1]
    half = width // 2
    near = width // dils[0]
    xs, ps = (x0, x1, x2.at[:count, :], x3.at[count:, :]), (p0, p1, p2, p3)
    for s in range(4):
        pairs[s] = xs[s][:width, :].astype(F32)
    for t in range(2):
        a = xs[2 * t][width:, :].astype(F32)
        b = xs[2 * t + 1][width:, :].astype(F32)
        lane = lane_of(a.shape)
        lasts[t, :half, :] = jnp.where(lane < DH, a, swap(b))
        lasts[t, half:, :] = jnp.where(lane < DH, swap(a), b)
    for s in range(4):
        in_low = s % 2 == 0
        put = functools.partial(put_rows, off_ref, dils[0], 0)
        head = (me ^ s) * 3
        new = ps[s][:near, :].astype(F32)
        for h in range(2):
            put(head + h, 0, pairs, s, new, h == 0)
        new = ps[s][near:, :].astype(F32)
        turned = swap(new)
        put(head + 2, 0, lasts, s // 2, new if in_low else turned, in_low)
        put(head + 2, near // 2, lasts, s // 2, turned if in_low else new, in_low)


def project_kernel(dils, off_ref, pairs_in, lasts_in, p0, p1, p2, p3, w_ref, out_hbm, pairs, lasts, out_ref, sem):
    me = lax.axis_index("head")
    width = out_ref.shape[0]
    branches = len(dils) - 1
    size = width // dils[1]
    rows = 3 * DH
    sources = [me ^ s for s in range(4)]
    ps = (p0, p1, p2, p3)
    for s in range(4):
        in_low = s % 2 == 0
        head = sources[s] * 3
        for b in range(branches):
            put = functools.partial(put_rows, off_ref, dils[b + 1], b + 1)
            new = ps[s][b * size : (b + 1) * size, :].astype(F32)
            for h in range(2):
                put(head + h, 0, pairs, s, new, h == 0)
            new = ps[s][branches * size :, :].astype(F32)
            if b != s % 2:
                new = swap(new)
            put(head + 2, 0, lasts, s // 2, new, in_low)

    def w_rows(s, start, count):
        return w_ref[pl.ds(pl.multiple_of(sources[s] * rows + start, DH), count), :]

    ws = [jnp.concatenate([w_rows(2 * t, 0, LANES), w_rows(2 * t + 1, 0, LANES)], 0) for t in range(2)]
    ws.append(jnp.concatenate([w_rows(s, LANES, DH) for s in range(4)], 0))
    xs = [jnp.concatenate([pairs[0], pairs[1]], 1), jnp.concatenate([pairs[2], pairs[3]], 1)]
    xs = [x.astype(BF16) for x in xs + [jnp.concatenate([lasts[0], lasts[1]], 1)]]
    step = out_ref.shape[1] // 3
    copies = []
    for c in range(3):
        cols = slice(c * step, (c + 1) * step)
        total = None
        for x, w in zip(xs, ws):
            part = dot(x, w[:, cols], NN)
            total = part if total is None else total + part
        out_ref[:, cols] = total.astype(BF16)
        at = pl.ds(c * step, step)
        copies.append(pltpu.make_async_copy(out_ref.at[:, at], out_hbm.at[:, at], sem.at[c]))
        copies[-1].start()
    for copy in copies:
        copy.wait()


def partner(block, axis, apart):
    count = lax.axis_size(axis)
    return lax.ppermute(block, axis, [(i, i ^ apart) for i in range(count)])


def call(kernel, name, outs, in_specs, scratch=(), aliases={}, spaces=None):
    estimate = pl.CostEstimate(flops=int(COVER[name] * 1e9), bytes_accessed=1024, transcendentals=0)
    return pl.pallas_call(
        kernel,
        out_shape=tuple(jax.ShapeDtypeStruct(*o) for o in outs),
        in_specs=in_specs,
        out_specs=tuple(pl.BlockSpec(memory_space=m) for m in spaces or (pltpu.VMEM,) * len(outs)),
        input_output_aliases=aliases,
        scratch_shapes=scratch,
        compiler_params=pltpu.CompilerParams(vmem_limit_bytes=VMEM_BYTES),
        cost_estimate=estimate,
        name=name,
    )


def spread_far(acc, top, query_h, key_h, value_h, dil, head_offsets):
    hit = jnp.arange(dil)[None, :] == head_offsets[:, None]

    def pick(x):
        shaped = x.reshape(x.shape[:2] + (x.shape[2] // dil, dil))
        return jnp.sum(shaped * hit[:, None, None, :].astype(x.dtype), axis=-1, dtype=x.dtype)

    pair = lax.all_gather(jnp.stack([pick(key_h), pick(value_h)], 0), "seq", axis=3, tiled=True)
    scores = jnp.einsum("hdq,hdk->hqk", pick(query_h), pair[0], preferred_element_type=F32)
    new_max = jnp.max(scores, axis=2, keepdims=True)
    e = jnp.exp2((scores - new_max) * EXP2_SCALE)
    new_sum = jnp.sum(e, axis=2, keepdims=True)
    new_acc = jnp.einsum("hqk,hdk->hqd", e.astype(BF16), pair[1], preferred_element_type=F32)
    heads, tok, _ = acc.shape
    shaped = acc.reshape(heads, tok // dil, dil, LANES)
    cur = jnp.sum(jnp.where(hit[:, None, :, None], shaped, 0.0), axis=2)
    sums = jnp.broadcast_to(new_sum, new_acc.shape)
    cur_top = jnp.sum(jnp.where(hit[:, None, :, None], top.reshape(shaped.shape), 0.0), axis=2)
    rows = []
    for h in range(heads):
        halves = [new_acc[h], sums[h]] if h % 2 == 0 else [sums[h], new_acc[h]]
        rows.append(merge_rows(cur[h], cur_top[h], jnp.concatenate(halves, 1), new_max[h]))

    def put(update, old):
        return jnp.where(hit[:, None, :, None], update[:, :, None, :], old).reshape(acc.shape)

    out_top, out = (jnp.stack(r, 0) for r in zip(*rows))
    return put(out, shaped), put(out_top, top.reshape(shaped.shape))


def packed_mains(acc):
    heads, tok, _ = acc.shape
    width = tok // 4
    me = lax.axis_index("head")
    rows = []
    for h in range(heads):
        low, high = acc[h, :, :DH], acc[h, :, DH:]
        rows.append(low / high if h % 2 == 0 else high / low)
    blocks = []
    for s in range(4):
        mine = [lax.dynamic_slice_in_dim(r, (me ^ s) * width, width, 0) for r in rows]
        last = jnp.concatenate([mine[2][: width // 2], mine[2][width // 2 :]], 1)
        blocks.append(jnp.concatenate([jnp.concatenate(mine[:2], 1), last], 0).astype(BF16))
    return blocks[0], blocks[1], jnp.concatenate(blocks[2:], 0)


def local(queries, key_vectors, value_vectors, offsets, out_weight):
    tok = queries.shape[1]
    heads = queries.shape[0] // DH
    seq_count = lax.axis_size("seq")
    far_rate = tok * seq_count // KEYS
    dils = (4, 16, 16) if far_rate == 16 else (4, 16)
    branches = len(dils) - 1
    n1, n2 = tok // 4, tok // 16
    width = tok // 4
    whole = pl.BlockSpec(memory_space=pltpu.VMEM)
    smem = pl.BlockSpec(memory_space=pltpu.SMEM)
    hbm = pl.BlockSpec(memory_space=pltpu.HBM)
    far_shape = ((branches, heads, n2, LANES), F32)
    acc_shape = ((heads, tok, LANES), F32)

    stay = [
        pltpu.with_memory_space_constraint(a, pltpu.HBM) for a in (offsets, queries, key_vectors, value_vectors)
    ]
    q, k, v, near, far = call(
        functools.partial(select_kernel, dils),
        "select",
        [(queries.shape, BF16)] * 3 + [((heads, n1, LANES), BF16), ((branches, heads, n2, LANES), BF16)],
        [hbm] * 4,
        [
            pltpu.VMEM((heads, tok, LANES), F32),
            pltpu.SMEM(offsets.shape, jnp.int32),
            pltpu.SemaphoreType.DMA((heads, 3)),
            pltpu.SemaphoreType.DMA,
        ],
    )(*stay)
    fars = [far] + [partner(far, "seq", apart) for apart in (4, 6, 2)]

    q1, q23 = call(
        functools.partial(query_kernel, dils),
        "query",
        [((heads, n1, LANES), BF16), ((heads, n2, LANES), BF16)],
        [hbm, whole],
        [
            pltpu.VMEM((heads, tok, LANES), F32),
            pltpu.SMEM(offsets.shape, jnp.int32),
            pltpu.SemaphoreType.DMA,
        ],
    )(stay[0], q)
    q23_other = partner(q23, "seq", 1)
    near_other = partner(near, "seq", 1)

    q, q23 = lax.optimization_barrier((q, q23))
    main = heads * width // 2
    acc, top, m_own, m_core, m_far = call(
        local_kernel,
        "local",
        [acc_shape] * 2 + [((main, LANES), BF16)] * 2 + [((2 * main, LANES), BF16)],
        [whole] * 3,
        [pltpu.VMEM((heads, tok, DH), BF16)],
    )(q, k, v)

    if branches == 1:
        shape = (heads, DH, tok)
        my_offsets = lax.dynamic_slice_in_dim(offsets[2], lax.axis_index("head") * heads, heads, 0)
        parts = [a.reshape(shape) for a in (queries, key_vectors, value_vectors)]
        acc, top = spread_far(acc, top, *parts, far_rate, my_offsets)
        m_own, m_core, m_far = packed_mains(acc)

    y_in = partner(m_far, "head", 2)
    core_in = partner(m_core, "head", 1)

    acc, near_other = lax.optimization_barrier((acc, near_other))
    *early, cur, cur_top, _, _ = call(
        functools.partial(pair_kernel, dils),
        "pair",
        [((n1 * 3 // 8, LANES), BF16)] * 4 + [far_shape] * 2 + [acc_shape] * 2,
        [smem] + [whole] * 5,
        aliases={4: 6, 5: 7},
    )(offsets, q1, near, near_other, acc, top)
    early = [early[0]] + [partner(early[s], "head", s) for s in range(1, 4)]

    fars, cur = lax.optimization_barrier((fars, cur))
    part, part_top, send = call(
        functools.partial(far_kernel, branches),
        "far",
        [far_shape] * 2 + [((heads, n2 + 2 * STATS, LANES), BF16)],
        [whole] * 6,
    )(q23, q23_other, *fars)
    got = partner(send, "seq", 1)
    y_core = partner(y_in, "head", 1)

    patches = call(
        functools.partial(patch_kernel, branches),
        "patch",
        [(((branches + 1) * n2 // 4, LANES), BF16)] * 4,
        [smem] + [whole] * 5,
        [pltpu.VMEM((branches + 1, n2, LANES), F32)],
    )(offsets, cur, cur_top, part, part_top, got)
    fixes = [patches[0]] + [partner(patches[s], "head", s) for s in range(1, 4)]

    out_shape = (width, out_weight.shape[1])
    spread_shapes = [((4, width, LANES), F32), ((2, width, LANES), F32)]
    pairs, lasts = call(
        functools.partial(arrange_kernel, dils), "arrange", spread_shapes, [smem] + [whole] * 8
    )(offsets, m_own, core_in, y_in, y_core, *early)
    out, _, _ = call(
        functools.partial(project_kernel, dils),
        "project",
        [(out_shape, BF16)] + spread_shapes,
        [smem] + [whole] * 7,
        [pltpu.VMEM(out_shape, BF16), pltpu.SemaphoreType.DMA((3,))],
        aliases={1: 1, 2: 2},
        spaces=(pltpu.HBM, pltpu.VMEM, pltpu.VMEM),
    )(offsets, pairs, lasts, *fixes, out_weight)
    return out


def solution(mesh):
    in_specs = (P("head", "seq"), P("head", "seq"), P("head", "seq"), P(), P())
    out_specs = P(("seq", "head"), None)
    return jax.shard_map(local, mesh=mesh, in_specs=in_specs, out_specs=out_specs, check_vma=False)
```

```python
import functools
import math

import jax
import jax.numpy as jnp
from jax import lax
from jax.experimental import pallas as pl
from jax.experimental.pallas import tpu as pltpu
from jax.sharding import PartitionSpec as P

DH = 64
KEYS = 1024
LANES = 128
QBLK = 256
EXP2_SCALE = DH ** (-0.5) * math.log2(math.e)
NT = (((1,), (1,)), ((), ()))
NN = (((1,), (0,)), ((), ()))
STATS = 16
VMEM_BYTES = 24 << 20
COVER = dict(select=6, query=4, local=25, far=1, pair=3, patch=5, arrange=4, project=6)
BF16, F32 = jnp.bfloat16, jnp.float32


def dot(a, b, dims):
    return lax.dot_general(a, b, dims, preferred_element_type=F32)


def lane_of(shape):
    return lax.broadcasted_iota(jnp.int32, shape, len(shape) - 1)


def in_values(shape, head):
    return (lane_of(shape) < DH) == (head % 2 == 0)


def stack_halves(values, others, head):
    return jnp.concatenate([values, others] if head % 2 == 0 else [others, values], 0)


def swap(rows):
    return pltpu.roll(rows, DH, 1)


def softmax_block(scores):
    row_max = jnp.max(scores, axis=1, keepdims=True)
    weights = jnp.exp2((scores - row_max) * EXP2_SCALE).astype(BF16)
    return row_max, weights


def attend(items):
    scores = items[0][0]()
    for i, (_, values, sink) in enumerate(items):
        ahead = items[i + 1][0]() if i + 1 < len(items) else None
        row_max, weights = softmax_block(scores)
        sink(row_max, values(weights))
        scores = ahead


def merge_rows(cur, cur_max, new, new_max):
    both = jnp.maximum(cur_max, new_max)
    keep_cur = jnp.exp2((cur_max - both) * EXP2_SCALE)
    keep_new = jnp.exp2((new_max - both) * EXP2_SCALE)
    return both, cur * keep_cur + new * keep_new


def pack_pair(even, odd):
    low = lane_of(even.shape) < DH
    return jnp.where(low, even, odd) * pl.reciprocal(swap(jnp.where(low, odd, even)))


def pack_even(first, second):
    low = lane_of(first.shape) < DH
    return jnp.where(low, first, swap(second)) * pl.reciprocal(jnp.where(low, swap(first), second))


def select_kernel(dils, off_hbm, q_hbm, k_hbm, v_hbm, q_ref, k_ref, v_ref, near_ref, far_ref, kvt, off_ref, sems, off_sem):
    heads = q_ref.shape[0] // DH
    tok = q_ref.shape[1]
    off_copy = pltpu.make_async_copy(off_hbm, off_ref, off_sem)
    off_copy.start()
    copies = []
    for h in range(heads):
        rows = pl.ds(h * DH, DH)
        for i, (src, dst) in enumerate(((k_hbm, k_ref), (v_hbm, v_ref))):
            copies.append(pltpu.make_async_copy(src.at[rows, :], dst.at[rows, :], sems.at[h, i]))
            copies[-1].start()
    q_copy = pltpu.make_async_copy(q_hbm, q_ref, sems.at[0, 2])
    q_copy.start()
    off_copy.wait()
    for h in range(heads):
        rows = slice(h * DH, (h + 1) * DH)
        head = lax.axis_index("head") * heads + h
        copies[2 * h].wait()
        copies[2 * h + 1].wait()
        kvt[h] = stack_halves(v_ref[rows, :], k_ref[rows, :], h).T.astype(F32)
        near_ref[h] = kvt[h, pl.ds(off_ref[0, head], tok // dils[0], stride=dils[0]), :].astype(BF16)
        for b in range(1, len(dils)):
            pick = pl.ds(off_ref[b, head], tok // dils[b], stride=dils[b])
            far_ref[b - 1, h] = kvt[h, pick, :].astype(BF16)
    q_copy.wait()


def query_kernel(dils, off_hbm, q_ref, q1_ref, q23_ref, qt, off_ref, off_sem):
    heads = q_ref.shape[0] // DH
    tok = q_ref.shape[1]
    copy = pltpu.make_async_copy(off_hbm, off_ref, off_sem)
    copy.start()
    for h in range(heads):
        head = lax.axis_index("head") * heads + h
        query = q_ref[h * DH : (h + 1) * DH, :]
        qt[h] = stack_halves(jnp.zeros_like(query), query, h).T.astype(F32)
        if h == 0:
            copy.wait()
        picks = [pl.ds(off_ref[b, head], tok // d, stride=d) for b, d in enumerate(dils)]
        q1_ref[h] = qt[h, picks[0], :].astype(BF16)
        far_q = qt[h, picks[1], :]
        if len(dils) == 3:
            far_q = far_q + swap(qt[h, picks[2], :])
        q23_ref[h] = far_q.astype(BF16)


def local_kernel(q_ref, k_ref, v_ref, acc_ref, max_ref, own_ref, core_ref, far_ref, qts):
    heads = q_ref.shape[0] // DH
    tok = q_ref.shape[1]
    width = tok // 4
    half = width // 2
    size = own_ref.shape[0]
    me = lax.axis_index("head")
    mains = (own_ref, core_ref, far_ref.at[:size, :], far_ref.at[size:, :])
    items = []

    def block(h, seg, keys, vals, s, part):
        start = pl.multiple_of((me ^ s) * width + part * half, half)
        at = pl.ds(start, half)

        def sink(row_max, out):
            acc_ref[h, at, :] = out
            max_ref[h, at, :] = jnp.broadcast_to(row_max, out.shape)
            if h == 1:
                mains[s][part * half : (part + 1) * half, :] = pack_pair(acc_ref[0, at, :], out).astype(BF16)
            elif h == 2 and part == 1:
                first = acc_ref[2, pl.ds(start - half, half), :]
                mains[s][width:, :] = pack_even(first, out).astype(BF16)

        items.append((lambda: dot(qts[h, at, :], keys, NN), lambda weights: dot(weights, vals, NT), sink))

    for h in range(heads):
        rows = slice(h * DH, (h + 1) * DH)
        qts[h] = q_ref[rows, :].T
        for pair in range(2):
            cols = pl.ds(pl.multiple_of(((me // 2) ^ pair) * KEYS, KEYS), KEYS)
            keys = k_ref[rows, cols]
            vals = v_ref[rows, cols]
            vals = stack_halves(vals, jnp.ones_like(vals), h)
            for s in (2 * pair, 2 * pair + 1):
                for part in range(2):
                    block(h, pair, keys, vals, s, part)
    attend(items)


def pair_kernel(dils, off_ref, q_ref, own_ref, other_ref, acc_in, max_in, p0, p1, p2, p3, cur_ref, top_ref, acc, top):
    heads, n1, _ = q_ref.shape
    tok = acc.shape[1]
    me = lax.axis_index("head")
    patches = (p0, p1, p2, p3)
    size = n1 // len(patches)
    half = size // 2
    items = []
    held = {}
    odd = me % 2 == 1

    def block(h, kv, vals, blk):
        first = pl.multiple_of(((me // 2) ^ blk) * QBLK, QBLK)
        rows = pl.ds(off_ref[0, me * heads + h] + first * dils[0], QBLK, stride=dils[0])

        def sink(row_max, out):
            both, new = merge_rows(acc[h, rows, :], top[h, rows, :], out, row_max)
            acc[h, rows, :] = new
            top[h, rows, :] = both
            if h == 0:
                held[blk] = new
                return
            if h == 1:
                done = pack_pair(held[blk], new)
                ends = [done[:size], done[size:]]
                at = slice(0, size)
            else:
                ends = [pack_even(new[i : i + half], new[i + half : i + size]) for i in (0, size)]
                at = slice(size, size + half)
            patches[2 * blk][at, :] = jnp.where(odd, ends[1], ends[0]).astype(BF16)
            patches[2 * blk + 1][at, :] = jnp.where(odd, ends[0], ends[1]).astype(BF16)

        query = q_ref[h, pl.ds(first, QBLK), :]
        items.append((lambda: dot(query, kv, NT), lambda weights: dot(weights, vals, NN), sink))

    for h in range(heads):
        kv = jnp.concatenate([own_ref[h], other_ref[h]], 0)
        vals = jnp.where(in_values(kv.shape, h), kv, jnp.ones_like(kv))
        for blk in range(n1 // QBLK):
            block(h, kv, vals, blk)
    attend(items)
    for h in range(heads):
        for b in range(1, len(dils)):
            pick = pl.ds(off_ref[b, me * heads + h], tok // dils[b], stride=dils[b])
            cur_ref[b - 1, h] = acc[h, pick, :]
            top_ref[b - 1, h] = top[h, pick, :]


def far_kernel(branches, q_own, q_other, kv0, kv1, kv2, kv3, part_ref, top_ref, send_ref):
    heads, n, _ = q_own.shape
    a_lanes = [in_values((n, LANES), h) for h in range(2)]
    items = []
    held = {}

    def block(h, b, query, kv, vals):
        def sink(row_max, out):
            part_ref[b, h] = out[:n]
            top_ref[b, h] = jnp.broadcast_to(row_max[:n], (n, LANES))
            held[b] = out[n:], row_max[n:]
            if b == branches - 1:
                pack(h)

        items.append((lambda: dot(query, kv, NT), lambda weights: dot(weights, vals, NN), sink))

    def pack(h):
        first, first_top = held[0]
        other, other_top = held[branches - 1]
        if branches == 2:
            other = swap(other)
        mine = a_lanes[h % 2]
        send_ref[h, :n, :] = jnp.where(mine, first, other).astype(BF16)
        slot = lane_of((n, LANES)) % DH
        stats = jnp.where(slot >= 3, jnp.where(mine, other, first), jnp.where(mine, other_top, first_top))
        high = stats.astype(BF16).astype(F32)
        mid = (stats - high).astype(BF16).astype(F32)
        low = stats - high - mid
        coded = jnp.where(slot % 3 == 0, high, jnp.where(slot % 3 == 1, mid, low))
        coded = coded.T
        send_ref[h, n : n + STATS, :] = coded[:STATS].astype(BF16)
        send_ref[h, n + STATS :, :] = coded[DH : DH + STATS].astype(BF16)

    for h in range(heads):
        q_all = jnp.concatenate([q_own[h], q_other[h]], 0)
        for b in range(branches):
            kv = jnp.concatenate([r[b, h] for r in (kv0, kv1, kv2, kv3)], 0)
            query = q_all if b == 0 else swap(q_all.astype(F32)).astype(BF16)
            query = jnp.where(in_values(query.shape, h), jnp.zeros_like(query), query)
            block(h, b, query, kv, jnp.where(in_values(kv.shape, h), kv, jnp.ones_like(kv)))
    attend(items)


def patch_kernel(branches, off_ref, cur_ref, cur_top, part_ref, part_top, got_ref, p0, p1, p2, p3, packed):
    heads, n = cur_ref.shape[1:3]
    me = lax.axis_index("head")
    patches = (p0, p1, p2, p3)
    size = n // len(patches)
    spread = []
    for parity in range(2):
        first = lax.broadcasted_iota(jnp.int32, (2 * STATS, 4 * LANES), 0)
        kind = lax.broadcasted_iota(jnp.int32, (2 * STATS, 4 * LANES), 1) // LANES
        base = jnp.where((kind // 2 == 0) == (parity == 0), STATS, 0) + 3 * (kind % 2)
        spread.append(jnp.where((first >= base) & (first < base + 3), 1.0, 0.0).astype(BF16))
    done = []
    for h in range(heads):
        a_lanes = in_values((n, LANES), h)
        got = got_ref[h, :n, :].astype(F32)
        stats = dot(got_ref[h, n:, :], spread[h % 2], (((0,), (0,)), ((), ())))
        states = []
        for b in range(branches):
            got_max = stats[:, 2 * b * LANES : (2 * b + 1) * LANES]
            got_sum = stats[:, (2 * b + 1) * LANES : (2 * b + 2) * LANES]
            new = jnp.where(a_lanes, got if b == 0 else swap(got), got_sum)
            states.append(merge_rows(part_ref[b, h], part_top[b, h], new, got_max))
        head = me * heads + h
        first_max, first = merge_rows(cur_ref[0, h], cur_top[0, h], states[0][1], states[0][0])
        merged = [first]
        if branches == 2:
            same = off_ref[1, head] == off_ref[2, head]
            base = jnp.where(same, first, cur_ref[1, h])
            base_max = jnp.where(same, first_max, cur_top[1, h])
            _, second = merge_rows(base, base_max, states[1][1], states[1][0])
            merged = [jnp.where(same, second, first), second]
        done.append(merged)
    for b in range(branches):
        packed[b] = pack_pair(done[0][b], done[1][b])
    packed[branches] = pack_even(done[2][0], done[2][-1])
    for s, out in enumerate(patches):
        start = pl.multiple_of((me ^ s) * size, size)
        for i in range(branches + 1):
            out[i * size : (i + 1) * size, :] = packed[i, pl.ds(start, size), :].astype(BF16)


def put_rows(off_ref, dil, branch, head, first, ref, index, new, in_low):
    at = pl.ds(off_ref[branch, head] + first * dil, new.shape[0], stride=dil)
    ref[index, at, :] = jnp.where((lane_of(new.shape) < DH) == in_low, new, ref[index, at, :])


def arrange_kernel(dils, off_ref, x0, x1, x2, x3, p0, p1, p2, p3, pairs, lasts):
    me = lax.axis_index("head")
    count = x0.shape[0]
    width = pairs.shape[1]
    half = width // 2
    near = width // dils[0]
    xs, ps = (x0, x1, x2.at[:count, :], x3.at[count:, :]), (p0, p1, p2, p3)
    for s in range(4):
        pairs[s] = xs[s][:width, :].astype(F32)
    for t in range(2):
        a = xs[2 * t][width:, :].astype(F32)
        b = xs[2 * t + 1][width:, :].astype(F32)
        lane = lane_of(a.shape)
        lasts[t, :half, :] = jnp.where(lane < DH, a, swap(b))
        lasts[t, half:, :] = jnp.where(lane < DH, swap(a), b)
    for s in range(4):
        in_low = s % 2 == 0
        put = functools.partial(put_rows, off_ref, dils[0], 0)
        head = (me ^ s) * 3
        new = ps[s][:near, :].astype(F32)
        for h in range(2):
            put(head + h, 0, pairs, s, new, h == 0)
        new = ps[s][near:, :].astype(F32)
        turned = swap(new)
        put(head + 2, 0, lasts, s // 2, new if in_low else turned, in_low)
        put(head + 2, near // 2, lasts, s // 2, turned if in_low else new, in_low)


def project_kernel(dils, off_ref, pairs_in, lasts_in, p0, p1, p2, p3, w_ref, out_hbm, pairs, lasts, out_ref, sem):
    me = lax.axis_index("head")
    width = out_ref.shape[0]
    branches = len(dils) - 1
    size = width // dils[1]
    rows = 3 * DH
    sources = [me ^ s for s in range(4)]
    ps = (p0, p1, p2, p3)
    for s in range(4):
        in_low = s % 2 == 0
        head = sources[s] * 3
        for b in range(branches):
            put = functools.partial(put_rows, off_ref, dils[b + 1], b + 1)
            new = ps[s][b * size : (b + 1) * size, :].astype(F32)
            for h in range(2):
                put(head + h, 0, pairs, s, new, h == 0)
            new = ps[s][branches * size :, :].astype(F32)
            if b != s % 2:
                new = swap(new)
            put(head + 2, 0, lasts, s // 2, new, in_low)

    def w_rows(s, start, count):
        return w_ref[pl.ds(pl.multiple_of(sources[s] * rows + start, DH), count), :]

    ws = [jnp.concatenate([w_rows(2 * t, 0, LANES), w_rows(2 * t + 1, 0, LANES)], 0) for t in range(2)]
    ws.append(jnp.concatenate([w_rows(s, LANES, DH) for s in range(4)], 0))
    xs = [jnp.concatenate([pairs[0], pairs[1]], 1), jnp.concatenate([pairs[2], pairs[3]], 1)]
    xs = [x.astype(BF16) for x in xs + [jnp.concatenate([lasts[0], lasts[1]], 1)]]
    step = out_ref.shape[1] // 3
    copies = []
    for c in range(3):
        cols = slice(c * step, (c + 1) * step)
        total = None
        for x, w in zip(xs, ws):
            part = dot(x, w[:, cols], NN)
            total = part if total is None else total + part
        out_ref[:, cols] = total.astype(BF16)
        at = pl.ds(c * step, step)
        copies.append(pltpu.make_async_copy(out_ref.at[:, at], out_hbm.at[:, at], sem.at[c]))
        copies[-1].start()
    for copy in copies:
        copy.wait()


def partner(block, axis, apart):
    count = lax.axis_size(axis)
    return lax.ppermute(block, axis, [(i, i ^ apart) for i in range(count)])


def call(kernel, name, outs, in_specs, scratch=(), aliases={}, spaces=None):
    estimate = pl.CostEstimate(flops=int(COVER[name] * 1e9), bytes_accessed=1024, transcendentals=0)
    return pl.pallas_call(
        kernel,
        out_shape=tuple(jax.ShapeDtypeStruct(*o) for o in outs),
        in_specs=in_specs,
        out_specs=tuple(pl.BlockSpec(memory_space=m) for m in spaces or (pltpu.VMEM,) * len(outs)),
        input_output_aliases=aliases,
        scratch_shapes=scratch,
        compiler_params=pltpu.CompilerParams(vmem_limit_bytes=VMEM_BYTES),
        cost_estimate=estimate,
        name=name,
    )


def spread_far(acc, top, query_h, key_h, value_h, dil, head_offsets):
    hit = jnp.arange(dil)[None, :] == head_offsets[:, None]

    def pick(x):
        shaped = x.reshape(x.shape[:2] + (x.shape[2] // dil, dil))
        return jnp.sum(shaped * hit[:, None, None, :].astype(x.dtype), axis=-1, dtype=x.dtype)

    pair = lax.all_gather(jnp.stack([pick(key_h), pick(value_h)], 0), "seq", axis=3, tiled=True)
    scores = jnp.einsum("hdq,hdk->hqk", pick(query_h), pair[0], preferred_element_type=F32)
    new_max = jnp.max(scores, axis=2, keepdims=True)
    e = jnp.exp2((scores - new_max) * EXP2_SCALE)
    new_sum = jnp.sum(e, axis=2, keepdims=True)
    new_acc = jnp.einsum("hqk,hdk->hqd", e.astype(BF16), pair[1], preferred_element_type=F32)
    heads, tok, _ = acc.shape
    shaped = acc.reshape(heads, tok // dil, dil, LANES)
    cur = jnp.sum(jnp.where(hit[:, None, :, None], shaped, 0.0), axis=2)
    sums = jnp.broadcast_to(new_sum, new_acc.shape)
    cur_top = jnp.sum(jnp.where(hit[:, None, :, None], top.reshape(shaped.shape), 0.0), axis=2)
    rows = []
    for h in range(heads):
        halves = [new_acc[h], sums[h]] if h % 2 == 0 else [sums[h], new_acc[h]]
        rows.append(merge_rows(cur[h], cur_top[h], jnp.concatenate(halves, 1), new_max[h]))

    def put(update, old):
        return jnp.where(hit[:, None, :, None], update[:, :, None, :], old).reshape(acc.shape)

    out_top, out = (jnp.stack(r, 0) for r in zip(*rows))
    return put(out, shaped), put(out_top, top.reshape(shaped.shape))


def packed_mains(acc):
    heads, tok, _ = acc.shape
    width = tok // 4
    me = lax.axis_index("head")
    rows = []
    for h in range(heads):
        low, high = acc[h, :, :DH], acc[h, :, DH:]
        rows.append(low / high if h % 2 == 0 else high / low)
    blocks = []
    for s in range(4):
        mine = [lax.dynamic_slice_in_dim(r, (me ^ s) * width, width, 0) for r in rows]
        last = jnp.concatenate([mine[2][: width // 2], mine[2][width // 2 :]], 1)
        blocks.append(jnp.concatenate([jnp.concatenate(mine[:2], 1), last], 0).astype(BF16))
    return blocks[0], blocks[1], jnp.concatenate(blocks[2:], 0)


def local(queries, key_vectors, value_vectors, offsets, out_weight):
    tok = queries.shape[1]
    heads = queries.shape[0] // DH
    seq_count = lax.axis_size("seq")
    far_rate = tok * seq_count // KEYS
    dils = (4, 16, 16) if far_rate == 16 else (4, 16)
    branches = len(dils) - 1
    n1, n2 = tok // 4, tok // 16
    width = tok // 4
    whole = pl.BlockSpec(memory_space=pltpu.VMEM)
    smem = pl.BlockSpec(memory_space=pltpu.SMEM)
    hbm = pl.BlockSpec(memory_space=pltpu.HBM)
    far_shape = ((branches, heads, n2, LANES), F32)
    acc_shape = ((heads, tok, LANES), F32)

    stay = [
        pltpu.with_memory_space_constraint(a, pltpu.HBM) for a in (offsets, queries, key_vectors, value_vectors)
    ]
    q, k, v, near, far = call(
        functools.partial(select_kernel, dils),
        "select",
        [(queries.shape, BF16)] * 3 + [((heads, n1, LANES), BF16), ((branches, heads, n2, LANES), BF16)],
        [hbm] * 4,
        [
            pltpu.VMEM((heads, tok, LANES), F32),
            pltpu.SMEM(offsets.shape, jnp.int32),
            pltpu.SemaphoreType.DMA((heads, 3)),
            pltpu.SemaphoreType.DMA,
        ],
    )(*stay)
    fars = [far] + [partner(far, "seq", apart) for apart in (4, 6, 2)]

    q1, q23 = call(
        functools.partial(query_kernel, dils),
        "query",
        [((heads, n1, LANES), BF16), ((heads, n2, LANES), BF16)],
        [hbm, whole],
        [
            pltpu.VMEM((heads, tok, LANES), F32),
            pltpu.SMEM(offsets.shape, jnp.int32),
            pltpu.SemaphoreType.DMA,
        ],
    )(stay[0], q)
    q23_other = partner(q23, "seq", 1)
    near_other = partner(near, "seq", 1)

    q, q23 = lax.optimization_barrier((q, q23))
    main = heads * width // 2
    acc, top, m_own, m_core, m_far = call(
        local_kernel,
        "local",
        [acc_shape] * 2 + [((main, LANES), BF16)] * 2 + [((2 * main, LANES), BF16)],
        [whole] * 3,
        [pltpu.VMEM((heads, tok, DH), BF16)],
    )(q, k, v)

    if branches == 1:
        shape = (heads, DH, tok)
        my_offsets = lax.dynamic_slice_in_dim(offsets[2], lax.axis_index("head") * heads, heads, 0)
        parts = [a.reshape(shape) for a in (queries, key_vectors, value_vectors)]
        acc, top = spread_far(acc, top, *parts, far_rate, my_offsets)
        m_own, m_core, m_far = packed_mains(acc)

    y_in = partner(m_far, "head", 2)
    core_in = partner(m_core, "head", 1)

    acc, near_other = lax.optimization_barrier((acc, near_other))
    *early, cur, cur_top, _, _ = call(
        functools.partial(pair_kernel, dils),
        "pair",
        [((n1 * 3 // 8, LANES), BF16)] * 4 + [far_shape] * 2 + [acc_shape] * 2,
        [smem] + [whole] * 5,
        aliases={4: 6, 5: 7},
    )(offsets, q1, near, near_other, acc, top)
    early = [early[0]] + [partner(early[s], "head", s) for s in range(1, 4)]

    fars, cur = lax.optimization_barrier((fars, cur))
    part, part_top, send = call(
        functools.partial(far_kernel, branches),
        "far",
        [far_shape] * 2 + [((heads, n2 + 2 * STATS, LANES), BF16)],
        [whole] * 6,
    )(q23, q23_other, *fars)
    got = partner(send, "seq", 1)
    y_core = partner(y_in, "head", 1)

    patches = call(
        functools.partial(patch_kernel, branches),
        "patch",
        [(((branches + 1) * n2 // 4, LANES), BF16)] * 4,
        [smem] + [whole] * 5,
        [pltpu.VMEM((branches + 1, n2, LANES), F32)],
    )(offsets, cur, cur_top, part, part_top, got)
    fixes = [patches[0]] + [partner(patches[s], "head", s) for s in range(1, 4)]

    out_shape = (width, out_weight.shape[1])
    spread_shapes = [((4, width, LANES), F32), ((2, width, LANES), F32)]
    pairs, lasts = call(
        functools.partial(arrange_kernel, dils), "arrange", spread_shapes, [smem] + [whole] * 8
    )(offsets, m_own, core_in, y_in, y_core, *early)
    out, _, _ = call(
        functools.partial(project_kernel, dils),
        "project",
        [(out_shape, BF16)] + spread_shapes,
        [smem] + [whole] * 7,
        [pltpu.VMEM(out_shape, BF16), pltpu.SemaphoreType.DMA((3,))],
        aliases={1: 1, 2: 2},
        spaces=(pltpu.HBM, pltpu.VMEM, pltpu.VMEM),
    )(offsets, pairs, lasts, *fixes, out_weight)
    return out


def solution(mesh):
    in_specs = (P("head", "seq"), P("head", "seq"), P("head", "seq"), P(), P())
    out_specs = P(("seq", "head"), None)
    return jax.shard_map(local, mesh=mesh, in_specs=in_specs, out_specs=out_specs, check_vma=False)
```
